32 devices in a mesh: dp: 16 (over z, y, x), tensor: 2 (over core).
Axes of the slice: x: 2, y: 2, z: 4, core: 2. Of those that a mesh axis runs over, the one named last changes fastest.
Arguments:
- hidden_in: bfloat16 [32768, 1024], P(('dp', 'tensor')), may hold values from -6 to 6
- value_first: bfloat16 [32768, 1024], P('dp', 'tensor'), may hold values from -6 to 6
- segment_ids: int32 [16, 2048], P('dp'), may hold values from 0 to 3, never falling along the last dimension, each value on 1 to 1024 neighbouring positions
- out_cotangent: bfloat16 [32768, 1024], P(('dp', 'tensor')), may hold values from -6 to 6
- attn_gain: bfloat16 [1024], P('dp'), may hold values from 0.5 to 1.5
- w_query: bfloat16 [1024, 1024], P('dp', 'tensor'), may hold values from -0.1875 to 0.1875
- w_key: bfloat16 [1024, 1024], P('dp', 'tensor'), may hold values from -0.1875 to 0.1875
- w_value: bfloat16 [1024, 1024], P('dp', 'tensor'), may hold values from -0.1875 to 0.1875
- w_output: bfloat16 [1024, 1024], P('tensor', 'dp'), may hold values from -0.75 to 0.75
- mlp_gain: bfloat16 [1024], P('dp'), may hold values from 0.5 to 1.5
- w_gate: bfloat16 [1024, 2816], P('dp', 'tensor'), may hold values from -0.1875 to 0.1875
- w_up: bfloat16 [1024, 2816], P('dp', 'tensor'), may hold values from -0.1875 to 0.1875
- w_down: bfloat16 [2816, 1024], P('tensor', 'dp'), may hold values from -0.109375 to 0.109375
Outputs:
- layer_out: bfloat16 [32768, 1024], P(('dp', 'tensor'))
- grad_input: float32 [32768, 1024], P(('dp', 'tensor'))
- grad_value_first: float32 [32768, 1024], P('dp', 'tensor')
- grad_attn_gain: float32 [1024], P('dp')
- grad_query: float32 [1024, 1024], P('dp', 'tensor')
- grad_key: float32 [1024, 1024], P('dp', 'tensor')
- grad_value: float32 [1024, 1024], P('dp', 'tensor')
- grad_output: float32 [1024, 1024], P('tensor', 'dp')
- grad_mlp_gain: float32 [1024], P('dp')
- grad_gate: float32 [1024, 2816], P('dp', 'tensor')
- grad_up: float32 [1024, 2816], P('dp', 'tensor')
- grad_down: float32 [2816, 1024], P('tensor', 'dp')
The draws below stay inside these ranges and needn't reach their ends.
Inputs may be any that keep to these rules, and one draw needn't show every extreme that they name: `segment_ids`: segment ids never fall along a sequence; each sequence holds 4 documents of 1 to 1024 tokens, one of exactly 1024.
All inputs are finite; a program needn't handle non-finite values.
Results may differ from the reference program's by a relative error of at most 0.023.
Values may be sent and summed in bfloat16 or wider, within the bound.
No kernel may reach another device: no remote copies, remote signals or barrier semaphores. Data moves between devices by JAX's collectives and lax.ppermute only.
A program may use at most 256 MiB of HBM per device.

```python
import math
import jax
import jax.numpy as jnp
import numpy as np
from jax import lax

D = 1024
HEADS = 16
HEAD = 64
FF = 2816
SEQ = 2048
DOCS = 4
DOC_MOST = 1024
SEQS = 16
TOKENS = 32768


def steps_of(rng, dims, shards, least, top_value):
    factor_of, own = 1.0, jax.random.fold_in(rng, 6)
    for position, blocks in shards:
        draws = jnp.exp(jax.random.uniform(jax.random.fold_in(own, position), (blocks,), jnp.float32, least / len(shards), top_value / len(shards)))
        factor_of = factor_of * jnp.repeat(draws, dims[position] // blocks).reshape([-1 if axis == position else 1 for axis in range(len(dims))])
    return factor_of


def split_up(count, total, reach, skew):
    loads = [(1 << 20) // math.isqrt(rank ** skew) + 1 for rank in range(2, count + 1)]
    spare, counts = total - reach - (count - 1), [1] * (count - 1)
    while spare > 0:
        movable = [i for i in range(count - 1) if counts[i] < reach]
        mass, left = sum([loads[i] for i in movable]), spare
        for i in movable:
            extra = min(reach - counts[i], max(1, left * loads[i] // mass), spare)
            counts[i] = counts[i] + extra
            spare = spare - extra
    return np.array([reach] + counts)


def ragged(key, amount, total, most, skew):
    if amount == 2:
        one = jax.random.randint(key, (), max(1, total - most), min(most, total - 1) + 1)
        return jnp.stack([one, total - one])
    sizes = jnp.asarray(split_up(amount, total, most, skew), jnp.int32)
    couples = (amount - 1) // 2
    source_of, sink = sizes[1:1 + 2 * couples:2], sizes[2:2 + 2 * couples:2]
    slack = jnp.minimum(source_of - 1, most - sink)
    moved = jax.random.randint(jax.random.fold_in(key, 1), (couples,), 0, 1 << 20) % (slack + 1)
    sizes = sizes.at[1:1 + 2 * couples:2].set(source_of - moved).at[2:2 + 2 * couples:2].set(sink + moved)
    return sizes[jax.random.permutation(jax.random.fold_in(key, 2), amount)]


def normal_values(stream_key, extent, width, most, cuts=(), kind=jnp.bfloat16):
    values = width * jax.random.normal(stream_key, extent, jnp.float32)
    if cuts:
        values = values * steps_of(stream_key, extent, cuts, -0.22, 0.18)
    return jnp.clip(values, -most, most).astype(kind)


def setup_inputs(seed: int = 0) -> dict:
    seeds = jax.random.split(jax.random.key(seed), 14)
    hidden_in = normal_values(seeds[0], (TOKENS, D), 1.0, 6.0, ((0, 32),))
    value_first = normal_values(seeds[1], (TOKENS, D), 1.0, 6.0, ((0, 16), (1, 2)))
    segment_ids = jax.vmap(lambda own: jnp.searchsorted(jnp.cumsum(ragged(own, DOCS, SEQ, DOC_MOST, 0)), jnp.arange(SEQ), side="right"))(jax.random.split(seeds[2], SEQS)).reshape((SEQS, SEQ)).astype(jnp.int32)
    out_cotangent = normal_values(seeds[3], (TOKENS, D), 1.0, 6.0, ((0, 32),))
    attn_gain = jnp.clip(1.0 + 0.1 * jax.random.normal(seeds[4], (D,), jnp.float32), 0.5, 1.5).astype(jnp.bfloat16)
    w_query = normal_values(seeds[5], (D, D), D ** -0.5, 0.1875, ((0, 16), (1, 2)))
    w_key = normal_values(seeds[6], (D, D), D ** -0.5, 0.1875, ((0, 16), (1, 2)))
    w_value = normal_values(seeds[7], (D, D), D ** -0.5, 0.1875, ((0, 16), (1, 2)))
    w_output = normal_values(seeds[8], (D, D), (D // 16) ** -0.5, 0.75, ((0, 2), (1, 16)))
    mlp_gain = jnp.clip(1.0 + 0.1 * jax.random.normal(seeds[9], (D,), jnp.float32), 0.5, 1.5).astype(jnp.bfloat16)
    w_gate = normal_values(seeds[10], (D, FF), D ** -0.5, 0.1875, ((0, 16), (1, 2)))
    w_up = normal_values(seeds[11], (D, FF), D ** -0.5, 0.1875, ((0, 16), (1, 2)))
    w_down = normal_values(seeds[12], (FF, D), FF ** -0.5, 0.109375, ((0, 2), (1, 16)))
    return {"hidden_in": hidden_in, "value_first": value_first, "segment_ids": segment_ids, "out_cotangent": out_cotangent, "attn_gain": attn_gain, "w_query": w_query, "w_key": w_key, "w_value": w_value, "w_output": w_output, "mlp_gain": mlp_gain, "w_gate": w_gate, "w_up": w_up, "w_down": w_down}


EPS = 1e-06
NEG = -1e+30

@jax.custom_vjp
def low(v):
    return lax.optimization_barrier(v.astype(jnp.bfloat16)).astype(jnp.float32)

@jax.custom_vjp
def low_back(v):
    return v

def low_keep(v):
    return (low(v), None)

def low_pass(kept, grad):
    return (grad,)

def back_keep(v):
    return (v, None)

def back_low(kept, grad):
    return (low(grad),)
low.defvjp(low_keep, low_pass)
low_back.defvjp(back_keep, back_low)

def product(left, right):
    return jnp.dot(left, right, precision=lax.Precision.HIGHEST)

def rms_norm(values, gain):
    factor = lax.rsqrt(lax.optimization_barrier(jnp.mean(values * values, axis=-1, keepdims=True)) + EPS)
    return values * factor * gain

def rotary_tables(length, head_size):
    half_head = head_size // 2
    frequency = 10000.0 ** (-(jnp.arange(half_head, dtype=jnp.float32) * 2.0 / head_size))
    angles = jnp.arange(length, dtype=jnp.float32)[:, None] * frequency[None, :]
    return (jnp.cos(angles)[:, None, :], jnp.sin(angles)[:, None, :])

def rotate(values, cosine_table, sine_table):
    half_head = values.shape[-1] // 2
    first_half = values[..., :half_head]
    second_half = values[..., half_head:]
    return jnp.concatenate([first_half * cosine_table - second_half * sine_table, second_half * cosine_table + first_half * sine_table], axis=-1)

def attend(query_heads, key_heads, value_heads, doc_ids):
    length = query_heads.shape[0]
    block_rows = min(512, length)
    block_count = length // block_rows
    score_scale = HEAD ** (-0.5)
    key_places = jnp.arange(length, dtype=jnp.int32)
    query_blocks = query_heads.reshape(block_count, block_rows, HEADS, HEAD)
    doc_blocks = doc_ids.reshape(block_count, block_rows)
    starts = jnp.arange(block_count, dtype=jnp.int32) * block_rows

    def one_block(items):
        query_block, doc_block, row_start = items
        raw_scores = jnp.einsum('qhe,khe->hqk', query_block, key_heads, precision=lax.Precision.HIGHEST) * score_scale
        raw_scores = low_back(raw_scores)
        query_places = row_start + jnp.arange(block_rows, dtype=jnp.int32)
        allowed = (key_places[None, :] <= query_places[:, None]) & (doc_block[:, None] == doc_ids[None, :])
        masked = jnp.where(allowed[None], raw_scores, NEG)
        row_max = lax.optimization_barrier(jnp.max(masked, axis=-1, keepdims=True))
        exponent = jnp.exp(masked - row_max)
        attn_probs = low(exponent / lax.optimization_barrier(jnp.sum(exponent, axis=-1, keepdims=True)))
        return jnp.einsum('hqk,khe->qhe', attn_probs, value_heads, precision=lax.Precision.HIGHEST)
    outputs = lax.map(jax.checkpoint(one_block), (query_blocks, doc_blocks, starts))
    return outputs.reshape(length, HEADS, HEAD)

def decoder_layer(doc_ids, hidden, first_values, attn_g, query_w, key_w, value_w, output_w, mlp_g, gate_w, up_w, down_w):
    length = hidden.shape[0]
    cosine_table, sine_table = rotary_tables(length, HEAD)
    normed_one = low(rms_norm(hidden, attn_g))
    query_lin = low_back(product(normed_one, query_w)).reshape(length, HEADS, HEAD)
    key_lin = low_back(product(normed_one, key_w)).reshape(length, HEADS, HEAD)
    query_heads = low(rotate(query_lin, cosine_table, sine_table))
    key_heads = low(rotate(key_lin, cosine_table, sine_table))
    value_lin = low_back(product(normed_one, value_w))
    value_heads = low(0.5 * value_lin + 0.5 * first_values).reshape(length, HEADS, HEAD)
    attended = attend(query_heads, key_heads, value_heads, doc_ids).reshape(length, D)
    attended = low(low_back(attended))
    middle = hidden + low_back(product(attended, output_w))
    normed_two = low(rms_norm(middle, mlp_g))
    gate_lin = low_back(product(normed_two, gate_w))
    up_lin = low_back(product(normed_two, up_w))
    hidden_units = low(gate_lin * jax.nn.sigmoid(gate_lin) * up_lin)
    return middle + low_back(product(hidden_units, down_w))

def reference(hidden_in, value_first, segment_ids, out_cotangent, attn_gain, w_query, w_key, w_value, w_output, mlp_gain, w_gate, w_up, w_down):
    params = tuple((weight.astype(jnp.float32) for weight in (attn_gain, w_query, w_key, w_value, w_output, mlp_gain, w_gate, w_up, w_down)))
    hidden_seqs = hidden_in.astype(jnp.float32).reshape(SEQS, SEQ, D)
    first_seqs = value_first.astype(jnp.float32).reshape(SEQS, SEQ, D)
    cot_seqs = out_cotangent.astype(jnp.float32).reshape(SEQS, SEQ, D)

    def scan_step(totals, items):
        hidden, first_values, doc_ids, cotangent = items

        def forward(hidden_x, first_x, attn_g, query_w, key_w, value_w, output_w, mlp_g, gate_w, up_w, down_w):
            return decoder_layer(doc_ids, hidden_x, first_x, attn_g, query_w, key_w, value_w, output_w, mlp_g, gate_w, up_w, down_w)
        result, pullback = jax.vjp(forward, hidden, first_values, params[0], params[1], params[2], params[3], params[4], params[5], params[6], params[7], params[8])
        grads = pullback(cotangent)
        new_totals = tuple((total + grad for total, grad in zip(totals, grads[2:])))
        return (new_totals, (result.astype(jnp.bfloat16), grads[0], grads[1]))
    zero_totals = tuple((jnp.zeros_like(weight) for weight in params))
    totals, outputs = lax.scan(scan_step, zero_totals, (hidden_seqs, first_seqs, segment_ids, cot_seqs))
    layer_out = outputs[0].reshape(TOKENS, D)
    grad_input = outputs[1].reshape(TOKENS, D)
    grad_value_first = outputs[2].reshape(TOKENS, D)
    return (layer_out, grad_input, grad_value_first, totals[0], totals[1], totals[2], totals[3], totals[4], totals[5], totals[6], totals[7], totals[8])
```

```python
import functools

import jax
import jax.numpy as jnp
from jax import lax
from jax.experimental import pallas as pl
from jax.experimental.pallas import tpu as pltpu
from jax.sharding import PartitionSpec as P

HEAD = 64
PIECE = 128
NEG = -1e30
BLK = 256
F32 = jnp.float32
BF16 = jnp.bfloat16


def dot_nt(a, b, precision=None):
    return lax.dot_general(a, b, (((1,), (1,)), ((), ())), precision=precision, preferred_element_type=F32)


def dot_nn(a, b):
    return jnp.dot(a, b, preferred_element_type=F32)


def bias_tile(starts_ref, first_key, first_query):
    keys = lax.broadcasted_iota(jnp.int32, (BLK, BLK), 0) + first_key
    queries = lax.broadcasted_iota(jnp.int32, (BLK, BLK), 1) + first_query
    allowed = (keys >= starts_ref[...]) & (keys <= queries)
    return jnp.where(allowed, 0.0, NEG)


def forward_kernel(heads, first_ref, starts_ref, q_ref, k_ref, vt_ref, out_ref, lse_ref, masked_q, bias_ref, top_ref, total_ref, acc_ref):
    step = pl.program_id(0)
    lane = lax.broadcasted_iota(jnp.int32, (BLK, 128), 1)
    for head in range(heads):
        pair = pl.ds((head // 2) * 128, 128)
        block = q_ref[:, pair]
        keep = (lane < 64) if head % 2 == 0 else (lane >= 64)
        masked_q[head] = jnp.where(keep, block, jnp.zeros_like(block))
    top_ref[...] = jnp.full_like(top_ref, NEG)
    total_ref[...] = jnp.zeros_like(total_ref)
    acc_ref[...] = jnp.zeros_like(acc_ref)

    def chunk(c, carry):
        base = pl.multiple_of(c * BLK, BLK)
        bias_ref[...] = bias_tile(starts_ref, base, step * BLK)
        for head in range(heads):
            keys = k_ref[pl.ds(base, BLK), pl.ds((head // 2) * 128, 128)]
            scores = dot_nt(keys, masked_q[head]) + bias_ref[...]
            old = top_ref[head : head + 1, :]
            new = jnp.maximum(old, jnp.max(scores, axis=0, keepdims=True))
            probs = jnp.exp(scores - new)
            shrink = jnp.exp(old - new)
            top_ref[head : head + 1, :] = new
            total_ref[head : head + 1, :] = total_ref[head : head + 1, :] * shrink + jnp.sum(probs, axis=0, keepdims=True)
            rows = slice(head * 64, head * 64 + 64)
            part = dot_nn(vt_ref[rows, pl.ds(base, BLK)], probs.astype(BF16))
            acc_ref[rows, :] = acc_ref[rows, :] * shrink + part
        return carry

    lax.fori_loop(first_ref[step], step + 1, chunk, 0)
    for head in range(heads):
        rows = slice(head * 64, head * 64 + 64)
        acc_ref[rows, :] = acc_ref[rows, :] / total_ref[head : head + 1, :]
    out_ref[...] = acc_ref[...].T.astype(BF16)
    lse_ref[...] = top_ref[...] + jnp.log(total_ref[...])


def attention_forward(first, starts, q, k, vt):
    length, width = q.shape
    heads = width // HEAD
    return pl.pallas_call(
        functools.partial(forward_kernel, heads),
        grid_spec=pltpu.PrefetchScalarGridSpec(
            num_scalar_prefetch=1,
            grid=(length // BLK,),
            in_specs=[
                pl.BlockSpec((1, BLK), lambda i, f: (0, i)),
                pl.BlockSpec((BLK, width), lambda i, f: (i, 0)),
                pl.BlockSpec((length, width), lambda i, f: (0, 0)),
                pl.BlockSpec((width, length), lambda i, f: (0, 0)),
            ],
            out_specs=[
                pl.BlockSpec((BLK, width), lambda i, f: (i, 0)),
                pl.BlockSpec((heads, BLK), lambda i, f: (0, i)),
            ],
            scratch_shapes=[
                pltpu.VMEM((heads, BLK, 128), BF16),
                pltpu.VMEM((BLK, BLK), F32),
                pltpu.VMEM((heads, BLK), F32),
                pltpu.VMEM((heads, BLK), F32),
                pltpu.VMEM((width, BLK), F32),
            ],
        ),
        out_shape=[
            jax.ShapeDtypeStruct((length, width), BF16),
            jax.ShapeDtypeStruct((heads, length), F32),
        ],
        compiler_params=pltpu.CompilerParams(dimension_semantics=("arbitrary",)),
        name="attention_forward",
    )(first, starts, q, k, vt)


def unrotate_lanes(block, cosine, sine, lane):
    other = jnp.where(lane % 64 < 32, pltpu.roll(block, 96, 1), pltpu.roll(block, 32, 1))
    return block * cosine - other * sine


def backward_kernel(heads, first_ref, starts_ref, q_ref, k_ref, kt_ref, v_ref, do_ref, o_ref, lse_ref, cosine_ref, sine_ref, cost_ref, sint_ref,
                    dq_ref, dk_ref, dv_ref, gv_ref, masked_q, masked_do, bias_ref, delta_ref, dqt_ref, dk_acc, dv_acc):
    step = pl.program_id(0)
    width = heads * HEAD
    lane = lax.broadcasted_iota(jnp.int32, (BLK, 128), 1)

    @pl.when(step == 0)
    def _():
        dk_acc[...] = jnp.zeros_like(dk_acc)
        dv_acc[...] = jnp.zeros_like(dv_acc)

    for head in range(heads):
        pair = pl.ds((head // 2) * 128, 128)
        keep = (lane < 64) if head % 2 == 0 else (lane >= 64)
        block = q_ref[:, pair]
        masked_q[head] = jnp.where(keep, block, jnp.zeros_like(block))
        block = do_ref[:, pair]
        masked_do[head] = jnp.where(keep, block, jnp.zeros_like(block))
    product = do_ref[...].astype(F32) * o_ref[...].astype(F32)
    chooser = (lax.broadcasted_iota(jnp.int32, (8, width), 1) // HEAD == lax.broadcasted_iota(jnp.int32, (8, width), 0)).astype(F32)
    delta_ref[...] = dot_nt(chooser, product, lax.Precision.HIGHEST)
    dqt_ref[...] = jnp.zeros_like(dqt_ref)

    def chunk(c, carry):
        base = pl.multiple_of(c * BLK, BLK)
        here = pl.ds(base, BLK)
        bias_ref[...] = bias_tile(starts_ref, base, step * BLK)
        for p in range(heads // 2):
            pair = pl.ds(p * 128, 128)
            keys = k_ref[here, pair]
            vals = v_ref[here, pair]
            probs_low, grads_low = [], []
            for head in (2 * p, 2 * p + 1):
                scores = dot_nt(keys, masked_q[head]) + bias_ref[...]
                probs = jnp.exp(scores - lse_ref[head : head + 1, :])
                prob_grad = dot_nt(vals, masked_do[head])
                score_grad = (probs * (prob_grad - delta_ref[head : head + 1, :])).astype(BF16)
                probs_low.append(probs.astype(BF16))
                grads_low.append(score_grad)
                rows = slice(head * 64, head * 64 + 64)
                dqt_ref[rows, :] += dot_nn(kt_ref[rows, here], score_grad)
            both = masked_do[2 * p : 2 * p + 2].reshape(2 * BLK, 128)
            dv_acc[here, pair] += dot_nn(jnp.concatenate(probs_low, axis=1), both)
            both = masked_q[2 * p : 2 * p + 2].reshape(2 * BLK, 128)
            dk_acc[here, pair] += dot_nn(jnp.concatenate(grads_low, axis=1), both)
        return carry

    lax.fori_loop(first_ref[step], step + 1, chunk, 0)
    cost, sint = cost_ref[...] * (HEAD**-0.5), sint_ref[...] * (HEAD**-0.5)
    for head in range(heads):
        low = dqt_ref[head * 64 : head * 64 + 32, :]
        high = dqt_ref[head * 64 + 32 : head * 64 + 64, :]
        dqt_ref[head * 64 : head * 64 + 32, :] = low * cost + high * sint
        dqt_ref[head * 64 + 32 : head * 64 + 64, :] = high * cost - low * sint
    dq_ref[...] = dqt_ref[...].T.astype(BF16)

    @pl.when(step == pl.num_programs(0) - 1)
    def _():
        def finish(c, carry):
            here = pl.ds(pl.multiple_of(c * BLK, BLK), BLK)
            for p in range(heads // 2):
                pair = pl.ds(p * 128, 128)
                dk_ref[here, pair] = unrotate_lanes(dk_acc[here, pair], cosine_ref[here, :], sine_ref[here, :], lane).astype(BF16)
                half = 0.5 * dv_acc[here, pair]
                gv_ref[here, pair] = half
                dv_ref[here, pair] = half.astype(BF16)
            return carry
        lax.fori_loop(0, dk_acc.shape[0] // BLK, finish, 0)


def attention_backward(first, starts, q, k, kt, v, do, o, lse, cosine, sine, cost, sint):
    length, width = q.shape
    heads = width // HEAD
    rows = pl.BlockSpec((BLK, width), lambda i, f: (i, 0))
    whole = pl.BlockSpec((length, width), lambda i, f: (0, 0))
    return pl.pallas_call(
        functools.partial(backward_kernel, heads),
        grid_spec=pltpu.PrefetchScalarGridSpec(
            num_scalar_prefetch=1,
            grid=(length // BLK,),
            in_specs=[
                pl.BlockSpec((1, BLK), lambda i, f: (0, i)),
                rows, whole,
                pl.BlockSpec((width, length), lambda i, f: (0, 0)),
                whole, rows, rows,
                pl.BlockSpec((heads, BLK), lambda i, f: (0, i)),
                pl.BlockSpec((length, 128), lambda i, f: (0, 0)),
                pl.BlockSpec((length, 128), lambda i, f: (0, 0)),
                pl.BlockSpec((32, BLK), lambda i, f: (0, i)),
                pl.BlockSpec((32, BLK), lambda i, f: (0, i)),
            ],
            out_specs=[rows, whole, whole, whole],
            scratch_shapes=[
                pltpu.VMEM((heads, BLK, 128), BF16),
                pltpu.VMEM((heads, BLK, 128), BF16),
                pltpu.VMEM((BLK, BLK), F32),
                pltpu.VMEM((8, BLK), F32),
                pltpu.VMEM((width, BLK), F32),
                pltpu.VMEM((length, width), F32),
                pltpu.VMEM((length, width), F32),
            ],
        ),
        out_shape=[
            jax.ShapeDtypeStruct((length, width), BF16),
            jax.ShapeDtypeStruct((length, width), BF16),
            jax.ShapeDtypeStruct((length, width), BF16),
            jax.ShapeDtypeStruct((length, width), F32),
        ],
        compiler_params=pltpu.CompilerParams(dimension_semantics=("arbitrary",)),
        name="attention_backward",
    )(first, starts, q, k, kt, v, do, o, lse, cosine, sine, cost, sint)

def feedforward_kernel(width, n_ref, nt_ref, y_ref, yt_ref, w_ref, out_ref, e_ref, g_ref, h_ref, dg_ref, du_ref):
    step = pl.program_id(0)
    rows = n_ref.shape[0]
    tile = 256 if rows % 256 == 0 else rows

    @pl.when(step == 0)
    def _():
        out_ref[...] = jnp.zeros_like(out_ref)
        e_ref[...] = jnp.zeros_like(e_ref)

    def weight(which):
        cols = slice(which * PIECE, which * PIECE + PIECE)
        return jnp.concatenate([w_ref[:, side, :, cols].reshape(width, PIECE) for side in range(2)], axis=1)

    gate_w, up_w, down_w = weight(0), weight(1), weight(2)

    def row_block(i, carry):
        here = pl.ds(pl.multiple_of(i * tile, tile), tile)
        gate = dot_nn(n_ref[here, :], gate_w)
        up = dot_nn(n_ref[here, :], up_w)
        dhid = dot_nn(y_ref[here, :], down_w)
        sig = 1.0 / (1.0 + jnp.exp(-gate))
        silu = gate * sig
        hidden = (silu * up).astype(BF16)
        dgate = (dhid * up * (sig * (1.0 + gate * (1.0 - sig)))).astype(BF16)
        dup = (dhid * silu).astype(BF16)
        h_ref[here, :] = hidden
        dg_ref[here, :] = dgate
        du_ref[here, :] = dup
        out_ref[here, :] += dot_nt(hidden, down_w)
        e_ref[here, :] += dot_nt(dgate, gate_w) + dot_nt(dup, up_w)
        return carry

    lax.fori_loop(0, rows // tile, row_block, 0)
    for which, (left, right) in enumerate(((nt_ref, dg_ref), (nt_ref, du_ref), (yt_ref, h_ref))):
        cols = slice(which * PIECE, which * PIECE + PIECE)
        grad = dot_nn(left[...], right[...]).astype(BF16)
        for side in range(2):
            g_ref[:, side, :, cols] = grad[:, side * PIECE : side * PIECE + PIECE].reshape(g_ref.shape[0], g_ref.shape[2], PIECE)


def feedforward(n, y, w, steps):
    rows, width = n.shape
    outer, _, inner, _ = w.shape
    full = lambda shape: pl.BlockSpec(shape, lambda j: (0, 0), pipeline_mode=pl.Buffered(1))
    block = pl.BlockSpec((outer, 2, inner, 3 * PIECE), lambda j: (0, 0, 0, j))
    flops = 18 * rows * width * steps * 2 * PIECE
    return pl.pallas_call(
        functools.partial(feedforward_kernel, width),
        grid=(steps,),
        in_specs=[full((rows, width)), full((width, rows)), full((rows, width)), full((width, rows)), block],
        out_specs=[pl.BlockSpec((rows, width), lambda j: (0, 0)), pl.BlockSpec((rows, width), lambda j: (0, 0)), block],
        out_shape=[
            jax.ShapeDtypeStruct((rows, width), F32),
            jax.ShapeDtypeStruct((rows, width), F32),
            jax.ShapeDtypeStruct(w.shape, BF16),
        ],
        scratch_shapes=[pltpu.VMEM((rows, 2 * PIECE), BF16)] * 3,
        compiler_params=pltpu.CompilerParams(dimension_semantics=("arbitrary",), vmem_limit_bytes=60 << 20),
        cost_estimate=pl.CostEstimate(flops=flops, bytes_accessed=40 << 20, transcendentals=rows * steps * 256),
        name="feedforward",
    )(n, n.T, y, y.T, w)


def project_kernel(heads, x_ref, w_ref, first_ref, cosine_ref, sine_ref, q_ref, k_ref, v_ref, kt_ref, vt_ref):
    width = heads * 64
    lin = dot_nn(x_ref[...], w_ref[:, : 3 * width])
    lane = lax.broadcasted_iota(jnp.int32, (x_ref.shape[0], 128), 1)
    first = lane % 64 < 32
    cosine, sine = cosine_ref[...], sine_ref[...]
    for p in range(width // 128):
        cols = slice(p * 128, p * 128 + 128)
        for base, ref, scale in ((0, q_ref, 0.125), (width, k_ref, None)):
            u = lin[:, base + p * 128 : base + p * 128 + 128]
            other = jnp.where(first, pltpu.roll(u, 96, 1), pltpu.roll(u, 32, 1))
            turned = u * cosine + other * sine
            if scale is not None:
                turned = turned * scale
            ref[:, cols] = turned.astype(BF16)
    v_ref[...] = (0.5 * lin[:, 2 * width : 3 * width] + 0.5 * first_ref[...].astype(F32)).astype(BF16)
    kt_ref[...] = k_ref[...].T
    vt_ref[...] = v_ref[...].T


def project(x, w, first, cosine, sine, width):
    length, depth = x.shape
    block = min(256, length)
    rows = lambda n: pl.BlockSpec((block, n), lambda i: (i, 0))
    out = jax.ShapeDtypeStruct((length, width), BF16)
    turned = jax.ShapeDtypeStruct((width, length), BF16)
    across = pl.BlockSpec((width, block), lambda i: (0, i))
    return pl.pallas_call(
        functools.partial(project_kernel, width // 64),
        grid=(length // block,),
        in_specs=[rows(depth), pl.BlockSpec(w.shape, lambda i: (0, 0), pipeline_mode=pl.Buffered(1)), rows(width), rows(128), rows(128)],
        out_specs=[rows(width)] * 3 + [across] * 2,
        out_shape=[out] * 3 + [turned] * 2,
        compiler_params=pltpu.CompilerParams(dimension_semantics=("arbitrary",), vmem_limit_bytes=60 << 20),
        cost_estimate=pl.CostEstimate(flops=6 * length * depth * width, bytes_accessed=20 << 20, transcendentals=0),
        name="project",
    )(x, w, first, cosine, sine)


EPS = 1e-06
BOTH = ("dp", "tensor")


def norm_parts(values):
    factor = lax.rsqrt(jnp.mean(values * values, axis=-1, keepdims=True) + EPS)
    return values * factor, factor


def norm_back(incoming, gain, normalized, factor):
    scaled = incoming * gain
    gain_grad = jnp.sum(incoming * normalized, axis=0)
    input_grad = factor * (scaled - normalized * jnp.mean(scaled * normalized, axis=-1, keepdims=True))
    return input_grad, gain_grad


def swap(values):
    return lax.ppermute(values, "tensor", [(0, 1), (1, 0)])


def part(values, index, count, axis):
    size = values.shape[axis] // count
    return lax.dynamic_slice_in_dim(values, index * size, size, axis)


def in_order(mine, theirs, axis):
    first = lax.axis_index("tensor") == 0
    return jnp.concatenate([jnp.where(first, mine, theirs), jnp.where(first, theirs, mine)], axis=axis)


def gather_rows(rows, count):
    if count != 2:
        return lax.all_gather(rows, "tensor", axis=0, tiled=True)
    return in_order(rows, swap(rows), 0)


def heads_to_rows(values, count):
    if count != 2:
        return lax.all_to_all(values, "tensor", split_axis=0, concat_axis=1, tiled=True)
    me = lax.axis_index("tensor")
    theirs = swap(part(values, 1 - me, 2, 0))
    return in_order(part(values, me, 2, 0), theirs, 1)


def rows_to_heads(values, count):
    if count != 2:
        return lax.all_to_all(values, "tensor", split_axis=1, concat_axis=0, tiled=True)
    me = lax.axis_index("tensor")
    theirs = swap(part(values, 1 - me, 2, 1))
    return in_order(part(values, me, 2, 1), theirs, 0)


def scatter_product(left, weight, count):
    product = lambda rows: dot_nt(rows, weight)
    if count != 2:
        return lax.psum_scatter(product(left), "tensor", scatter_dimension=0, tiled=True)
    me = lax.axis_index("tensor")
    theirs = swap(product(part(left, 1 - me, 2, 0)).astype(BF16))
    return product(part(left, me, 2, 0)) + theirs.astype(F32)


def tensor_sum(values, count):
    if count != 2:
        return lax.psum(values, "tensor")
    return values + swap(values)


def pack_hidden(gate, up, down, blocks):
    rows = gate.shape[0]
    stacked = jnp.stack([w.reshape(rows, blocks, -1) for w in (gate, up, down)], axis=2)
    return stacked.reshape(rows, -1)


def unpack_hidden(packed, blocks):
    rows = packed.shape[0]
    pieces = packed.reshape(rows, blocks, 3, -1)
    return [pieces[:, :, which].reshape(rows, -1) for which in range(3)]


def per_device(dp, count, hidden_in, value_first, segment_ids, out_cotangent, attn_gain, w_query, w_key, w_value, w_output, mlp_gain, w_gate, w_up, w_down):
    rows, depth = hidden_in.shape
    width = w_query.shape[1]
    length = segment_ids.shape[1]
    slab = w_query.shape[0]
    blocks = w_gate.shape[1] * count // 256
    hidden_columns = 3 * w_gate.shape[1]

    gains = jnp.pad(jnp.stack([attn_gain, mlp_gain], axis=1), ((0, 0), (0, 126)))
    first_pack = jnp.concatenate([w_query, w_key, w_value, gains], axis=1)
    first_all = lax.all_gather(first_pack, "dp", axis=0, tiled=True)
    second_pack = jnp.concatenate([pack_hidden(w_gate, w_up, w_down.T, blocks), w_output.T], axis=1)
    second_pack, first_all = lax.optimization_barrier((second_pack, first_all))
    second_all = lax.all_gather(second_pack, BOTH, axis=0, tiled=True).reshape(dp, count, slab, -1)
    gain_one = first_all[:, 3 * width].astype(F32)
    gain_two = first_all[:, 3 * width + 1].astype(F32)

    doc_ids = segment_ids[0]
    counts = [jnp.sum(doc_ids < d) for d in (1, 2, 3)]
    starts = jnp.where(doc_ids == 1, counts[0], jnp.where(doc_ids == 2, counts[1], jnp.where(doc_ids == 3, counts[2], 0))).astype(jnp.int32)
    first = starts[::BLK] // BLK
    starts = starts[None, :]
    frequency = 10000.0 ** (-(jnp.arange(HEAD // 2, dtype=F32) * 2.0 / HEAD))
    angles = jnp.arange(length, dtype=F32)[:, None] * frequency[None, :]
    cos, sin = jnp.cos(angles), jnp.sin(angles)
    cosine = jnp.concatenate([cos] * 4, axis=1)
    sine = jnp.concatenate([-sin, sin] * 2, axis=1)
    cost, sint = cos.T, sin.T

    residual = hidden_in.astype(F32)
    flat_one, factor_one = norm_parts(residual)
    rows_one = gather_rows((flat_one * gain_one).astype(BF16), count)
    query, key, value, key_t, value_t = project(rows_one, first_all, value_first, cosine, sine, width)
    attended, log_totals = attention_forward(first, starts, query, key, value_t)
    attended_rows = heads_to_rows(attended, count)
    output_w = second_all[:, :, :, hidden_columns:].transpose(0, 2, 1, 3).reshape(depth, count * width)
    middle = residual + dot_nt(attended_rows, output_w)

    flat_two, factor_two = norm_parts(middle)
    normed_two = (flat_two * gain_two).astype(BF16)
    if count == 2:
        hidden_w = second_all
    else:
        hidden_w = second_all[:, :, :, :hidden_columns].reshape(dp, 2, count // 2, slab, blocks, 3, -1)
        hidden_w = hidden_w.transpose(1, 0, 3, 4, 5, 2, 6).reshape(1, 2, depth, blocks * 3 * PIECE)
    branch, normed_two_grad, hidden_grads = feedforward(normed_two, out_cotangent, hidden_w, blocks)
    layer_out = (middle + branch).astype(BF16)
    middle_norm_grad, gain_two_grad = norm_back(normed_two_grad, gain_two, flat_two, factor_two)
    middle_grad = out_cotangent.astype(F32) + middle_norm_grad
    branch_grad = middle_grad.astype(BF16)

    attended_grad = rows_to_heads(dot_nn(branch_grad, output_w).astype(BF16), count)
    output_grad = lax.dot_general(branch_grad, attended_rows, (((0,), (0,)), ((), ())), preferred_element_type=F32).astype(BF16)
    output_grad = output_grad.reshape(dp, slab, count, width).transpose(0, 2, 1, 3)
    if count == 2:
        second_grads = hidden_grads.at[:, :, :, hidden_columns:].set(output_grad)
    else:
        hidden_grads = hidden_grads.reshape(2, dp, slab, blocks, 3, count // 2, -1).transpose(1, 0, 5, 2, 3, 4, 6)
        second_grads = jnp.concatenate([hidden_grads.reshape(dp, count, slab, -1), output_grad], axis=3)
    second_sum = lax.psum_scatter(second_grads.reshape(dp * count * slab, -1), BOTH, scatter_dimension=0, tiled=True).astype(F32)
    query_pre, key_pre, value_pre, grad_value_first = attention_backward(
        first, starts, query, key, key_t, value, attended_grad, attended, log_totals, cosine, sine, cost, sint
    )
    pre = jnp.concatenate([query_pre, key_pre, value_pre], axis=1)
    normed_one_grad = scatter_product(pre, first_all[:, : 3 * width], count)
    input_norm_grad, gain_one_grad = norm_back(normed_one_grad, gain_one, flat_one, factor_one)
    grad_input = middle_grad + input_norm_grad
    gain_grads = tensor_sum(jnp.stack([gain_one_grad, gain_two_grad]), count)
    gain_grads = jnp.pad(gain_grads.T.astype(BF16), ((0, 0), (0, 126)))
    projection_grads = lax.dot_general(rows_one, pre, (((0,), (0,)), ((), ())), preferred_element_type=F32).astype(BF16)
    first_sum = lax.psum_scatter(jnp.concatenate([projection_grads, gain_grads], axis=1), "dp", scatter_dimension=0, tiled=True).astype(F32)
    grad_gate, grad_up, grad_down = unpack_hidden(second_sum[:, :hidden_columns], blocks)
    return (
        layer_out,
        grad_input,
        grad_value_first,
        first_sum[:, 3 * width],
        first_sum[:, :width],
        first_sum[:, width : 2 * width],
        first_sum[:, 2 * width : 3 * width],
        second_sum[:, hidden_columns:].T,
        first_sum[:, 3 * width + 1],
        grad_gate,
        grad_up,
        grad_down.T,
    )


def solution(mesh):
    tokens, split = P(BOTH, None), P("dp", "tensor")
    across = P("tensor", "dp")
    return jax.shard_map(
        functools.partial(per_device, mesh.shape["dp"], mesh.shape["tensor"]),
        mesh=mesh,
        in_specs=(tokens, split, P("dp", None), tokens, P("dp"), split, split, split, across, P("dp"), split, split, across),
        out_specs=(tokens, tokens, split, P("dp"), split, split, split, across, P("dp"), split, split, across),
        check_vma=False,
    )
```

```python
import functools

import jax
import jax.numpy as jnp
from jax import lax
from jax.experimental import pallas as pl
from jax.experimental.pallas import tpu as pltpu
from jax.sharding import PartitionSpec as P

HEAD = 64
PIECE = 128
NEG = -1e30
BLK = 256
F32 = jnp.float32
BF16 = jnp.bfloat16


def dot_nt(a, b, precision=None):
    return lax.dot_general(a, b, (((1,), (1,)), ((), ())), precision=precision, preferred_element_type=F32)


def dot_nn(a, b):
    return jnp.dot(a, b, preferred_element_type=F32)


def bias_tile(starts_ref, first_key, first_query):
    keys = lax.broadcasted_iota(jnp.int32, (BLK, BLK), 0) + first_key
    queries = lax.broadcasted_iota(jnp.int32, (BLK, BLK), 1) + first_query
    allowed = (keys >= starts_ref[...]) & (keys <= queries)
    return jnp.where(allowed, 0.0, NEG)


def forward_kernel(heads, first_ref, starts_ref, q_ref, k_ref, vt_ref, out_ref, lse_ref, masked_q, bias_ref, top_ref, total_ref, acc_ref):
    step = pl.program_id(0)
    lane = lax.broadcasted_iota(jnp.int32, (BLK, 128), 1)
    for head in range(heads):
        pair = pl.ds((head // 2) * 128, 128)
        block = q_ref[:, pair]
        keep = (lane < 64) if head % 2 == 0 else (lane >= 64)
        masked_q[head] = jnp.where(keep, block, jnp.zeros_like(block))
    top_ref[...] = jnp.full_like(top_ref, NEG)
    total_ref[...] = jnp.zeros_like(total_ref)
    acc_ref[...] = jnp.zeros_like(acc_ref)

    def chunk(c, carry):
        base = pl.multiple_of(c * BLK, BLK)
        bias_ref[...] = bias_tile(starts_ref, base, step * BLK)
        for head in range(heads):
            keys = k_ref[pl.ds(base, BLK), pl.ds((head // 2) * 128, 128)]
            scores = dot_nt(keys, masked_q[head]) + bias_ref[...]
            old = top_ref[head : head + 1, :]
            new = jnp.maximum(old, jnp.max(scores, axis=0, keepdims=True))
            probs = jnp.exp(scores - new)
            shrink = jnp.exp(old - new)
            top_ref[head : head + 1, :] = new
            total_ref[head : head + 1, :] = total_ref[head : head + 1, :] * shrink + jnp.sum(probs, axis=0, keepdims=True)
            rows = slice(head * 64, head * 64 + 64)
            part = dot_nn(vt_ref[rows, pl.ds(base, BLK)], probs.astype(BF16))
            acc_ref[rows, :] = acc_ref[rows, :] * shrink + part
        return carry

    lax.fori_loop(first_ref[step], step + 1, chunk, 0)
    for head in range(heads):
        rows = slice(head * 64, head * 64 + 64)
        acc_ref[rows, :] = acc_ref[rows, :] / total_ref[head : head + 1, :]
    out_ref[...] = acc_ref[...].T.astype(BF16)
    lse_ref[...] = (top_ref[...] + jnp.log(total_ref[...])).reshape(lse_ref.shape)


def attention_forward(first, starts, q, k, vt):
    length, width = q.shape
    heads = width // HEAD
    return pl.pallas_call(
        functools.partial(forward_kernel, heads),
        grid_spec=pltpu.PrefetchScalarGridSpec(
            num_scalar_prefetch=1,
            grid=(length // BLK,),
            in_specs=[
                pl.BlockSpec((1, BLK), lambda i, f: (0, i)),
                pl.BlockSpec((BLK, width), lambda i, f: (i, 0)),
                pl.BlockSpec((length, width), lambda i, f: (0, 0)),
                pl.BlockSpec((width, length), lambda i, f: (0, 0)),
            ],
            out_specs=[
                pl.BlockSpec((BLK, width), lambda i, f: (i, 0)),
                pl.BlockSpec((heads // 2, 2, BLK), lambda i, f: (0, 0, i)),
            ],
            scratch_shapes=[
                pltpu.VMEM((heads, BLK, 128), BF16),
                pltpu.VMEM((BLK, BLK), F32),
                pltpu.VMEM((heads, BLK), F32),
                pltpu.VMEM((heads, BLK), F32),
                pltpu.VMEM((width, BLK), F32),
            ],
        ),
        out_shape=[
            jax.ShapeDtypeStruct((length, width), BF16),
            jax.ShapeDtypeStruct((heads // 2, 2, length), F32),
        ],
        compiler_params=pltpu.CompilerParams(dimension_semantics=("arbitrary",)),
        name="attention_forward",
    )(first, starts, q, k, vt)


def unrotate_lanes(block, cosine, sine, lane):
    other = jnp.where(lane % 64 < 32, pltpu.roll(block, 96, 1), pltpu.roll(block, 32, 1))
    return block * cosine - other * sine


def backward_kernel(first_ref, starts_ref, q_ref, k_ref, kt_ref, v_ref, do_ref, o_ref, lse_ref, cosine_ref, sine_ref, cost_ref, sint_ref,
                    pre_ref, gv_ref, masked_q, masked_do, bias_ref, delta_ref, dqt_ref, dk_acc, dv_acc):
    step = pl.program_id(0)
    lane = lax.broadcasted_iota(jnp.int32, (BLK, 128), 1)

    @pl.when(step == 0)
    def _():
        dk_acc[...] = jnp.zeros_like(dk_acc)
        dv_acc[...] = jnp.zeros_like(dv_acc)

    for head in range(2):
        keep = (lane < 64) if head == 0 else (lane >= 64)
        masked_q[head] = jnp.where(keep, q_ref[...], jnp.zeros_like(q_ref))
        masked_do[head] = jnp.where(keep, do_ref[...], jnp.zeros_like(do_ref))
    product = do_ref[...].astype(F32) * o_ref[...].astype(F32)
    chooser = (lax.broadcasted_iota(jnp.int32, (8, 128), 1) // HEAD == lax.broadcasted_iota(jnp.int32, (8, 128), 0)).astype(F32)
    delta_ref[...] = dot_nt(chooser, product, lax.Precision.HIGHEST)
    dqt_ref[...] = jnp.zeros_like(dqt_ref)
    both_q = masked_q[...].reshape(2 * BLK, 128)
    both_do = masked_do[...].reshape(2 * BLK, 128)

    def chunk(c, carry):
        here = pl.ds(pl.multiple_of(c * BLK, BLK), BLK)
        bias_ref[...] = bias_tile(starts_ref, c * BLK, step * BLK)
        keys = k_ref[here, :]
        vals = v_ref[here, :]
        probs_low, grads_low = [], []
        for head in range(2):
            scores = dot_nt(keys, masked_q[head]) + bias_ref[...]
            probs = jnp.exp(scores - lse_ref[0, head : head + 1, :])
            prob_grad = dot_nt(vals, masked_do[head])
            score_grad = (probs * (prob_grad - delta_ref[head : head + 1, :])).astype(BF16)
            probs_low.append(probs.astype(BF16))
            grads_low.append(score_grad)
            rows = slice(head * 64, head * 64 + 64)
            dqt_ref[rows, :] += dot_nn(kt_ref[rows, here], score_grad)
        dv_acc[here, :] += dot_nn(jnp.concatenate(probs_low, axis=1), both_do)
        dk_acc[here, :] += dot_nn(jnp.concatenate(grads_low, axis=1), both_q)
        return carry

    lax.fori_loop(first_ref[step], step + 1, chunk, 0)
    cost, sint = cost_ref[...] * (HEAD**-0.5), sint_ref[...] * (HEAD**-0.5)
    for head in range(2):
        low = dqt_ref[head * 64 : head * 64 + 32, :]
        high = dqt_ref[head * 64 + 32 : head * 64 + 64, :]
        dqt_ref[head * 64 : head * 64 + 32, :] = low * cost + high * sint
        dqt_ref[head * 64 + 32 : head * 64 + 64, :] = high * cost - low * sint
    pre_ref[pl.ds(pl.multiple_of(step * BLK, BLK), BLK), :128] = dqt_ref[...].T.astype(BF16)

    @pl.when(step == pl.num_programs(0) - 1)
    def _():
        def finish(c, carry):
            here = pl.ds(pl.multiple_of(c * BLK, BLK), BLK)
            pre_ref[here, 128:256] = unrotate_lanes(dk_acc[here, :], cosine_ref[here, :], sine_ref[here, :], lane).astype(BF16)
            half = 0.5 * dv_acc[here, :]
            gv_ref[here, :] = half
            pre_ref[here, 256:] = half.astype(BF16)
            return carry
        lax.fori_loop(0, dk_acc.shape[0] // BLK, finish, 0)


def attention_backward(pair, first, starts, q, k, kt, v, do, o, lse, cosine, sine, cost, sint):
    length = q.shape[0]
    rows = pl.BlockSpec((BLK, 128), lambda i, f: (i, pair))
    whole = pl.BlockSpec((length, 128), lambda i, f: (0, pair))
    table = pl.BlockSpec((length, 128), lambda i, f: (0, 0))
    tile = length * BLK * 2 * 3
    return pl.pallas_call(
        backward_kernel,
        grid_spec=pltpu.PrefetchScalarGridSpec(
            num_scalar_prefetch=1,
            grid=(length // BLK,),
            in_specs=[
                pl.BlockSpec((1, BLK), lambda i, f: (0, i)),
                rows, whole,
                pl.BlockSpec((128, length), lambda i, f: (pair, 0)),
                whole, rows, rows,
                pl.BlockSpec((1, 2, BLK), lambda i, f: (pair, 0, i)),
                table, table,
                pl.BlockSpec((32, BLK), lambda i, f: (0, i)),
                pl.BlockSpec((32, BLK), lambda i, f: (0, i)),
            ],
            out_specs=[pl.BlockSpec((length, 384), lambda i, f: (0, 0)), table],
            scratch_shapes=[
                pltpu.VMEM((2, BLK, 128), BF16),
                pltpu.VMEM((2, BLK, 128), BF16),
                pltpu.VMEM((BLK, BLK), F32),
                pltpu.VMEM((8, BLK), F32),
                pltpu.VMEM((128, BLK), F32),
                pltpu.VMEM((length, 128), F32),
                pltpu.VMEM((length, 128), F32),
            ],
        ),
        out_shape=[jax.ShapeDtypeStruct((length, 384), BF16), jax.ShapeDtypeStruct((length, 128), F32)],
        compiler_params=pltpu.CompilerParams(dimension_semantics=("arbitrary",)),
        cost_estimate=pl.CostEstimate(flops=tile * 128 * 32, bytes_accessed=8 << 20, transcendentals=tile),
        name="attention_backward",
    )(first, starts, q, k, kt, v, do, o, lse, cosine, sine, cost, sint)

def feedforward_kernel(width, chained, side_ref, n_ref, nt_ref, y_ref, yt_ref, w_ref, *refs):
    if chained:
        out_in, e_in, *refs = refs
    out_ref, e_ref, keep_ref, send_ref, h_ref, dg_ref, du_ref = refs
    step = pl.program_id(0)
    rows = n_ref.shape[0]
    tile = 256 if rows % 256 == 0 else rows

    @pl.when(step == 0)
    def _():
        out_ref[...] = out_in[...] if chained else jnp.zeros_like(out_ref)
        e_ref[...] = e_in[...] if chained else jnp.zeros_like(e_ref)

    def weight(which):
        cols = slice(which * PIECE, which * PIECE + PIECE)
        return jnp.concatenate([w_ref[:, side, :, cols].reshape(width, PIECE) for side in range(2)], axis=1)

    gate_w, up_w, down_w = weight(0), weight(1), weight(2)

    def row_block(i, carry):
        here = pl.ds(pl.multiple_of(i * tile, tile), tile)
        gate = dot_nn(n_ref[here, :], gate_w)
        up = dot_nn(n_ref[here, :], up_w)
        dhid = dot_nn(y_ref[here, :], down_w)
        sig = 1.0 / (1.0 + jnp.exp(-gate))
        silu = gate * sig
        hidden = (silu * up).astype(BF16)
        dgate = (dhid * up * (sig * (1.0 + gate * (1.0 - sig)))).astype(BF16)
        dup = (dhid * silu).astype(BF16)
        h_ref[here, :] = hidden
        dg_ref[here, :] = dgate
        du_ref[here, :] = dup
        out_ref[here, :] += dot_nt(hidden, down_w)
        e_ref[here, :] += dot_nt(dgate, gate_w) + dot_nt(dup, up_w)
        return carry

    lax.fori_loop(0, rows // tile, row_block, 0)
    swapped = side_ref[0] != 0
    for which, (left, right) in enumerate(((nt_ref, dg_ref), (nt_ref, du_ref), (yt_ref, h_ref))):
        cols = slice(which * PIECE, which * PIECE + PIECE)
        grad = dot_nn(left[...], right[...])
        low, high = grad[:, :PIECE], grad[:, PIECE:]
        keep_ref[:, cols] = jnp.where(swapped, high, low).astype(BF16)
        send_ref[:, cols] = jnp.where(swapped, low, high).astype(BF16)


def feedforward(side, n, nt, y, yt, w, start, steps, partial=None):
    rows, width = n.shape
    outer, _, inner, _ = w.shape
    chained = partial is not None
    full = lambda shape: pl.BlockSpec(shape, lambda j, s: (0, 0), pipeline_mode=pl.Buffered(1))
    grads = pl.BlockSpec((width, 3 * PIECE), lambda j, s: (0, j))
    total = pl.BlockSpec((rows, width), lambda j, s: (0, 0))
    grads_shape = jax.ShapeDtypeStruct((width, steps * 3 * PIECE), BF16)
    flops = 18 * rows * width * steps * 2 * PIECE
    return pl.pallas_call(
        functools.partial(feedforward_kernel, width, chained),
        grid_spec=pltpu.PrefetchScalarGridSpec(
            num_scalar_prefetch=1,
            grid=(steps,),
            in_specs=[
                full((rows, width)), full((width, rows)), full((rows, width)), full((width, rows)),
                pl.BlockSpec((outer, 2, inner, 3 * PIECE), lambda j, s: (0, 0, 0, j + start)),
            ] + ([full((rows, width))] * 2 if chained else []),
            out_specs=[total, total, grads, grads],
            scratch_shapes=[pltpu.VMEM((rows, 2 * PIECE), BF16)] * 3,
        ),
        out_shape=[jax.ShapeDtypeStruct((rows, width), F32)] * 2 + [grads_shape] * 2,
        compiler_params=pltpu.CompilerParams(dimension_semantics=("arbitrary",), vmem_limit_bytes=60 << 20),
        cost_estimate=pl.CostEstimate(flops=flops, bytes_accessed=40 << 20, transcendentals=rows * steps * 256),
        name="feedforward",
    )(side, n, nt, y, yt, w, *(partial or ()))


def project_kernel(pairs, sizes, x_ref, *refs):
    weights, refs = refs[: len(sizes)], refs[len(sizes) :]
    first_ref, cosine_ref, sine_ref, q_ref, k_ref, v_ref, kt_ref, vt_ref = refs
    lane = lax.broadcasted_iota(jnp.int32, (x_ref.shape[0], 128), 1)
    first = lane % 64 < 32
    cosine, sine = cosine_ref[...], sine_ref[...]

    def turn(u):
        return u * cosine + jnp.where(first, pltpu.roll(u, 96, 1), pltpu.roll(u, 32, 1)) * sine

    pair = 0
    for ref, size in zip(weights, sizes):
        lin = dot_nn(x_ref[...], ref[:, : size * 384])
        for p in range(size):
            cols = slice(pair * 128, pair * 128 + 128)
            q_ref[:, cols] = (turn(lin[:, p * 384 : p * 384 + 128]) * 0.125).astype(BF16)
            k_ref[:, cols] = turn(lin[:, p * 384 + 128 : p * 384 + 256]).astype(BF16)
            v_ref[:, cols] = (0.5 * lin[:, p * 384 + 256 : p * 384 + 384] + 0.5 * first_ref[:, cols].astype(F32)).astype(BF16)
            pair += 1
    kt_ref[...] = k_ref[...].T
    vt_ref[...] = v_ref[...].T


def project(x, weights, sizes, first, cosine, sine):
    length, depth = x.shape
    width = first.shape[1]
    block = min(256, length)
    rows = lambda n: pl.BlockSpec((block, n), lambda i: (i, 0))
    out = jax.ShapeDtypeStruct((length, width), BF16)
    turned = jax.ShapeDtypeStruct((width, length), BF16)
    across = pl.BlockSpec((width, block), lambda i: (0, i))
    return pl.pallas_call(
        functools.partial(project_kernel, width // 128, sizes),
        grid=(length // block,),
        in_specs=[rows(depth)] + [pl.BlockSpec(w.shape, lambda i: (0, 0), pipeline_mode=pl.Buffered(1)) for w in weights] + [rows(width), rows(128), rows(128)],
        out_specs=[rows(width)] * 3 + [across] * 2,
        out_shape=[out] * 3 + [turned] * 2,
        compiler_params=pltpu.CompilerParams(dimension_semantics=("arbitrary",), vmem_limit_bytes=60 << 20),
        cost_estimate=pl.CostEstimate(flops=6 * length * depth * width, bytes_accessed=20 << 20, transcendentals=0),
        name="project",
    )(x, *weights, first, cosine, sine)


EPS = 1e-06
BOTH = ("dp", "tensor")


def norm_parts(values):
    factor = lax.rsqrt(jnp.mean(values * values, axis=-1, keepdims=True) + EPS)
    return values * factor, factor


def norm_back(incoming, gain, normalized, factor):
    scaled = incoming * gain
    gain_grad = jnp.sum(incoming * normalized, axis=0)
    input_grad = factor * (scaled - normalized * jnp.mean(scaled * normalized, axis=-1, keepdims=True))
    return input_grad, gain_grad


def swap(values):
    return lax.ppermute(values, "tensor", [(0, 1), (1, 0)])


def part(values, index, count, axis):
    size = values.shape[axis] // count
    return lax.dynamic_slice_in_dim(values, index * size, size, axis)


def in_order(mine, theirs, axis):
    first = lax.axis_index("tensor") == 0
    return jnp.concatenate([jnp.where(first, mine, theirs), jnp.where(first, theirs, mine)], axis=axis)


def gather_rows(rows, count):
    if count != 2:
        return lax.all_gather(rows, "tensor", axis=0, tiled=True)
    return in_order(rows, swap(rows), 0)


def heads_to_rows(values, count):
    if count != 2:
        return lax.all_to_all(values, "tensor", split_axis=0, concat_axis=1, tiled=True)
    me = lax.axis_index("tensor")
    theirs = swap(part(values, 1 - me, 2, 0))
    return in_order(part(values, me, 2, 0), theirs, 1)


def rows_to_heads(values, count):
    if count != 2:
        return lax.all_to_all(values, "tensor", split_axis=1, concat_axis=0, tiled=True)
    me = lax.axis_index("tensor")
    theirs = swap(part(values, 1 - me, 2, 1))
    return in_order(part(values, me, 2, 1), theirs, 0)


def scatter_product(left, weights, count):
    def product(rows):
        total, start = 0.0, 0
        for weight in weights:
            size = weight.shape[1]
            total = total + dot_nt(rows[:, start : start + size], weight)
            start += size
        return total

    if count != 2:
        return lax.psum_scatter(product(left), "tensor", scatter_dimension=0, tiled=True)
    me = lax.axis_index("tensor")
    theirs = swap(product(part(left, 1 - me, 2, 0)).astype(BF16))
    return product(part(left, me, 2, 0)) + theirs.astype(F32)


def tensor_sum(values, count):
    if count != 2:
        return lax.psum(values, "tensor")
    return values + swap(values)


def pack_hidden(gate, up, down, blocks):
    rows = gate.shape[0]
    stacked = jnp.stack([w.reshape(rows, blocks, -1) for w in (gate, up, down)], axis=2)
    return stacked.reshape(rows, -1)


def unpack_hidden(packed, blocks):
    rows = packed.shape[0]
    pieces = packed.reshape(rows, blocks, 3, -1)
    return [pieces[:, :, which].reshape(rows, -1) for which in range(3)]


def plane_pairs(bit):
    return [(d, d ^ bit) for d in range(16)]


def ring_pairs(shift):
    return [(d, (d + 4 * shift) % 16) for d in range(16)]


def places():
    me = lax.axis_index("dp")
    return me // 4, me // 2 % 2, me % 2


def pick(values, index, axis):
    return lax.dynamic_index_in_dim(values, index, axis, keepdims=False)


def gather_tree(shard, cuts):
    z, y, x = places()
    column = jnp.zeros((4,) + shard.shape, shard.dtype)
    for shift in range(4):
        piece = shard if shift == 0 else lax.ppermute(shard, "dp", ring_pairs(shift))
        column = lax.dynamic_update_index_in_dim(column, piece, (z + 4 - shift) % 4, 0)
    out, start = [], 0
    for turn, size in enumerate(cuts):
        mine = column[:, :, start : start + size]
        start += size
        near, far = ((1, 2), (2, 1))[turn % 2]
        pieces = {0: mine, near: lax.ppermute(mine, "dp", plane_pairs(near))}
        pieces[far] = lax.ppermute(mine, "dp", plane_pairs(far))
        pieces[3] = lax.ppermute(pieces[near], "dp", plane_pairs(far))
        whole = jnp.zeros((4, 2, 2) + mine.shape[1:], shard.dtype)
        for bits, piece in pieces.items():
            spot = (0, y ^ (bits // 2), x ^ (bits % 2), 0, 0)
            whole = lax.dynamic_update_slice(whole, piece[:, None, None], spot)
        out.append(whole.reshape(-1, size))
    return out


def halve(values, index, axis, bit):
    other = lax.ppermute(pick(values, 1 - index, axis), "dp", plane_pairs(bit))
    return pick(values, index, axis) + other


def scatter_tree(values, cuts):
    z, y, x = places()
    values = values.reshape(4, 2, 2, -1, values.shape[1])
    out, start = [], 0
    for turn, size in enumerate(cuts):
        mine = values[..., start : start + size]
        start += size
        if turn % 2 == 0:
            mine = halve(halve(mine, x, 2, 1), y, 1, 2)
        else:
            mine = halve(halve(mine, y, 1, 2), x, 1, 1)
        total = pick(mine, z, 0).astype(F32)
        for shift in range(1, 4):
            total = total + lax.ppermute(pick(mine, (z + shift) % 4, 0), "dp", ring_pairs(shift)).astype(F32)
        out.append(total)
    return jnp.concatenate(out, axis=1)


def gain_tree(grads):
    z, y, x = places()
    grads = grads.T.reshape(2, 4, 2, 2, -1)
    grads = grads + swap(grads)
    grads = halve(halve(grads, x, 3, 1), y, 2, 2)
    total = pick(grads, z, 1)
    for shift in range(1, 4):
        total = total + lax.ppermute(pick(grads, (z + shift) % 4, 1), "dp", ring_pairs(shift))
    return total.T


def two_cuts(size):
    half = (size // 128 + 1) // 2 * 128
    return (half, size - half)


def per_device(dp, count, hidden_in, value_first, segment_ids, out_cotangent, attn_gain, w_query, w_key, w_value, w_output, mlp_gain, w_gate, w_up, w_down):
    rows, depth = hidden_in.shape
    width = w_query.shape[1]
    pairs = width // 128
    length = segment_ids.shape[1]
    slab = w_query.shape[0]
    blocks = w_gate.shape[1] * count // 256
    hidden_columns = 3 * w_gate.shape[1]
    tree = dp == 16 and count == 2

    gains = jnp.pad(jnp.stack([attn_gain, mlp_gain], axis=1), ((0, 0), (0, 126)))
    projections = jnp.stack([w.reshape(slab, pairs, 128) for w in (w_query, w_key, w_value)], axis=2).reshape(slab, -1)
    second_pack = jnp.concatenate([pack_hidden(w_gate, w_up, w_down.T, blocks), w_output.T], axis=1)
    if tree:
        sizes = (pairs - pairs // 2, pairs // 2)
        cut = sizes[0] * 384
        first_pack = jnp.concatenate([projections[:, :cut], projections[:, cut:], gains], axis=1)
        first_all = gather_tree(first_pack, (cut, 3 * width - cut + 128))
        all_gains = first_all[1][:, sizes[1] * 384 :]
    else:
        sizes = (pairs,)
        first_all = [lax.all_gather(jnp.concatenate([projections, gains], axis=1), "dp", axis=0, tiled=True)]
        all_gains = first_all[0][:, 3 * width :]
    second_all = lax.all_gather(second_pack, BOTH, axis=0, tiled=True).reshape(dp, count, slab, -1)
    gain_one = all_gains[:, 0].astype(F32)
    gain_two = all_gains[:, 1].astype(F32)

    doc_ids = segment_ids[0]
    counts = [jnp.sum(doc_ids < d) for d in (1, 2, 3)]
    starts = jnp.where(doc_ids == 1, counts[0], jnp.where(doc_ids == 2, counts[1], jnp.where(doc_ids == 3, counts[2], 0))).astype(jnp.int32)
    first = starts[::BLK] // BLK
    starts = starts[None, :]
    frequency = 10000.0 ** (-(jnp.arange(HEAD // 2, dtype=F32) * 2.0 / HEAD))
    angles = jnp.arange(length, dtype=F32)[:, None] * frequency[None, :]
    cos, sin = jnp.cos(angles), jnp.sin(angles)
    cosine = jnp.concatenate([cos] * 4, axis=1)
    sine = jnp.concatenate([-sin, sin] * 2, axis=1)
    cost, sint = cos.T, sin.T

    residual = hidden_in.astype(F32)
    flat_one, factor_one = norm_parts(residual)
    rows_one = gather_rows((flat_one * gain_one).astype(BF16), count)
    query, key, value, key_t, value_t = project(rows_one, first_all, sizes, value_first, cosine, sine)
    attended, log_totals = attention_forward(first, starts, query, key, value_t)
    attended_rows = heads_to_rows(attended, count)
    output_w = second_all[:, :, :, hidden_columns:].transpose(0, 2, 1, 3).reshape(depth, count * width)
    middle = residual + dot_nt(attended_rows, output_w)

    flat_two, factor_two = norm_parts(middle)
    normed_two = (flat_two * gain_two).astype(BF16)
    if count == 2:
        hidden_w = second_all
    else:
        hidden_w = second_all[:, :, :, :hidden_columns].reshape(dp, 2, count // 2, slab, blocks, 3, -1)
        hidden_w = hidden_w.transpose(1, 0, 3, 4, 5, 2, 6).reshape(1, 2, depth, blocks * 3 * PIECE)
    side = jnp.full((1,), lax.axis_index("tensor") if tree else 0, jnp.int32)
    cuts = (4, 4, 3) if tree else (blocks,)
    done, partial, keeps, sends, sums = 0, None, [], [], []
    for steps in cuts:
        *partial, keep, send = feedforward(side, normed_two, normed_two.T, out_cotangent, out_cotangent.T, hidden_w, done, steps, partial)
        done += steps
        if tree:
            sums.append(scatter_tree(keep + swap(send), two_cuts(steps * 384)))
        else:
            keeps.append(keep)
            sends.append(send)
    branch, normed_two_grad = partial
    layer_out = (middle + branch).astype(BF16)
    middle_norm_grad, gain_two_grad = norm_back(normed_two_grad, gain_two, flat_two, factor_two)
    middle_grad = out_cotangent.astype(F32) + middle_norm_grad
    branch_grad = middle_grad.astype(BF16)

    attended_grad = rows_to_heads(dot_nn(branch_grad, output_w).astype(BF16), count)
    output_grad = lax.dot_general(branch_grad, attended_rows, (((0,), (0,)), ((), ())), preferred_element_type=F32).astype(BF16)
    if tree:
        me = lax.axis_index("tensor")
        output_grad = part(output_grad, me, 2, 1) + swap(part(output_grad, 1 - me, 2, 1))
        grad_output = scatter_tree(output_grad, two_cuts(width)).T
        hidden_sum = jnp.concatenate(sums, axis=1)
    else:
        output_grad = output_grad.reshape(dp, slab, count, width).transpose(0, 2, 1, 3)
        hidden_grads = jnp.stack([keeps[0], sends[0]]).reshape(2, dp, slab, blocks, 3, count // 2, -1).transpose(1, 0, 5, 2, 3, 4, 6)
        second_grads = jnp.concatenate([hidden_grads.reshape(dp, count, slab, -1), output_grad], axis=3)
        second_sum = lax.psum_scatter(second_grads.reshape(dp * count * slab, -1), BOTH, scatter_dimension=0, tiled=True).astype(F32)
        hidden_sum, grad_output = second_sum[:, :hidden_columns], second_sum[:, hidden_columns:].T
    pre, value_grads, projection_grads = [], [], []
    for pair in range(pairs):
        pair_pre, value_grad = attention_backward(
            pair, first, starts, query, key, key_t, value, attended_grad, attended, log_totals, cosine, sine, cost, sint
        )
        pair_grad = lax.dot_general(rows_one, pair_pre, (((0,), (0,)), ((), ())), preferred_element_type=F32).astype(BF16)
        projection_grads.append(scatter_tree(pair_grad, (256, 128)) if tree else pair_grad)
        pre.append(pair_pre)
        value_grads.append(value_grad)
    grad_value_first = jnp.concatenate(value_grads, axis=1)
    projection_grads = jnp.concatenate(projection_grads, axis=1)
    weights = [w[:, : size * 384] for w, size in zip(first_all, sizes)]
    normed_one_grad = scatter_product(jnp.concatenate(pre, axis=1), weights, count)
    input_norm_grad, gain_one_grad = norm_back(normed_one_grad, gain_one, flat_one, factor_one)
    grad_input = middle_grad + input_norm_grad
    gain_grads = jnp.stack([gain_one_grad, gain_two_grad], axis=1)
    if tree:
        gain_sum = gain_tree(gain_grads)
        first_sum = projection_grads
    else:
        gain_grads = jnp.pad(lax.psum(gain_grads, "tensor").astype(BF16), ((0, 0), (0, 126)))
        first_sum = lax.psum_scatter(jnp.concatenate([projection_grads, gain_grads], axis=1), "dp", scatter_dimension=0, tiled=True).astype(F32)
        gain_sum = first_sum[:, 3 * width : 3 * width + 2]
        first_sum = first_sum[:, : 3 * width]
    grad_gate, grad_up, grad_down = unpack_hidden(hidden_sum, blocks)
    grad_query, grad_key, grad_value = unpack_hidden(first_sum, pairs)
    return (
        layer_out,
        grad_input,
        grad_value_first,
        gain_sum[:, 0],
        grad_query,
        grad_key,
        grad_value,
        grad_output,
        gain_sum[:, 1],
        grad_gate,
        grad_up,
        grad_down.T,
    )


def solution(mesh):
    tokens, split = P(BOTH, None), P("dp", "tensor")
    across = P("tensor", "dp")
    return jax.shard_map(
        functools.partial(per_device, mesh.shape["dp"], mesh.shape["tensor"]),
        mesh=mesh,
        in_specs=(tokens, split, P("dp", None), tokens, P("dp"), split, split, split, across, P("dp"), split, split, across),
        out_specs=(tokens, tokens, split, P("dp"), split, split, split, across, P("dp"), split, split, across),
        check_vma=False,
    )
```

```python
import functools

import jax
import jax.numpy as jnp
from jax import lax
from jax.experimental import pallas as pl
from jax.experimental.pallas import tpu as pltpu
from jax.sharding import PartitionSpec as P

HEAD = 64
PIECE = 128
NEG = -1e30
BLK = 256
F32 = jnp.float32
BF16 = jnp.bfloat16


def dot_nt(a, b, precision=None):
    return lax.dot_general(a, b, (((1,), (1,)), ((), ())), precision=precision, preferred_element_type=F32)


def dot_nn(a, b):
    return jnp.dot(a, b, preferred_element_type=F32)


def bias_tile(starts_ref, first_key, first_query):
    keys = lax.broadcasted_iota(jnp.int32, (BLK, BLK), 0) + first_key
    queries = lax.broadcasted_iota(jnp.int32, (BLK, BLK), 1) + first_query
    allowed = (keys >= starts_ref[...]) & (keys <= queries)
    return jnp.where(allowed, 0.0, NEG)


def forward_kernel(heads, first_ref, starts_ref, q_ref, k_ref, vt_ref, out_ref, lse_ref, masked_q, bias_ref, top_ref, total_ref, acc_ref):
    step = pl.program_id(0)
    lane = lax.broadcasted_iota(jnp.int32, (BLK, 128), 1)
    for head in range(heads):
        pair = pl.ds((head // 2) * 128, 128)
        block = q_ref[:, pair]
        keep = (lane < 64) if head % 2 == 0 else (lane >= 64)
        masked_q[head] = jnp.where(keep, block, jnp.zeros_like(block))
    top_ref[...] = jnp.full_like(top_ref, NEG)
    total_ref[...] = jnp.zeros_like(total_ref)
    acc_ref[...] = jnp.zeros_like(acc_ref)

    def chunk(c, carry):
        base = pl.multiple_of(c * BLK, BLK)
        bias_ref[...] = bias_tile(starts_ref, base, step * BLK)
        for head in range(heads):
            keys = k_ref[pl.ds(base, BLK), pl.ds((head // 2) * 128, 128)]
            scores = dot_nt(keys, masked_q[head]) + bias_ref[...]
            old = top_ref[head : head + 1, :]
            new = jnp.maximum(old, jnp.max(scores, axis=0, keepdims=True))
            probs = jnp.exp(scores - new)
            shrink = jnp.exp(old - new)
            top_ref[head : head + 1, :] = new
            total_ref[head : head + 1, :] = total_ref[head : head + 1, :] * shrink + jnp.sum(probs, axis=0, keepdims=True)
            rows = slice(head * 64, head * 64 + 64)
            part = dot_nn(vt_ref[rows, pl.ds(base, BLK)], probs.astype(BF16))
            acc_ref[rows, :] = acc_ref[rows, :] * shrink + part
        return carry

    lax.fori_loop(first_ref[step], step + 1, chunk, 0)
    for head in range(heads):
        rows = slice(head * 64, head * 64 + 64)
        acc_ref[rows, :] = acc_ref[rows, :] / total_ref[head : head + 1, :]
    out_ref[...] = acc_ref[...].T.astype(BF16)
    lse_ref[...] = (top_ref[...] + jnp.log(total_ref[...])).reshape(lse_ref.shape)


def attention_forward(first, starts, q, k, vt):
    length, width = q.shape
    heads = width // HEAD
    return pl.pallas_call(
        functools.partial(forward_kernel, heads),
        grid_spec=pltpu.PrefetchScalarGridSpec(
            num_scalar_prefetch=1,
            grid=(length // BLK,),
            in_specs=[
                pl.BlockSpec((1, BLK), lambda i, f: (0, i)),
                pl.BlockSpec((BLK, width), lambda i, f: (i, 0)),
                pl.BlockSpec((length, width), lambda i, f: (0, 0)),
                pl.BlockSpec((width, length), lambda i, f: (0, 0)),
            ],
            out_specs=[
                pl.BlockSpec((BLK, width), lambda i, f: (i, 0)),
                pl.BlockSpec((heads // 2, 2, BLK), lambda i, f: (0, 0, i)),
            ],
            scratch_shapes=[
                pltpu.VMEM((heads, BLK, 128), BF16),
                pltpu.VMEM((BLK, BLK), F32),
                pltpu.VMEM((heads, BLK), F32),
                pltpu.VMEM((heads, BLK), F32),
                pltpu.VMEM((width, BLK), F32),
            ],
        ),
        out_shape=[
            jax.ShapeDtypeStruct((length, width), BF16),
            jax.ShapeDtypeStruct((heads // 2, 2, length), F32),
        ],
        compiler_params=pltpu.CompilerParams(dimension_semantics=("arbitrary",)),
        name="attention_forward",
    )(first, starts, q, k, vt)


def unrotate_lanes(block, cosine, sine, lane):
    other = jnp.where(lane % 64 < 32, pltpu.roll(block, 96, 1), pltpu.roll(block, 32, 1))
    return block * cosine - other * sine


def backward_kernel(first_ref, starts_ref, q_ref, k_ref, kt_ref, v_ref, do_ref, o_ref, lse_ref, cosine_ref, sine_ref, cost_ref, sint_ref,
                    pre_ref, gv_ref, masked_q, masked_do, bias_ref, delta_ref, dqt_ref, dk_acc, dv_acc):
    step = pl.program_id(0)
    lane = lax.broadcasted_iota(jnp.int32, (BLK, 128), 1)

    @pl.when(step == 0)
    def _():
        dk_acc[...] = jnp.zeros_like(dk_acc)
        dv_acc[...] = jnp.zeros_like(dv_acc)

    for head in range(2):
        keep = (lane < 64) if head == 0 else (lane >= 64)
        masked_q[head] = jnp.where(keep, q_ref[...], jnp.zeros_like(q_ref))
        masked_do[head] = jnp.where(keep, do_ref[...], jnp.zeros_like(do_ref))
    product = do_ref[...].astype(F32) * o_ref[...].astype(F32)
    chooser = (lax.broadcasted_iota(jnp.int32, (8, 128), 1) // HEAD == lax.broadcasted_iota(jnp.int32, (8, 128), 0)).astype(F32)
    delta_ref[...] = dot_nt(chooser, product, lax.Precision.HIGHEST)
    dqt_ref[...] = jnp.zeros_like(dqt_ref)
    both_q = masked_q[...].reshape(2 * BLK, 128)
    both_do = masked_do[...].reshape(2 * BLK, 128)

    def chunk(c, carry):
        here = pl.ds(pl.multiple_of(c * BLK, BLK), BLK)
        bias_ref[...] = bias_tile(starts_ref, c * BLK, step * BLK)
        keys = k_ref[here, :]
        vals = v_ref[here, :]
        probs_low, grads_low = [], []
        for head in range(2):
            scores = dot_nt(keys, masked_q[head]) + bias_ref[...]
            probs = jnp.exp(scores - lse_ref[0, head : head + 1, :])
            prob_grad = dot_nt(vals, masked_do[head])
            score_grad = (probs * (prob_grad - delta_ref[head : head + 1, :])).astype(BF16)
            probs_low.append(probs.astype(BF16))
            grads_low.append(score_grad)
            rows = slice(head * 64, head * 64 + 64)
            dqt_ref[rows, :] += dot_nn(kt_ref[rows, here], score_grad)
        dv_acc[here, :] += dot_nn(jnp.concatenate(probs_low, axis=1), both_do)
        dk_acc[here, :] += dot_nn(jnp.concatenate(grads_low, axis=1), both_q)
        return carry

    lax.fori_loop(first_ref[step], step + 1, chunk, 0)
    cost, sint = cost_ref[...] * (HEAD**-0.5), sint_ref[...] * (HEAD**-0.5)
    for head in range(2):
        low = dqt_ref[head * 64 : head * 64 + 32, :]
        high = dqt_ref[head * 64 + 32 : head * 64 + 64, :]
        dqt_ref[head * 64 : head * 64 + 32, :] = low * cost + high * sint
        dqt_ref[head * 64 + 32 : head * 64 + 64, :] = high * cost - low * sint
    pre_ref[pl.ds(pl.multiple_of(step * BLK, BLK), BLK), :128] = dqt_ref[...].T.astype(BF16)

    @pl.when(step == pl.num_programs(0) - 1)
    def _():
        def finish(c, carry):
            here = pl.ds(pl.multiple_of(c * BLK, BLK), BLK)
            pre_ref[here, 128:256] = unrotate_lanes(dk_acc[here, :], cosine_ref[here, :], sine_ref[here, :], lane).astype(BF16)
            half = 0.5 * dv_acc[here, :]
            gv_ref[here, :] = half
            pre_ref[here, 256:] = half.astype(BF16)
            return carry
        lax.fori_loop(0, dk_acc.shape[0] // BLK, finish, 0)


def attention_backward(pair, first, starts, q, k, kt, v, do, o, lse, cosine, sine, cost, sint):
    length = q.shape[0]
    rows = pl.BlockSpec((BLK, 128), lambda i, f: (i, pair))
    whole = pl.BlockSpec((length, 128), lambda i, f: (0, pair))
    table = pl.BlockSpec((length, 128), lambda i, f: (0, 0))
    tile = length * BLK * 2 * 3
    return pl.pallas_call(
        backward_kernel,
        grid_spec=pltpu.PrefetchScalarGridSpec(
            num_scalar_prefetch=1,
            grid=(length // BLK,),
            in_specs=[
                pl.BlockSpec((1, BLK), lambda i, f: (0, i)),
                rows, whole,
                pl.BlockSpec((128, length), lambda i, f: (pair, 0)),
                whole, rows, rows,
                pl.BlockSpec((1, 2, BLK), lambda i, f: (pair, 0, i)),
                table, table,
                pl.BlockSpec((32, BLK), lambda i, f: (0, i)),
                pl.BlockSpec((32, BLK), lambda i, f: (0, i)),
            ],
            out_specs=[pl.BlockSpec((length, 384), lambda i, f: (0, 0)), table],
            scratch_shapes=[
                pltpu.VMEM((2, BLK, 128), BF16),
                pltpu.VMEM((2, BLK, 128), BF16),
                pltpu.VMEM((BLK, BLK), F32),
                pltpu.VMEM((8, BLK), F32),
                pltpu.VMEM((128, BLK), F32),
                pltpu.VMEM((length, 128), F32),
                pltpu.VMEM((length, 128), F32),
            ],
        ),
        out_shape=[jax.ShapeDtypeStruct((length, 384), BF16), jax.ShapeDtypeStruct((length, 128), F32)],
        compiler_params=pltpu.CompilerParams(dimension_semantics=("arbitrary",)),
        cost_estimate=pl.CostEstimate(flops=tile * 128 * 32, bytes_accessed=8 << 20, transcendentals=tile),
        name="attention_backward",
    )(first, starts, q, k, kt, v, do, o, lse, cosine, sine, cost, sint)

def feedforward_kernel(width, chained, side_ref, n_ref, nt_ref, y_ref, yt_ref, w_ref, *refs):
    if chained:
        out_in, e_in, *refs = refs
    out_ref, e_ref, keep_ref, send_ref, h_ref, dg_ref, du_ref = refs
    step = pl.program_id(0)
    rows = n_ref.shape[0]
    tile = 256 if rows % 256 == 0 else rows

    @pl.when(step == 0)
    def _():
        out_ref[...] = out_in[...] if chained else jnp.zeros_like(out_ref)
        e_ref[...] = e_in[...] if chained else jnp.zeros_like(e_ref)

    def weight(which):
        cols = slice(which * PIECE, which * PIECE + PIECE)
        return jnp.concatenate([w_ref[:, side, :, cols].reshape(width, PIECE) for side in range(2)], axis=1)

    gate_w, up_w, down_w = weight(0), weight(1), weight(2)

    def row_block(i, carry):
        here = pl.ds(pl.multiple_of(i * tile, tile), tile)
        gate = dot_nn(n_ref[here, :], gate_w)
        up = dot_nn(n_ref[here, :], up_w)
        dhid = dot_nn(y_ref[here, :], down_w)
        sig = 1.0 / (1.0 + jnp.exp(-gate))
        silu = gate * sig
        hidden = (silu * up).astype(BF16)
        dgate = (dhid * up * (sig * (1.0 + gate * (1.0 - sig)))).astype(BF16)
        dup = (dhid * silu).astype(BF16)
        h_ref[here, :] = hidden
        dg_ref[here, :] = dgate
        du_ref[here, :] = dup
        out_ref[here, :] += dot_nt(hidden, down_w)
        e_ref[here, :] += dot_nt(dgate, gate_w) + dot_nt(dup, up_w)
        return carry

    lax.fori_loop(0, rows // tile, row_block, 0)
    swapped = side_ref[0] != 0
    for which, (left, right) in enumerate(((nt_ref, dg_ref), (nt_ref, du_ref), (yt_ref, h_ref))):
        cols = slice(which * PIECE, which * PIECE + PIECE)
        grad = dot_nn(left[...], right[...])
        low, high = grad[:, :PIECE], grad[:, PIECE:]
        keep_ref[:, cols] = jnp.where(swapped, high, low).astype(BF16)
        send_ref[:, cols] = jnp.where(swapped, low, high).astype(BF16)


def feedforward(side, n, nt, y, yt, w, start, steps, partial=None):
    rows, width = n.shape
    outer, _, inner, _ = w.shape
    chained = partial is not None
    full = lambda shape: pl.BlockSpec(shape, lambda j, s: (0, 0), pipeline_mode=pl.Buffered(1))
    grads = pl.BlockSpec((width, 3 * PIECE), lambda j, s: (0, j))
    total = pl.BlockSpec((rows, width), lambda j, s: (0, 0))
    grads_shape = jax.ShapeDtypeStruct((width, steps * 3 * PIECE), BF16)
    flops = 18 * rows * width * steps * 2 * PIECE
    return pl.pallas_call(
        functools.partial(feedforward_kernel, width, chained),
        grid_spec=pltpu.PrefetchScalarGridSpec(
            num_scalar_prefetch=1,
            grid=(steps,),
            in_specs=[
                full((rows, width)), full((width, rows)), full((rows, width)), full((width, rows)),
                pl.BlockSpec((outer, 2, inner, 3 * PIECE), lambda j, s: (0, 0, 0, j + start)),
            ] + ([full((rows, width))] * 2 if chained else []),
            out_specs=[total, total, grads, grads],
            scratch_shapes=[pltpu.VMEM((rows, 2 * PIECE), BF16)] * 3,
        ),
        out_shape=[jax.ShapeDtypeStruct((rows, width), F32)] * 2 + [grads_shape] * 2,
        compiler_params=pltpu.CompilerParams(dimension_semantics=("arbitrary",), vmem_limit_bytes=60 << 20),
        cost_estimate=pl.CostEstimate(flops=flops, bytes_accessed=40 << 20, transcendentals=rows * steps * 256),
        name="feedforward",
    )(side, n, nt, y, yt, w, *(partial or ()))


def project_kernel(pairs, sizes, x_ref, *refs):
    weights, refs = refs[: len(sizes)], refs[len(sizes) :]
    first_ref, cosine_ref, sine_ref, q_ref, k_ref, v_ref, kt_ref, vt_ref = refs
    lane = lax.broadcasted_iota(jnp.int32, (x_ref.shape[0], 128), 1)
    first = lane % 64 < 32
    cosine, sine = cosine_ref[...], sine_ref[...]

    def turn(u):
        return u * cosine + jnp.where(first, pltpu.roll(u, 96, 1), pltpu.roll(u, 32, 1)) * sine

    pair = 0
    for ref, size in zip(weights, sizes):
        lin = dot_nn(x_ref[...], ref[:, : size * 384])
        for p in range(size):
            cols = slice(pair * 128, pair * 128 + 128)
            q_ref[:, cols] = (turn(lin[:, p * 384 : p * 384 + 128]) * 0.125).astype(BF16)
            k_ref[:, cols] = turn(lin[:, p * 384 + 128 : p * 384 + 256]).astype(BF16)
            v_ref[:, cols] = (0.5 * lin[:, p * 384 + 256 : p * 384 + 384] + 0.5 * first_ref[:, cols].astype(F32)).astype(BF16)
            pair += 1
    kt_ref[...] = k_ref[...].T
    vt_ref[...] = v_ref[...].T


def project(x, weights, sizes, first, cosine, sine):
    length, depth = x.shape
    width = first.shape[1]
    block = min(256, length)
    rows = lambda n: pl.BlockSpec((block, n), lambda i: (i, 0))
    out = jax.ShapeDtypeStruct((length, width), BF16)
    turned = jax.ShapeDtypeStruct((width, length), BF16)
    across = pl.BlockSpec((width, block), lambda i: (0, i))
    return pl.pallas_call(
        functools.partial(project_kernel, width // 128, sizes),
        grid=(length // block,),
        in_specs=[rows(depth)] + [pl.BlockSpec(w.shape, lambda i: (0, 0), pipeline_mode=pl.Buffered(1)) for w in weights] + [rows(width), rows(128), rows(128)],
        out_specs=[rows(width)] * 3 + [across] * 2,
        out_shape=[out] * 3 + [turned] * 2,
        compiler_params=pltpu.CompilerParams(dimension_semantics=("arbitrary",), vmem_limit_bytes=60 << 20),
        cost_estimate=pl.CostEstimate(flops=6 * length * depth * width, bytes_accessed=20 << 20, transcendentals=0),
        name="project",
    )(x, *weights, first, cosine, sine)


EPS = 1e-06
BOTH = ("dp", "tensor")


def norm_parts(values):
    factor = lax.rsqrt(jnp.mean(values * values, axis=-1, keepdims=True) + EPS)
    return values * factor, factor


def norm_back(incoming, gain, normalized, factor):
    scaled = incoming * gain
    gain_grad = jnp.sum(incoming * normalized, axis=0)
    input_grad = factor * (scaled - normalized * jnp.mean(scaled * normalized, axis=-1, keepdims=True))
    return input_grad, gain_grad


def swap(values):
    return lax.ppermute(values, "tensor", [(0, 1), (1, 0)])


def part(values, index, count, axis):
    size = values.shape[axis] // count
    return lax.dynamic_slice_in_dim(values, index * size, size, axis)


def in_order(mine, theirs, axis):
    first = lax.axis_index("tensor") == 0
    return jnp.concatenate([jnp.where(first, mine, theirs), jnp.where(first, theirs, mine)], axis=axis)


def gather_rows(rows, count):
    if count != 2:
        return lax.all_gather(rows, "tensor", axis=0, tiled=True)
    return in_order(rows, swap(rows), 0)


def heads_to_rows(values, count):
    if count != 2:
        return lax.all_to_all(values, "tensor", split_axis=0, concat_axis=1, tiled=True)
    me = lax.axis_index("tensor")
    theirs = swap(part(values, 1 - me, 2, 0))
    return in_order(part(values, me, 2, 0), theirs, 1)


def rows_to_heads(values, count):
    if count != 2:
        return lax.all_to_all(values, "tensor", split_axis=1, concat_axis=0, tiled=True)
    me = lax.axis_index("tensor")
    theirs = swap(part(values, 1 - me, 2, 1))
    return in_order(part(values, me, 2, 1), theirs, 0)


def scatter_product(left, weights, count):
    def product(rows):
        total, start = 0.0, 0
        for weight in weights:
            size = weight.shape[1]
            total = total + dot_nt(rows[:, start : start + size], weight)
            start += size
        return total

    if count != 2:
        return lax.psum_scatter(product(left), "tensor", scatter_dimension=0, tiled=True)
    me = lax.axis_index("tensor")
    theirs = swap(product(part(left, 1 - me, 2, 0)).astype(BF16))
    return product(part(left, me, 2, 0)) + theirs.astype(F32)


def tensor_sum(values, count):
    if count != 2:
        return lax.psum(values, "tensor")
    return values + swap(values)


def pack_hidden(gate, up, down, blocks):
    rows = gate.shape[0]
    stacked = jnp.stack([w.reshape(rows, blocks, -1) for w in (gate, up, down)], axis=2)
    return stacked.reshape(rows, -1)


def unpack_hidden(packed, blocks):
    rows = packed.shape[0]
    pieces = packed.reshape(rows, blocks, 3, -1)
    return [pieces[:, :, which].reshape(rows, -1) for which in range(3)]


def plane_pairs(bit):
    return [(d, d ^ bit) for d in range(16)]


def ring_pairs(shift):
    return [(d, (d + 4 * shift) % 16) for d in range(16)]


def places():
    me = lax.axis_index("dp")
    return me // 4, me // 2 % 2, me % 2


def pick(values, index, axis):
    return lax.dynamic_index_in_dim(values, index, axis, keepdims=False)


def gather_column(shard):
    z, y, x = places()
    column = jnp.zeros((4,) + shard.shape, shard.dtype)
    for shift in range(4):
        piece = shard if shift == 0 else lax.ppermute(shard, "dp", ring_pairs(shift))
        column = lax.dynamic_update_index_in_dim(column, piece, (z + 4 - shift) % 4, 0)
    return column


def gather_plane(column, cuts):
    z, y, x = places()
    out, start = [], 0
    for turn, size in enumerate(cuts):
        mine = column[:, :, start : start + size]
        start += size
        near, far = ((1, 2), (2, 1))[turn % 2]
        pieces = {0: mine, near: lax.ppermute(mine, "dp", plane_pairs(near))}
        pieces[far] = lax.ppermute(mine, "dp", plane_pairs(far))
        pieces[3] = lax.ppermute(pieces[near], "dp", plane_pairs(far))
        whole = jnp.zeros((4, 2, 2) + mine.shape[1:], column.dtype)
        for bits, piece in pieces.items():
            spot = (0, y ^ (bits // 2), x ^ (bits % 2), 0, 0)
            whole = lax.dynamic_update_slice(whole, piece[:, None, None], spot)
        out.append(whole.reshape(-1, size))
    return out


def halve(values, index, axis, bit):
    other = lax.ppermute(pick(values, 1 - index, axis), "dp", plane_pairs(bit))
    return pick(values, index, axis) + other


def plane_sends(values):
    z, y, x = places()
    values = values.reshape(4, 2, 2, -1, values.shape[1])
    half = (values.shape[4] // 128 + 1) // 2 * 128
    one, two = values[..., :half], values[..., half:]
    return pick(one, 1 - x, 2), pick(two, 1 - y, 1), pick(one, x, 2), pick(two, y, 1)


def plane_turn(state):
    z, y, x = places()
    send_one, send_two, keep_one, keep_two = state
    one = keep_one + lax.ppermute(send_one, "dp", plane_pairs(1))
    two = keep_two + lax.ppermute(send_two, "dp", plane_pairs(2))
    return pick(one, 1 - y, 1), pick(two, 1 - x, 1), pick(one, y, 1), pick(two, x, 1)


def column_sum(state):
    z, y, x = places()
    send_one, send_two, keep_one, keep_two = state
    one = keep_one + lax.ppermute(send_one, "dp", plane_pairs(2))
    two = keep_two + lax.ppermute(send_two, "dp", plane_pairs(1))
    both = jnp.concatenate([one, two], axis=2)
    total = pick(both, z, 0).astype(F32)
    for shift in range(1, 4):
        total = total + lax.ppermute(pick(both, (z + shift) % 4, 0), "dp", ring_pairs(shift)).astype(F32)
    return total


def gain_tree(grads):
    z, y, x = places()
    grads = grads.T.reshape(2, 4, 2, 2, -1)
    grads = grads + swap(grads)
    grads = halve(halve(grads, x, 3, 1), y, 2, 2)
    total = pick(grads, z, 1)
    for shift in range(1, 4):
        total = total + lax.ppermute(pick(grads, (z + shift) % 4, 1), "dp", ring_pairs(shift))
    return total.T


def per_device(dp, count, hidden_in, value_first, segment_ids, out_cotangent, attn_gain, w_query, w_key, w_value, w_output, mlp_gain, w_gate, w_up, w_down):
    rows, depth = hidden_in.shape
    width = w_query.shape[1]
    pairs = width // 128
    length = segment_ids.shape[1]
    slab = w_query.shape[0]
    blocks = w_gate.shape[1] * count // 256
    hidden_columns = 3 * w_gate.shape[1]
    tree = dp == 16 and count == 2

    gains = jnp.pad(jnp.stack([attn_gain, mlp_gain], axis=1), ((0, 0), (0, 126)))
    projections = jnp.stack([w.reshape(slab, pairs, 128) for w in (w_query, w_key, w_value)], axis=2).reshape(slab, -1)
    hidden_pack = pack_hidden(w_gate, w_up, w_down.T, blocks)
    if tree:
        early = 6 * 384
        packs = [jnp.concatenate([hidden_pack[:, :early], w_output.T], axis=1), hidden_pack[:, early:]]
        sizes = (pairs - pairs // 2, pairs // 2)
        cut = sizes[0] * 384
        first_pack = jnp.concatenate([projections[:, :cut], projections[:, cut:], gains], axis=1)
        first_column = gather_column(first_pack)
    else:
        early = hidden_columns
        packs = [jnp.concatenate([hidden_pack, w_output.T], axis=1)]
        sizes = (pairs,)
        first_all = [lax.all_gather(jnp.concatenate([projections, gains], axis=1), "dp", axis=0, tiled=True)]
    second_all = [lax.all_gather(pack, BOTH, axis=0, tiled=True).reshape(dp, count, slab, -1) for pack in packs]
    doc_ids = segment_ids[0]
    counts = [jnp.sum(doc_ids < d) for d in (1, 2, 3)]
    starts = jnp.where(doc_ids == 1, counts[0], jnp.where(doc_ids == 2, counts[1], jnp.where(doc_ids == 3, counts[2], 0))).astype(jnp.int32)
    first = starts[::BLK] // BLK
    starts = starts[None, :]
    frequency = 10000.0 ** (-(jnp.arange(HEAD // 2, dtype=F32) * 2.0 / HEAD))
    angles = jnp.arange(length, dtype=F32)[:, None] * frequency[None, :]
    cos, sin = jnp.cos(angles), jnp.sin(angles)
    cosine = jnp.concatenate([cos] * 4, axis=1)
    sine = jnp.concatenate([-sin, sin] * 2, axis=1)
    cost, sint = cos.T, sin.T

    residual = hidden_in.astype(F32)
    flat_one, factor_one = norm_parts(residual)
    if tree:
        first_column, first, starts, cosine, sine, cost, sint, flat_one, factor_one = lax.optimization_barrier(
            (first_column, first, starts, cosine, sine, cost, sint, flat_one, factor_one)
        )
        first_all = gather_plane(first_column, (cut, 3 * width - cut + 128))
        all_gains = first_all[1][:, sizes[1] * 384 :]
    else:
        all_gains = first_all[0][:, 3 * width :]
    gain_one = all_gains[:, 0].astype(F32)
    gain_two = all_gains[:, 1].astype(F32)
    rows_one = gather_rows((flat_one * gain_one).astype(BF16), count)
    query, key, value, key_t, value_t = project(rows_one, first_all, sizes, value_first, cosine, sine)
    attended, log_totals = attention_forward(first, starts, query, key, value_t)
    attended_rows = heads_to_rows(attended, count)
    output_w = second_all[0][:, :, :, early:].transpose(0, 2, 1, 3).reshape(depth, count * width)
    middle = residual + dot_nt(attended_rows, output_w)

    flat_two, factor_two = norm_parts(middle)
    normed_two = (flat_two * gain_two).astype(BF16)
    if count == 2:
        hidden_w = second_all
    else:
        whole = second_all[0][:, :, :, :hidden_columns].reshape(dp, 2, count // 2, slab, blocks, 3, -1)
        hidden_w = [whole.transpose(1, 0, 3, 4, 5, 2, 6).reshape(1, 2, depth, blocks * 3 * PIECE)]
    side = jnp.full((1,), lax.axis_index("tensor") if tree else 0, jnp.int32)
    partial, keeps, sends = None, [], []
    for w, steps in zip(hidden_w, (6, blocks - 6) if tree else (blocks,)):
        *partial, keep, send = feedforward(side, normed_two, normed_two.T, out_cotangent, out_cotangent.T, w, 0, steps, partial)
        keeps.append(keep)
        sends.append(swap(send) if tree else send)
    branch, normed_two_grad = partial
    layer_out = (middle + branch).astype(BF16)
    middle_norm_grad, gain_two_grad = norm_back(normed_two_grad, gain_two, flat_two, factor_two)
    middle_grad = out_cotangent.astype(F32) + middle_norm_grad
    branch_grad = middle_grad.astype(BF16)

    attended_grad = rows_to_heads(dot_nn(branch_grad, output_w).astype(BF16), count)
    output_grad = lax.dot_general(branch_grad, attended_rows, (((0,), (0,)), ((), ())), preferred_element_type=F32).astype(BF16)
    if tree:
        me = lax.axis_index("tensor")
        output_grad = part(output_grad, me, 2, 1) + swap(part(output_grad, 1 - me, 2, 1))
        spare = -hidden_columns % 768
        hidden_grads = jnp.concatenate([a + b for a, b in zip(keeps, sends)] + [jnp.zeros((depth, spare), BF16)], axis=1)
        hidden_grads, attended_grad = lax.optimization_barrier((hidden_grads, attended_grad))
        hidden_sum = lax.psum_scatter(hidden_grads, "dp", scatter_dimension=0, tiled=True).astype(F32)
    else:
        output_grad = output_grad.reshape(dp, slab, count, width).transpose(0, 2, 1, 3)
        hidden_grads = jnp.stack([keeps[0], sends[0]]).reshape(2, dp, slab, blocks, 3, count // 2, -1).transpose(1, 0, 5, 2, 3, 4, 6)
        second_grads = jnp.concatenate([hidden_grads.reshape(dp, count, slab, -1), output_grad], axis=3)
        second_sum = lax.psum_scatter(second_grads.reshape(dp * count * slab, -1), BOTH, scatter_dimension=0, tiled=True).astype(F32)
        hidden_sum, grad_output = second_sum[:, :hidden_columns], second_sum[:, hidden_columns:].T
    pre, value_grads, pair_grads = [], [], []
    for pair in range(pairs):
        pair_pre, value_grad = attention_backward(
            pair, first, starts, query, key, key_t, value, attended_grad, attended, log_totals, cosine, sine, cost, sint
        )
        pre.append(pair_pre)
        value_grads.append(value_grad)
        pair_grads.append(lax.dot_general(rows_one, pair_pre, (((0,), (0,)), ((), ())), preferred_element_type=F32).astype(BF16))
        if tree and pair == 1:
            tree_one, attended_grad = lax.optimization_barrier((plane_sends(jnp.concatenate([output_grad] + pair_grads, axis=1)), attended_grad))
        if tree and pair == 2:
            tree_one, attended_grad = lax.optimization_barrier((plane_turn(tree_one), attended_grad))
    grad_value_first = jnp.concatenate(value_grads, axis=1)
    if tree:
        tree_two = plane_turn(plane_sends(jnp.concatenate(pair_grads[2:], axis=1)))
        tree_one = column_sum(tree_one)
        grad_output = tree_one[:, :width].T
        first_sum = jnp.concatenate([tree_one[:, width:], column_sum(tree_two)], axis=1)
    else:
        projection_grads = jnp.concatenate(pair_grads, axis=1)
    weights = [w[:, : size * 384] for w, size in zip(first_all, sizes)]
    normed_one_grad = scatter_product(jnp.concatenate(pre, axis=1), weights, count)
    input_norm_grad, gain_one_grad = norm_back(normed_one_grad, gain_one, flat_one, factor_one)
    grad_input = middle_grad + input_norm_grad
    gain_grads = jnp.stack([gain_one_grad, gain_two_grad], axis=1)
    if tree:
        gain_sum = gain_tree(gain_grads)
    else:
        gain_grads = jnp.pad(lax.psum(gain_grads, "tensor").astype(BF16), ((0, 0), (0, 126)))
        first_sum = lax.psum_scatter(jnp.concatenate([projection_grads, gain_grads], axis=1), "dp", scatter_dimension=0, tiled=True).astype(F32)
        gain_sum = first_sum[:, 3 * width : 3 * width + 2]
        first_sum = first_sum[:, : 3 * width]
    grad_gate, grad_up, grad_down = unpack_hidden(hidden_sum[:, :hidden_columns], blocks)
    grad_query, grad_key, grad_value = unpack_hidden(first_sum, pairs)
    return (
        layer_out,
        grad_input,
        grad_value_first,
        gain_sum[:, 0],
        grad_query,
        grad_key,
        grad_value,
        grad_output,
        gain_sum[:, 1],
        grad_gate,
        grad_up,
        grad_down.T,
    )


def solution(mesh):
    tokens, split = P(BOTH, None), P("dp", "tensor")
    across = P("tensor", "dp")
    return jax.shard_map(
        functools.partial(per_device, mesh.shape["dp"], mesh.shape["tensor"]),
        mesh=mesh,
        in_specs=(tokens, split, P("dp", None), tokens, P("dp"), split, split, split, across, P("dp"), split, split, across),
        out_specs=(tokens, tokens, split, P("dp"), split, split, split, across, P("dp"), split, split, across),
        check_vma=False,
    )
```

```python
import functools

import jax
import jax.numpy as jnp
from jax import lax
from jax.experimental import pallas as pl
from jax.experimental.pallas import tpu as pltpu
from jax.experimental.layout import Layout, with_layout_constraint
from jax.sharding import PartitionSpec as P

HEAD = 64
PIECE = 128
NEG = -1e30
BLK = 256
F32 = jnp.float32
BF16 = jnp.bfloat16


def dot_nt(a, b, precision=None):
    return lax.dot_general(a, b, (((1,), (1,)), ((), ())), precision=precision, preferred_element_type=F32)


def dot_nn(a, b):
    return jnp.dot(a, b, preferred_element_type=F32)


def bias_tile(starts_ref, first_key, first_query):
    keys = lax.broadcasted_iota(jnp.int32, (BLK, BLK), 0) + first_key
    queries = lax.broadcasted_iota(jnp.int32, (BLK, BLK), 1) + first_query
    allowed = (keys >= starts_ref[...]) & (keys <= queries)
    return jnp.where(allowed, 0.0, NEG)


def forward_kernel(heads, first_ref, starts_ref, q_ref, k_ref, vt_ref, out_ref, lse_ref, masked_q, bias_ref, top_ref, total_ref, acc_ref):
    step = pl.program_id(0)
    lane = lax.broadcasted_iota(jnp.int32, (BLK, 128), 1)
    for head in range(heads):
        pair = pl.ds((head // 2) * 128, 128)
        block = q_ref[:, pair]
        keep = (lane < 64) if head % 2 == 0 else (lane >= 64)
        masked_q[head] = jnp.where(keep, block, jnp.zeros_like(block))
    top_ref[...] = jnp.full_like(top_ref, NEG)
    total_ref[...] = jnp.zeros_like(total_ref)
    acc_ref[...] = jnp.zeros_like(acc_ref)

    def chunk(c, carry):
        base = pl.multiple_of(c * BLK, BLK)
        bias_ref[...] = bias_tile(starts_ref, base, step * BLK)
        for head in range(heads):
            keys = k_ref[pl.ds(base, BLK), pl.ds((head // 2) * 128, 128)]
            scores = dot_nt(keys, masked_q[head]) + bias_ref[...]
            old = top_ref[head : head + 1, :]
            new = jnp.maximum(old, jnp.max(scores, axis=0, keepdims=True))
            probs = jnp.exp(scores - new)
            shrink = jnp.exp(old - new)
            top_ref[head : head + 1, :] = new
            total_ref[head : head + 1, :] = total_ref[head : head + 1, :] * shrink + jnp.sum(probs, axis=0, keepdims=True)
            rows = slice(head * 64, head * 64 + 64)
            part = dot_nn(vt_ref[rows, pl.ds(base, BLK)], probs.astype(BF16))
            acc_ref[rows, :] = acc_ref[rows, :] * shrink + part
        return carry

    lax.fori_loop(first_ref[step], step + 1, chunk, 0)
    for head in range(heads):
        rows = slice(head * 64, head * 64 + 64)
        acc_ref[rows, :] = acc_ref[rows, :] / total_ref[head : head + 1, :]
    out_ref[...] = acc_ref[...].T.astype(BF16)
    lse_ref[...] = (top_ref[...] + jnp.log(total_ref[...])).reshape(lse_ref.shape)


def attention_forward(first, starts, q, k, vt):
    length, width = q.shape
    heads = width // HEAD
    return pl.pallas_call(
        functools.partial(forward_kernel, heads),
        grid_spec=pltpu.PrefetchScalarGridSpec(
            num_scalar_prefetch=1,
            grid=(length // BLK,),
            in_specs=[
                pl.BlockSpec((1, BLK), lambda i, f: (0, i)),
                pl.BlockSpec((BLK, width), lambda i, f: (i, 0)),
                pl.BlockSpec((length, width), lambda i, f: (0, 0)),
                pl.BlockSpec((width, length), lambda i, f: (0, 0)),
            ],
            out_specs=[
                pl.BlockSpec((BLK, width), lambda i, f: (i, 0)),
                pl.BlockSpec((heads // 2, 2, BLK), lambda i, f: (0, 0, i)),
            ],
            scratch_shapes=[
                pltpu.VMEM((heads, BLK, 128), BF16),
                pltpu.VMEM((BLK, BLK), F32),
                pltpu.VMEM((heads, BLK), F32),
                pltpu.VMEM((heads, BLK), F32),
                pltpu.VMEM((width, BLK), F32),
            ],
        ),
        out_shape=[
            jax.ShapeDtypeStruct((length, width), BF16),
            jax.ShapeDtypeStruct((heads // 2, 2, length), F32),
        ],
        compiler_params=pltpu.CompilerParams(dimension_semantics=("arbitrary",)),
        name="attention_forward",
    )(first, starts, q, k, vt)


def unrotate_lanes(block, cosine, sine, lane):
    other = jnp.where(lane % 64 < 32, pltpu.roll(block, 96, 1), pltpu.roll(block, 32, 1))
    return block * cosine - other * sine


def backward_kernel(first_ref, starts_ref, q_ref, k_ref, kt_ref, v_ref, do_ref, o_ref, lse_ref, cosine_ref, sine_ref, cost_ref, sint_ref, *refs):
    pre_ref, gv_ref, masked_q, masked_do, bias_ref, delta_ref, dqt_ref, dk_acc, dv_acc = refs[-9:]
    step = pl.program_id(0)
    lane = lax.broadcasted_iota(jnp.int32, (BLK, 128), 1)

    @pl.when(step == 0)
    def _():
        dk_acc[...] = jnp.zeros_like(dk_acc)
        dv_acc[...] = jnp.zeros_like(dv_acc)

    for head in range(2):
        keep = (lane < 64) if head == 0 else (lane >= 64)
        masked_q[head] = jnp.where(keep, q_ref[...], jnp.zeros_like(q_ref))
        masked_do[head] = jnp.where(keep, do_ref[...], jnp.zeros_like(do_ref))
    product = do_ref[...].astype(F32) * o_ref[...].astype(F32)
    chooser = (lax.broadcasted_iota(jnp.int32, (8, 128), 1) // HEAD == lax.broadcasted_iota(jnp.int32, (8, 128), 0)).astype(F32)
    delta_ref[...] = dot_nt(chooser, product, lax.Precision.HIGHEST)
    dqt_ref[...] = jnp.zeros_like(dqt_ref)
    both_q = masked_q[...].reshape(2 * BLK, 128)
    both_do = masked_do[...].reshape(2 * BLK, 128)

    def chunk(c, carry):
        here = pl.ds(pl.multiple_of(c * BLK, BLK), BLK)
        bias_ref[...] = bias_tile(starts_ref, c * BLK, step * BLK)
        keys = k_ref[here, :]
        vals = v_ref[here, :]
        probs_low, grads_low = [], []
        for head in range(2):
            scores = dot_nt(keys, masked_q[head]) + bias_ref[...]
            probs = jnp.exp(scores - lse_ref[0, head : head + 1, :])
            prob_grad = dot_nt(vals, masked_do[head])
            score_grad = (probs * (prob_grad - delta_ref[head : head + 1, :])).astype(BF16)
            probs_low.append(probs.astype(BF16))
            grads_low.append(score_grad)
            rows = slice(head * 64, head * 64 + 64)
            dqt_ref[rows, :] += dot_nn(kt_ref[rows, here], score_grad)
        dv_acc[here, :] += dot_nn(jnp.concatenate(probs_low, axis=1), both_do)
        dk_acc[here, :] += dot_nn(jnp.concatenate(grads_low, axis=1), both_q)
        return carry

    lax.fori_loop(first_ref[step], step + 1, chunk, 0)
    cost, sint = cost_ref[...] * (HEAD**-0.5), sint_ref[...] * (HEAD**-0.5)
    for head in range(2):
        low = dqt_ref[head * 64 : head * 64 + 32, :]
        high = dqt_ref[head * 64 + 32 : head * 64 + 64, :]
        dqt_ref[head * 64 : head * 64 + 32, :] = low * cost + high * sint
        dqt_ref[head * 64 + 32 : head * 64 + 64, :] = high * cost - low * sint
    pre_ref[pl.ds(pl.multiple_of(step * BLK, BLK), BLK), :128] = dqt_ref[...].T.astype(BF16)

    @pl.when(step == pl.num_programs(0) - 1)
    def _():
        def finish(c, carry):
            here = pl.ds(pl.multiple_of(c * BLK, BLK), BLK)
            pre_ref[here, 128:256] = unrotate_lanes(dk_acc[here, :], cosine_ref[here, :], sine_ref[here, :], lane).astype(BF16)
            half = 0.5 * dv_acc[here, :]
            gv_ref[here, :] = half
            pre_ref[here, 256:] = half.astype(BF16)
            return carry
        lax.fori_loop(0, dk_acc.shape[0] // BLK, finish, 0)


def attention_backward(pair, first, starts, q, k, kt, v, do, o, lse, cosine, sine, cost, sint, values=None):
    length = q.shape[0]
    earlier = [] if values is None else [values]
    rows = pl.BlockSpec((BLK, 128), lambda i, f: (i, pair))
    whole = pl.BlockSpec((length, 128), lambda i, f: (0, pair))
    table = pl.BlockSpec((length, 128), lambda i, f: (0, 0))
    tile = length * BLK * 2 * 3
    return pl.pallas_call(
        backward_kernel,
        grid_spec=pltpu.PrefetchScalarGridSpec(
            num_scalar_prefetch=1,
            grid=(length // BLK,),
            in_specs=[
                pl.BlockSpec((1, BLK), lambda i, f: (0, i)),
                rows, whole,
                pl.BlockSpec((128, length), lambda i, f: (pair, 0)),
                whole, rows, rows,
                pl.BlockSpec((1, 2, BLK), lambda i, f: (pair, 0, i)),
                table, table,
                pl.BlockSpec((32, BLK), lambda i, f: (0, i)),
                pl.BlockSpec((32, BLK), lambda i, f: (0, i)),
            ] + [pl.BlockSpec(memory_space=pl.ANY)] * len(earlier),
            out_specs=[pl.BlockSpec((length, 384), lambda i, f: (0, 0)), whole],
            scratch_shapes=[
                pltpu.VMEM((2, BLK, 128), BF16),
                pltpu.VMEM((2, BLK, 128), BF16),
                pltpu.VMEM((BLK, BLK), F32),
                pltpu.VMEM((8, BLK), F32),
                pltpu.VMEM((128, BLK), F32),
                pltpu.VMEM((length, 128), F32),
                pltpu.VMEM((length, 128), F32),
            ],
        ),
        out_shape=[jax.ShapeDtypeStruct((length, 384), BF16), jax.ShapeDtypeStruct(q.shape, F32)],
        input_output_aliases={13: 1} if earlier else {},
        compiler_params=pltpu.CompilerParams(dimension_semantics=("arbitrary",)),
        cost_estimate=pl.CostEstimate(flops=tile * 128 * 32, bytes_accessed=8 << 20, transcendentals=tile),
        name="attention_backward",
    )(first, starts, q, k, kt, v, do, o, lse, cosine, sine, cost, sint, *earlier)

def feedforward_kernel(width, chained, side_ref, n_ref, nt_ref, y_ref, yt_ref, w_ref, *refs):
    if chained:
        out_in, e_in, *refs = refs
    out_ref, e_ref, keep_ref, send_ref, h_ref, dg_ref, du_ref = refs
    step = pl.program_id(0)
    rows = n_ref.shape[0]
    tile = 256 if rows % 256 == 0 else rows

    @pl.when(step == 0)
    def _():
        out_ref[...] = out_in[...] if chained else jnp.zeros_like(out_ref)
        e_ref[...] = e_in[...] if chained else jnp.zeros_like(e_ref)

    def weight(which):
        cols = slice(which * PIECE, which * PIECE + PIECE)
        return jnp.concatenate([w_ref[:, side, :, cols].reshape(width, PIECE) for side in range(2)], axis=1)

    gate_w, up_w, down_w = weight(0), weight(1), weight(2)

    def row_block(i, carry):
        here = pl.ds(pl.multiple_of(i * tile, tile), tile)
        gate = dot_nn(n_ref[here, :], gate_w)
        up = dot_nn(n_ref[here, :], up_w)
        dhid = dot_nn(y_ref[here, :], down_w)
        sig = 1.0 / (1.0 + jnp.exp(-gate))
        silu = gate * sig
        hidden = (silu * up).astype(BF16)
        dgate = (dhid * up * (sig * (1.0 + gate * (1.0 - sig)))).astype(BF16)
        dup = (dhid * silu).astype(BF16)
        h_ref[here, :] = hidden
        dg_ref[here, :] = dgate
        du_ref[here, :] = dup
        out_ref[here, :] += dot_nt(hidden, down_w)
        e_ref[here, :] += dot_nt(dgate, gate_w) + dot_nt(dup, up_w)
        return carry

    lax.fori_loop(0, rows // tile, row_block, 0)
    swapped = side_ref[0] != 0
    for which, (left, right) in enumerate(((nt_ref, dg_ref), (nt_ref, du_ref), (yt_ref, h_ref))):
        cols = slice(which * PIECE, which * PIECE + PIECE)
        grad = dot_nn(left[...], right[...])
        low, high = grad[:, :PIECE], grad[:, PIECE:]
        keep_ref[:, cols] = jnp.where(swapped, high, low).astype(BF16)
        send_ref[:, cols] = jnp.where(swapped, low, high).astype(BF16)


def feedforward(side, n, nt, y, yt, w, start, steps, partial=None):
    rows, width = n.shape
    outer, _, inner, _ = w.shape
    chained = partial is not None
    full = lambda shape: pl.BlockSpec(shape, lambda j, s: (0, 0), pipeline_mode=pl.Buffered(1))
    grads = pl.BlockSpec((width, 3 * PIECE), lambda j, s: (0, j))
    total = pl.BlockSpec((rows, width), lambda j, s: (0, 0))
    grads_shape = jax.ShapeDtypeStruct((width, steps * 3 * PIECE), BF16)
    flops = 18 * rows * width * steps * 2 * PIECE
    return pl.pallas_call(
        functools.partial(feedforward_kernel, width, chained),
        grid_spec=pltpu.PrefetchScalarGridSpec(
            num_scalar_prefetch=1,
            grid=(steps,),
            in_specs=[
                full((rows, width)), full((width, rows)), full((rows, width)), full((width, rows)),
                pl.BlockSpec((outer, 2, inner, 3 * PIECE), lambda j, s: (0, 0, 0, j + start)),
            ] + ([full((rows, width))] * 2 if chained else []),
            out_specs=[total, total, grads, grads],
            scratch_shapes=[pltpu.VMEM((rows, 2 * PIECE), BF16)] * 3,
        ),
        out_shape=[jax.ShapeDtypeStruct((rows, width), F32)] * 2 + [grads_shape] * 2,
        compiler_params=pltpu.CompilerParams(dimension_semantics=("arbitrary",), vmem_limit_bytes=60 << 20),
        cost_estimate=pl.CostEstimate(flops=flops, bytes_accessed=40 << 20, transcendentals=rows * steps * 256),
        name="feedforward",
    )(side, n, nt, y, yt, w, *(partial or ()))


def project_kernel(pairs, sizes, x_ref, *refs):
    weights, refs = refs[: len(sizes)], refs[len(sizes) :]
    first_ref, cosine_ref, sine_ref, q_ref, k_ref, v_ref, kt_ref, vt_ref = refs
    lane = lax.broadcasted_iota(jnp.int32, (x_ref.shape[0], 128), 1)
    first = lane % 64 < 32
    cosine, sine = cosine_ref[...], sine_ref[...]

    def turn(u):
        return u * cosine + jnp.where(first, pltpu.roll(u, 96, 1), pltpu.roll(u, 32, 1)) * sine

    pair = 0
    for ref, size in zip(weights, sizes):
        lin = dot_nn(x_ref[...], ref[:, : size * 384])
        for p in range(size):
            cols = slice(pair * 128, pair * 128 + 128)
            q_ref[:, cols] = (turn(lin[:, p * 384 : p * 384 + 128]) * 0.125).astype(BF16)
            k_ref[:, cols] = turn(lin[:, p * 384 + 128 : p * 384 + 256]).astype(BF16)
            v_ref[:, cols] = (0.5 * lin[:, p * 384 + 256 : p * 384 + 384] + 0.5 * first_ref[:, cols].astype(F32)).astype(BF16)
            pair += 1
    kt_ref[...] = k_ref[...].T
    vt_ref[...] = v_ref[...].T


def project(x, weights, sizes, first, cosine, sine):
    length, depth = x.shape
    width = first.shape[1]
    block = min(256, length)
    rows = lambda n: pl.BlockSpec((block, n), lambda i: (i, 0))
    out = jax.ShapeDtypeStruct((length, width), BF16)
    turned = jax.ShapeDtypeStruct((width, length), BF16)
    across = pl.BlockSpec((width, block), lambda i: (0, i))
    return pl.pallas_call(
        functools.partial(project_kernel, width // 128, sizes),
        grid=(length // block,),
        in_specs=[rows(depth)] + [pl.BlockSpec(w.shape, lambda i: (0, 0), pipeline_mode=pl.Buffered(1)) for w in weights] + [rows(width), rows(128), rows(128)],
        out_specs=[rows(width)] * 3 + [across] * 2,
        out_shape=[out] * 3 + [turned] * 2,
        compiler_params=pltpu.CompilerParams(dimension_semantics=("arbitrary",), vmem_limit_bytes=60 << 20),
        cost_estimate=pl.CostEstimate(flops=6 * length * depth * width, bytes_accessed=20 << 20, transcendentals=0),
        name="project",
    )(x, *weights, first, cosine, sine)


EPS = 1e-06
BOTH = ("dp", "tensor")


def row_major(values):
    return with_layout_constraint(values, Layout(tuple(range(values.ndim))))


def norm_parts(values):
    factor = lax.rsqrt(jnp.mean(values * values, axis=-1, keepdims=True) + EPS)
    return values * factor, factor


def norm_back(incoming, gain, normalized, factor):
    scaled = incoming * gain
    gain_grad = jnp.sum(incoming * normalized, axis=0)
    input_grad = factor * (scaled - normalized * jnp.mean(scaled * normalized, axis=-1, keepdims=True))
    return input_grad, gain_grad


def swap(values):
    return lax.ppermute(values, "tensor", [(0, 1), (1, 0)])


def part(values, index, count, axis):
    size = values.shape[axis] // count
    return lax.dynamic_slice_in_dim(values, index * size, size, axis)


def in_order(mine, theirs, axis):
    first = lax.axis_index("tensor") == 0
    return jnp.concatenate([jnp.where(first, mine, theirs), jnp.where(first, theirs, mine)], axis=axis)


def gather_rows(rows, count):
    if count != 2:
        return lax.all_gather(rows, "tensor", axis=0, tiled=True)
    return in_order(rows, swap(rows), 0)


def heads_to_rows(values, count):
    if count != 2:
        return lax.all_to_all(values, "tensor", split_axis=0, concat_axis=1, tiled=True)
    me = lax.axis_index("tensor")
    theirs = swap(part(values, 1 - me, 2, 0))
    return in_order(part(values, me, 2, 0), theirs, 1)


def rows_to_heads(values, count):
    if count != 2:
        return lax.all_to_all(values, "tensor", split_axis=1, concat_axis=0, tiled=True)
    me = lax.axis_index("tensor")
    theirs = swap(part(values, 1 - me, 2, 1))
    return in_order(part(values, me, 2, 1), theirs, 0)


def scatter_product(left, weights, count):
    def product(rows):
        total, start = 0.0, 0
        for weight in weights:
            size = weight.shape[1]
            total = total + dot_nt(rows[:, start : start + size], weight)
            start += size
        return total

    if count != 2:
        return lax.psum_scatter(product(left), "tensor", scatter_dimension=0, tiled=True)
    me = lax.axis_index("tensor")
    theirs = swap(product(part(left, 1 - me, 2, 0)).astype(BF16))
    return product(part(left, me, 2, 0)) + theirs.astype(F32)


def tensor_sum(values, count):
    if count != 2:
        return lax.psum(values, "tensor")
    return values + swap(values)


def pack_hidden(gate, up, down, blocks):
    rows = gate.shape[0]
    stacked = jnp.stack([w.reshape(rows, blocks, -1) for w in (gate, up, down)], axis=2)
    return stacked.reshape(rows, -1)


def unpack_hidden(packed, blocks):
    rows = packed.shape[0]
    pieces = packed.reshape(rows, blocks, 3, -1)
    return [pieces[:, :, which].reshape(rows, -1) for which in range(3)]


def plane_pairs(bit):
    return [(d, d ^ bit) for d in range(16)]


def ring_pairs(shift):
    return [(d, (d + 4 * shift) % 16) for d in range(16)]


def places():
    me = lax.axis_index("dp")
    return me // 4, me // 2 % 2, me % 2


def pick(values, index, axis):
    return lax.dynamic_index_in_dim(values, index, axis, keepdims=False)


def gather_column(shard):
    z, y, x = places()
    column = jnp.zeros((4,) + shard.shape, shard.dtype)
    for shift in range(4):
        piece = shard if shift == 0 else lax.ppermute(shard, "dp", ring_pairs(shift))
        column = lax.dynamic_update_index_in_dim(column, piece, (z + 4 - shift) % 4, 0)
    return column


def gather_plane(column, cuts):
    z, y, x = places()
    mine, start = [], 0
    for size in cuts:
        mine.append(column[:, :, start : start + size])
        start += size
    orders = ((1, 2), (2, 1))
    mine = lax.optimization_barrier(mine)
    beside = [lax.ppermute(own, "dp", plane_pairs(near)) for own, (near, far) in zip(mine, orders)]
    mine, beside = lax.optimization_barrier((mine, beside))
    across = [
        (lax.ppermute(own, "dp", plane_pairs(far)), lax.ppermute(next_own, "dp", plane_pairs(far)))
        for own, next_own, (near, far) in zip(mine, beside, orders)
    ]
    across = lax.optimization_barrier(across)
    out = []
    for own, next_own, (far_own, far_next), (near, far), size in zip(mine, beside, across, orders, cuts):
        pieces = {0: own, near: next_own, far: far_own, 3: far_next}
        whole = jnp.zeros((4, 2, 2) + own.shape[1:], column.dtype)
        for bits, piece in pieces.items():
            spot = (0, y ^ (bits // 2), x ^ (bits % 2), 0, 0)
            whole = lax.dynamic_update_slice(whole, piece[:, None, None], spot)
        out.append(whole.reshape(-1, size))
    return out


def halve(values, index, axis, bit):
    other = lax.ppermute(pick(values, 1 - index, axis), "dp", plane_pairs(bit))
    return pick(values, index, axis) + other


def plane_sends(values):
    z, y, x = places()
    values = values.reshape(4, 2, 2, -1, values.shape[1])
    half = (values.shape[4] // 128 + 1) // 2 * 128
    one, two = values[..., :half], values[..., half:]
    return pick(one, 1 - x, 2), pick(two, 1 - y, 1), pick(one, x, 2), pick(two, y, 1)


def plane_turn(state):
    z, y, x = places()
    send_one, send_two, keep_one, keep_two = state
    one = keep_one + lax.ppermute(send_one, "dp", plane_pairs(1))
    two = keep_two + lax.ppermute(send_two, "dp", plane_pairs(2))
    return pick(one, 1 - y, 1), pick(two, 1 - x, 1), pick(one, y, 1), pick(two, x, 1)


def column_parts(state):
    send_one, send_two, keep_one, keep_two = state
    one = keep_one + lax.ppermute(send_one, "dp", plane_pairs(2))
    two = keep_two + lax.ppermute(send_two, "dp", plane_pairs(1))
    return jnp.concatenate([one, two], axis=2)


def column_sum(parts):
    z, y, x = places()
    total = pick(parts, z, 0).astype(F32)
    for shift in range(1, 4):
        total = total + lax.ppermute(pick(parts, (z + shift) % 4, 0), "dp", ring_pairs(shift)).astype(F32)
    return total


def gain_tree(grads):
    z, y, x = places()
    grads = grads.T.reshape(2, 4, 2, 2, -1)
    grads = grads + swap(grads)
    grads = halve(halve(grads, x, 3, 1), y, 2, 2)
    total = pick(grads, z, 1)
    for shift in range(1, 4):
        total = total + lax.ppermute(pick(grads, (z + shift) % 4, 1), "dp", ring_pairs(shift))
    return total.T


def per_device(dp, count, hidden_in, value_first, segment_ids, out_cotangent, attn_gain, w_query, w_key, w_value, w_output, mlp_gain, w_gate, w_up, w_down):
    rows, depth = hidden_in.shape
    width = w_query.shape[1]
    pairs = width // 128
    length = segment_ids.shape[1]
    slab = w_query.shape[0]
    blocks = w_gate.shape[1] * count // 256
    hidden_columns = 3 * w_gate.shape[1]
    tree = dp == 16 and count == 2

    gains = jnp.pad(jnp.stack([attn_gain, mlp_gain], axis=1), ((0, 0), (0, 126)))
    projections = jnp.stack([w.reshape(slab, pairs, 128) for w in (w_query, w_key, w_value)], axis=2).reshape(slab, -1)
    hidden_pack = pack_hidden(w_gate, w_up, w_down.T, blocks)
    if tree:
        early = 6 * 384
        packs = [jnp.concatenate([hidden_pack[:, :early], w_output.T], axis=1), hidden_pack[:, early:]]
        sizes = (pairs - pairs // 2, pairs // 2)
        cut = sizes[0] * 384
        first_pack = jnp.concatenate([projections[:, :cut], projections[:, cut:], gains], axis=1)
        first_column = gather_column(first_pack)
    else:
        early = hidden_columns
        packs = [jnp.concatenate([hidden_pack, w_output.T], axis=1)]
        sizes = (pairs,)
        first_all = [lax.all_gather(jnp.concatenate([projections, gains], axis=1), "dp", axis=0, tiled=True)]
    second_all = [lax.all_gather(pack, BOTH, axis=0, tiled=True).reshape(dp, count, slab, -1) for pack in packs]
    doc_ids = segment_ids[0]
    counts = [jnp.sum(doc_ids < d) for d in (1, 2, 3)]
    starts = jnp.where(doc_ids == 1, counts[0], jnp.where(doc_ids == 2, counts[1], jnp.where(doc_ids == 3, counts[2], 0))).astype(jnp.int32)
    first = starts[::BLK] // BLK
    starts = starts[None, :]
    frequency = 10000.0 ** (-(jnp.arange(HEAD // 2, dtype=F32) * 2.0 / HEAD))
    angles = jnp.arange(length, dtype=F32)[:, None] * frequency[None, :]
    cos, sin = jnp.cos(angles), jnp.sin(angles)
    cosine = jnp.concatenate([cos] * 4, axis=1)
    sine = jnp.concatenate([-sin, sin] * 2, axis=1)
    cost, sint = cos.T, sin.T

    residual = hidden_in.astype(F32)
    flat_one, factor_one = norm_parts(residual)
    if tree:
        first_column, first, starts, cosine, sine, cost, sint, flat_one, factor_one = lax.optimization_barrier(
            (first_column, first, starts, cosine, sine, cost, sint, flat_one, factor_one)
        )
        first_all = gather_plane(first_column, (cut, 3 * width - cut + 128))
        all_gains = first_all[1][:, sizes[1] * 384 :]
    else:
        all_gains = first_all[0][:, 3 * width :]
    gain_one = all_gains[:, 0].astype(F32)
    gain_two = all_gains[:, 1].astype(F32)
    rows_one = row_major(gather_rows(row_major((flat_one * gain_one).astype(BF16)), count))
    query, key, value, key_t, value_t = project(rows_one, first_all, sizes, value_first, cosine, sine)
    attended, log_totals = attention_forward(first, starts, query, key, value_t)
    attended_rows = heads_to_rows(attended, count)
    output_w = second_all[0][:, :, :, early:].transpose(0, 2, 1, 3).reshape(depth, count * width)
    middle = row_major(residual + dot_nt(attended_rows, output_w))

    flat_two, factor_two = norm_parts(middle)
    normed_two = row_major((flat_two * gain_two).astype(BF16))
    if count == 2:
        hidden_w = second_all
    else:
        whole = second_all[0][:, :, :, :hidden_columns].reshape(dp, 2, count // 2, slab, blocks, 3, -1)
        hidden_w = [whole.transpose(1, 0, 3, 4, 5, 2, 6).reshape(1, 2, depth, blocks * 3 * PIECE)]
    side = jnp.full((1,), lax.axis_index("tensor") if tree else 0, jnp.int32)
    partial, keeps, sends = None, [], []
    for w, steps in zip(hidden_w, (6, blocks - 6) if tree else (blocks,)):
        *partial, keep, send = feedforward(side, normed_two, normed_two.T, out_cotangent, out_cotangent.T, w, 0, steps, partial)
        keeps.append(keep)
        sends.append(swap(send) if tree else send)
    branch, normed_two_grad = [row_major(p) for p in partial]
    layer_out = (middle + branch).astype(BF16)
    middle_norm_grad, gain_two_grad = norm_back(normed_two_grad, gain_two, flat_two, factor_two)
    middle_grad = row_major(out_cotangent.astype(F32) + middle_norm_grad)
    branch_grad = row_major(middle_grad.astype(BF16))
    if tree:
        hidden_grads, start = jnp.zeros((depth, hidden_columns + -hidden_columns % 768), BF16), 0
        for keep, theirs in zip(keeps, sends):
            hidden_grads = lax.dynamic_update_slice(hidden_grads, keep + theirs, (0, start))
            start += keep.shape[1]
        hidden_grads, branch_grad = lax.optimization_barrier((hidden_grads, branch_grad))
        hidden_sum = lax.psum_scatter(hidden_grads, "dp", scatter_dimension=0, tiled=True).astype(F32)

    attended_grad = rows_to_heads(dot_nn(branch_grad, output_w).astype(BF16), count)
    output_grad = lax.dot_general(branch_grad, attended_rows, (((0,), (0,)), ((), ())), preferred_element_type=F32).astype(BF16)
    if tree:
        me = lax.axis_index("tensor")
        output_grad = part(output_grad, me, 2, 1) + swap(part(output_grad, 1 - me, 2, 1))
    else:
        output_grad = output_grad.reshape(dp, slab, count, width).transpose(0, 2, 1, 3)
        hidden_grads = jnp.stack([keeps[0], sends[0]]).reshape(2, dp, slab, blocks, 3, count // 2, -1).transpose(1, 0, 5, 2, 3, 4, 6)
        second_grads = jnp.concatenate([hidden_grads.reshape(dp, count, slab, -1), output_grad], axis=3)
        second_sum = lax.psum_scatter(second_grads.reshape(dp * count * slab, -1), BOTH, scatter_dimension=0, tiled=True).astype(F32)
        hidden_sum, grad_output = second_sum[:, :hidden_columns], second_sum[:, hidden_columns:].T
    pre, grad_value_first, pair_grads = [], None, []
    for pair in range(pairs):
        pair_pre, grad_value_first = attention_backward(
            pair, first, starts, query, key, key_t, value, attended_grad, attended, log_totals, cosine, sine, cost, sint, grad_value_first
        )
        if tree and pair == 3:
            tree_one, pair_pre = lax.optimization_barrier((column_parts(tree_one), pair_pre))
        pre.append(pair_pre)
        pair_grads.append(lax.dot_general(rows_one, pair_pre, (((0,), (0,)), ((), ())), preferred_element_type=F32).astype(BF16))
        if tree and pair == 1:
            tree_one, attended_grad = lax.optimization_barrier((plane_sends(jnp.concatenate([output_grad] + pair_grads, axis=1)), attended_grad))
        if tree and pair == 2:
            tree_one, attended_grad = lax.optimization_barrier((plane_turn(tree_one), attended_grad))
    if tree:
        tree_two, pre = lax.optimization_barrier((plane_sends(jnp.concatenate(pair_grads[2:], axis=1)), pre))
    else:
        projection_grads = jnp.concatenate(pair_grads, axis=1)
    weights = [w[:, : size * 384] for w, size in zip(first_all, sizes)]
    normed_one_grad = row_major(scatter_product(jnp.concatenate(pre, axis=1), weights, count))
    if tree:
        tree_two, tree_one, normed_one_grad = lax.optimization_barrier((plane_turn(tree_two), tree_one, normed_one_grad))
        tree_one = column_sum(tree_one)
    input_norm_grad, gain_one_grad = norm_back(normed_one_grad, gain_one, flat_one, factor_one)
    grad_input = row_major(middle_grad + input_norm_grad)
    gain_grads = jnp.stack([gain_one_grad, gain_two_grad], axis=1)
    if tree:
        gain_sum = gain_tree(gain_grads)
        grad_output = tree_one[:, :width].T
        first_sum = jnp.concatenate([tree_one[:, width:], column_sum(column_parts(tree_two))], axis=1)
    else:
        gain_grads = jnp.pad(lax.psum(gain_grads, "tensor").astype(BF16), ((0, 0), (0, 126)))
        first_sum = lax.psum_scatter(jnp.concatenate([projection_grads, gain_grads], axis=1), "dp", scatter_dimension=0, tiled=True).astype(F32)
        gain_sum = first_sum[:, 3 * width : 3 * width + 2]
        first_sum = first_sum[:, : 3 * width]
    grad_gate, grad_up, grad_down = unpack_hidden(hidden_sum[:, :hidden_columns], blocks)
    grad_query, grad_key, grad_value = unpack_hidden(first_sum, pairs)
    return (
        layer_out,
        grad_input,
        grad_value_first,
        gain_sum[:, 0],
        grad_query,
        grad_key,
        grad_value,
        grad_output,
        gain_sum[:, 1],
        grad_gate,
        grad_up,
        grad_down.T,
    )


def solution(mesh):
    tokens, split = P(BOTH, None), P("dp", "tensor")
    across = P("tensor", "dp")
    return jax.shard_map(
        functools.partial(per_device, mesh.shape["dp"], mesh.shape["tensor"]),
        mesh=mesh,
        in_specs=(tokens, split, P("dp", None), tokens, P("dp"), split, split, split, across, P("dp"), split, split, across),
        out_specs=(tokens, tokens, split, P("dp"), split, split, split, across, P("dp"), split, split, across),
        check_vma=False,
    )
```

```python
import functools

import jax
import jax.numpy as jnp
from jax import lax
from jax.experimental import pallas as pl
from jax.experimental.pallas import tpu as pltpu
from jax.experimental.layout import Layout, with_layout_constraint
from jax.sharding import PartitionSpec as P

HEAD = 64
PIECE = 128
NEG = -1e30
BLK = 256
F32 = jnp.float32
BF16 = jnp.bfloat16


def dot_nt(a, b, precision=None):
    return lax.dot_general(a, b, (((1,), (1,)), ((), ())), precision=precision, preferred_element_type=F32)


def dot_nn(a, b):
    return jnp.dot(a, b, preferred_element_type=F32)


def bias_tile(starts_ref, first_key, first_query):
    place = lax.broadcasted_iota(jnp.int32, (BLK, BLK), 0)
    low = starts_ref[...] - first_key
    high = lax.broadcasted_iota(jnp.int32, (1, BLK), 1) + (first_query - first_key)
    return jnp.where((place >= low) & (place <= high), 0.0, NEG)


def forward_kernel(heads, first_ref, starts_ref, q_ref, k_ref, vt_ref, out_ref, lse_ref, masked_q, bias_ref, top_ref, total_ref, acc_ref):
    step = pl.program_id(0)
    lane = lax.broadcasted_iota(jnp.int32, (BLK, 128), 1)
    for head in range(heads):
        pair = pl.ds((head // 2) * 128, 128)
        block = q_ref[:, pair]
        keep = (lane < 64) if head % 2 == 0 else (lane >= 64)
        masked_q[head] = jnp.where(keep, block, jnp.zeros_like(block))
    top_ref[...] = jnp.full_like(top_ref, NEG)
    total_ref[...] = jnp.zeros_like(total_ref)
    acc_ref[...] = jnp.zeros_like(acc_ref)

    def chunk(c, carry):
        base = pl.multiple_of(c * BLK, BLK)
        bias_ref[...] = bias_tile(starts_ref, base, step * BLK)
        for head in range(heads):
            keys = k_ref[pl.ds(base, BLK), pl.ds((head // 2) * 128, 128)]
            scores = dot_nt(keys, masked_q[head]) + bias_ref[...]
            old = top_ref[head : head + 1, :]
            new = jnp.maximum(old, jnp.max(scores, axis=0, keepdims=True))
            probs = jnp.exp(scores - new)
            shrink = jnp.exp(old - new)
            top_ref[head : head + 1, :] = new
            total_ref[head : head + 1, :] = total_ref[head : head + 1, :] * shrink + jnp.sum(probs, axis=0, keepdims=True)
            rows = slice(head * 64, head * 64 + 64)
            part = dot_nn(vt_ref[rows, pl.ds(base, BLK)], probs.astype(BF16))
            acc_ref[rows, :] = acc_ref[rows, :] * shrink + part
        return carry

    lax.fori_loop(first_ref[step], step + 1, chunk, 0)
    for head in range(heads):
        rows = slice(head * 64, head * 64 + 64)
        acc_ref[rows, :] = acc_ref[rows, :] / total_ref[head : head + 1, :]
    out_ref[...] = acc_ref[...].T.astype(BF16)
    lse_ref[...] = (top_ref[...] + jnp.log(total_ref[...])).reshape(lse_ref.shape)


def attention_forward(first, starts, q, k, vt):
    length, width = q.shape
    heads = width // HEAD
    return pl.pallas_call(
        functools.partial(forward_kernel, heads),
        grid_spec=pltpu.PrefetchScalarGridSpec(
            num_scalar_prefetch=1,
            grid=(length // BLK,),
            in_specs=[
                pl.BlockSpec((1, BLK), lambda i, f: (0, i)),
                pl.BlockSpec((BLK, width), lambda i, f: (i, 0)),
                pl.BlockSpec((length, width), lambda i, f: (0, 0)),
                pl.BlockSpec((width, length), lambda i, f: (0, 0)),
            ],
            out_specs=[
                pl.BlockSpec((BLK, width), lambda i, f: (i, 0)),
                pl.BlockSpec((heads // 2, 2, BLK), lambda i, f: (0, 0, i)),
            ],
            scratch_shapes=[
                pltpu.VMEM((heads, BLK, 128), BF16),
                pltpu.VMEM((BLK, BLK), F32),
                pltpu.VMEM((heads, BLK), F32),
                pltpu.VMEM((heads, BLK), F32),
                pltpu.VMEM((width, BLK), F32),
            ],
        ),
        out_shape=[
            jax.ShapeDtypeStruct((length, width), BF16),
            jax.ShapeDtypeStruct((heads // 2, 2, length), F32),
        ],
        compiler_params=pltpu.CompilerParams(dimension_semantics=("arbitrary",)),
        name="attention_forward",
    )(first, starts, q, k, vt)


def unrotate_lanes(block, cosine, sine, lane):
    other = jnp.where(lane % 64 < 32, pltpu.roll(block, 96, 1), pltpu.roll(block, 32, 1))
    return block * cosine - other * sine


def backward_kernel(first_ref, starts_ref, q_ref, k_ref, kt_ref, v_ref, do_ref, o_ref, lse_ref, cosine_ref, sine_ref, cost_ref, sint_ref, *refs):
    pre_ref, gv_ref, masked_q, masked_do, bias_ref, delta_ref, dqt_ref, dk_acc, dv_acc = refs[-9:]
    step = pl.program_id(0)
    lane = lax.broadcasted_iota(jnp.int32, (BLK, 128), 1)

    @pl.when(step == 0)
    def _():
        dk_acc[...] = jnp.zeros_like(dk_acc)
        dv_acc[...] = jnp.zeros_like(dv_acc)

    for head in range(2):
        keep = (lane < 64) if head == 0 else (lane >= 64)
        masked_q[head] = jnp.where(keep, q_ref[...], jnp.zeros_like(q_ref))
        masked_do[head] = jnp.where(keep, do_ref[...], jnp.zeros_like(do_ref))
    product = do_ref[...].astype(F32) * o_ref[...].astype(F32)
    chooser = (lax.broadcasted_iota(jnp.int32, (8, 128), 1) // HEAD == lax.broadcasted_iota(jnp.int32, (8, 128), 0)).astype(F32)
    delta_ref[...] = dot_nt(chooser, product, lax.Precision.HIGHEST)
    dqt_ref[...] = jnp.zeros_like(dqt_ref)
    both_q = masked_q[...].reshape(2 * BLK, 128)
    both_do = masked_do[...].reshape(2 * BLK, 128)

    def chunk(c, carry):
        here = pl.ds(pl.multiple_of(c * BLK, BLK), BLK)
        bias_ref[...] = bias_tile(starts_ref, c * BLK, step * BLK)
        keys = k_ref[here, :]
        vals = v_ref[here, :]
        probs_low, grads_low = [], []
        for head in range(2):
            scores = dot_nt(keys, masked_q[head]) + bias_ref[...]
            probs = jnp.exp(scores - lse_ref[0, head : head + 1, :])
            prob_grad = dot_nt(vals, masked_do[head])
            score_grad = (probs * (prob_grad - delta_ref[head : head + 1, :])).astype(BF16)
            probs_low.append(probs.astype(BF16))
            grads_low.append(score_grad)
            rows = slice(head * 64, head * 64 + 64)
            dqt_ref[rows, :] += dot_nn(kt_ref[rows, here], score_grad)
        dv_acc[here, :] += dot_nn(jnp.concatenate(probs_low, axis=1), both_do)
        dk_acc[here, :] += dot_nn(jnp.concatenate(grads_low, axis=1), both_q)
        return carry

    lax.fori_loop(first_ref[step], step + 1, chunk, 0)
    cost, sint = cost_ref[...] * (HEAD**-0.5), sint_ref[...] * (HEAD**-0.5)
    for head in range(2):
        low = dqt_ref[head * 64 : head * 64 + 32, :]
        high = dqt_ref[head * 64 + 32 : head * 64 + 64, :]
        dqt_ref[head * 64 : head * 64 + 32, :] = low * cost + high * sint
        dqt_ref[head * 64 + 32 : head * 64 + 64, :] = high * cost - low * sint
    pre_ref[pl.ds(pl.multiple_of(step * BLK, BLK), BLK), :128] = dqt_ref[...].T.astype(BF16)

    @pl.when(step == pl.num_programs(0) - 1)
    def _():
        def finish(c, carry):
            here = pl.ds(pl.multiple_of(c * BLK, BLK), BLK)
            pre_ref[here, 128:256] = unrotate_lanes(dk_acc[here, :], cosine_ref[here, :], sine_ref[here, :], lane).astype(BF16)
            half = 0.5 * dv_acc[here, :]
            gv_ref[here, :] = half
            pre_ref[here, 256:] = half.astype(BF16)
            return carry
        lax.fori_loop(0, dk_acc.shape[0] // BLK, finish, 0)


def attention_backward(pair, first, starts, q, k, kt, v, do, o, lse, cosine, sine, cost, sint, values=None):
    length = q.shape[0]
    earlier = [] if values is None else [values]
    rows = pl.BlockSpec((BLK, 128), lambda i, f: (i, pair))
    whole = pl.BlockSpec((length, 128), lambda i, f: (0, pair))
    table = pl.BlockSpec((length, 128), lambda i, f: (0, 0))
    tile = length * BLK * 2 * 3
    return pl.pallas_call(
        backward_kernel,
        grid_spec=pltpu.PrefetchScalarGridSpec(
            num_scalar_prefetch=1,
            grid=(length // BLK,),
            in_specs=[
                pl.BlockSpec((1, BLK), lambda i, f: (0, i)),
                rows, whole,
                pl.BlockSpec((128, length), lambda i, f: (pair, 0)),
                whole, rows, rows,
                pl.BlockSpec((1, 2, BLK), lambda i, f: (pair, 0, i)),
                table, table,
                pl.BlockSpec((32, BLK), lambda i, f: (0, i)),
                pl.BlockSpec((32, BLK), lambda i, f: (0, i)),
            ] + [pl.BlockSpec(memory_space=pl.ANY)] * len(earlier),
            out_specs=[pl.BlockSpec((length, 384), lambda i, f: (0, 0)), whole],
            scratch_shapes=[
                pltpu.VMEM((2, BLK, 128), BF16),
                pltpu.VMEM((2, BLK, 128), BF16),
                pltpu.VMEM((BLK, BLK), F32),
                pltpu.VMEM((8, BLK), F32),
                pltpu.VMEM((128, BLK), F32),
                pltpu.VMEM((length, 128), F32),
                pltpu.VMEM((length, 128), F32),
            ],
        ),
        out_shape=[jax.ShapeDtypeStruct((length, 384), BF16), jax.ShapeDtypeStruct(q.shape, F32)],
        input_output_aliases={13: 1} if earlier else {},
        compiler_params=pltpu.CompilerParams(dimension_semantics=("arbitrary",)),
        cost_estimate=pl.CostEstimate(flops=tile * 128 * 32, bytes_accessed=8 << 20, transcendentals=tile),
        name="attention_backward",
    )(first, starts, q, k, kt, v, do, o, lse, cosine, sine, cost, sint, *earlier)

def feedforward_kernel(width, chained, side_ref, n_ref, nt_ref, y_ref, yt_ref, w_ref, *refs):
    if chained:
        out_in, e_in, *refs = refs
    out_ref, e_ref, keep_ref, send_ref, h_ref, dg_ref, du_ref = refs
    step = pl.program_id(0)
    rows = n_ref.shape[0]
    tile = 256 if rows % 256 == 0 else rows

    @pl.when(step == 0)
    def _():
        out_ref[...] = out_in[...] if chained else jnp.zeros_like(out_ref)
        e_ref[...] = e_in[...] if chained else jnp.zeros_like(e_ref)

    def weight(which):
        cols = slice(which * PIECE, which * PIECE + PIECE)
        return jnp.concatenate([w_ref[:, side, :, cols].reshape(width, PIECE) for side in range(2)], axis=1)

    gate_w, up_w, down_w = weight(0), weight(1), weight(2)

    def row_block(i, carry):
        here = pl.ds(pl.multiple_of(i * tile, tile), tile)
        gate = dot_nn(n_ref[here, :], gate_w)
        up = dot_nn(n_ref[here, :], up_w)
        dhid = dot_nn(y_ref[here, :], down_w)
        sig = 1.0 / (1.0 + jnp.exp(-gate))
        silu = gate * sig
        hidden = (silu * up).astype(BF16)
        dgate = (dhid * up * (sig * (1.0 + gate * (1.0 - sig)))).astype(BF16)
        dup = (dhid * silu).astype(BF16)
        h_ref[here, :] = hidden
        dg_ref[here, :] = dgate
        du_ref[here, :] = dup
        out_ref[here, :] += dot_nt(hidden, down_w)
        e_ref[here, :] += dot_nt(dgate, gate_w) + dot_nt(dup, up_w)
        return carry

    lax.fori_loop(0, rows // tile, row_block, 0)
    swapped = side_ref[0] != 0

    def grad_block(i, carry):
        here = pl.ds(pl.multiple_of(i * 256, 256), 256)
        for which, (left, right) in enumerate(((nt_ref, dg_ref), (nt_ref, du_ref), (yt_ref, h_ref))):
            cols = slice(which * PIECE, which * PIECE + PIECE)
            grad = dot_nn(left[here, :], right[...])
            low, high = grad[:, :PIECE], grad[:, PIECE:]
            keep_ref[here, cols] = jnp.where(swapped, high, low).astype(BF16)
            send_ref[here, cols] = jnp.where(swapped, low, high).astype(BF16)
        return carry

    lax.fori_loop(0, width // 256, grad_block, 0)


def feedforward(side, n, nt, y, yt, w, start, steps, partial=None):
    rows, width = n.shape
    outer, _, inner, _ = w.shape
    chained = partial is not None
    full = lambda shape: pl.BlockSpec(shape, lambda j, s: (0, 0), pipeline_mode=pl.Buffered(1))
    grads = pl.BlockSpec((width, 3 * PIECE), lambda j, s: (0, j))
    total = pl.BlockSpec((rows, width), lambda j, s: (0, 0))
    grads_shape = jax.ShapeDtypeStruct((width, steps * 3 * PIECE), BF16)
    flops = 18 * rows * width * steps * 2 * PIECE
    return pl.pallas_call(
        functools.partial(feedforward_kernel, width, chained),
        grid_spec=pltpu.PrefetchScalarGridSpec(
            num_scalar_prefetch=1,
            grid=(steps,),
            in_specs=[
                full((rows, width)), full((width, rows)), full((rows, width)), full((width, rows)),
                pl.BlockSpec((outer, 2, inner, 3 * PIECE), lambda j, s: (0, 0, 0, j + start)),
            ] + ([full((rows, width))] * 2 if chained else []),
            out_specs=[total, total, grads, grads],
            scratch_shapes=[pltpu.VMEM((rows, 2 * PIECE), BF16)] * 3,
        ),
        out_shape=[jax.ShapeDtypeStruct((rows, width), F32)] * 2 + [grads_shape] * 2,
        compiler_params=pltpu.CompilerParams(dimension_semantics=("arbitrary",), vmem_limit_bytes=60 << 20),
        cost_estimate=pl.CostEstimate(flops=flops, bytes_accessed=40 << 20, transcendentals=rows * steps * 256),
        name="feedforward",
    )(side, n, nt, y, yt, w, *(partial or ()))


def project_kernel(pairs, sizes, x_ref, *refs):
    weights, refs = refs[: len(sizes)], refs[len(sizes) :]
    first_ref, cosine_ref, sine_ref, q_ref, k_ref, v_ref, kt_ref, vt_ref = refs
    lane = lax.broadcasted_iota(jnp.int32, (x_ref.shape[0], 128), 1)
    first = lane % 64 < 32
    cosine, sine = cosine_ref[...], sine_ref[...]

    def turn(u):
        return u * cosine + jnp.where(first, pltpu.roll(u, 96, 1), pltpu.roll(u, 32, 1)) * sine

    pair = 0
    for ref, size in zip(weights, sizes):
        lin = dot_nn(x_ref[...], ref[:, : size * 384])
        for p in range(size):
            cols = slice(pair * 128, pair * 128 + 128)
            q_ref[:, cols] = (turn(lin[:, p * 384 : p * 384 + 128]) * 0.125).astype(BF16)
            k_ref[:, cols] = turn(lin[:, p * 384 + 128 : p * 384 + 256]).astype(BF16)
            v_ref[:, cols] = (0.5 * lin[:, p * 384 + 256 : p * 384 + 384] + 0.5 * first_ref[:, cols].astype(F32)).astype(BF16)
            pair += 1
    kt_ref[...] = k_ref[...].T
    vt_ref[...] = v_ref[...].T


def project(x, weights, sizes, first, cosine, sine):
    length, depth = x.shape
    width = first.shape[1]
    block = min(256, length)
    rows = lambda n: pl.BlockSpec((block, n), lambda i: (i, 0))
    out = jax.ShapeDtypeStruct((length, width), BF16)
    turned = jax.ShapeDtypeStruct((width, length), BF16)
    across = pl.BlockSpec((width, block), lambda i: (0, i))
    return pl.pallas_call(
        functools.partial(project_kernel, width // 128, sizes),
        grid=(length // block,),
        in_specs=[rows(depth)] + [pl.BlockSpec(w.shape, lambda i: (0, 0), pipeline_mode=pl.Buffered(1)) for w in weights] + [rows(width), rows(128), rows(128)],
        out_specs=[rows(width)] * 3 + [across] * 2,
        out_shape=[out] * 3 + [turned] * 2,
        compiler_params=pltpu.CompilerParams(dimension_semantics=("arbitrary",), vmem_limit_bytes=60 << 20),
        cost_estimate=pl.CostEstimate(flops=6 * length * depth * width, bytes_accessed=20 << 20, transcendentals=0),
        name="project",
    )(x, *weights, first, cosine, sine)


def merge_kernel(count, *refs):
    out_ref, start = refs[-1], 0
    for mine, theirs in zip(refs[:count], refs[count:-1]):
        size = mine.shape[1]
        out_ref[:, start : start + size] = (mine[...].astype(F32) + theirs[...].astype(F32)).astype(BF16)
        start += size
    if start < out_ref.shape[1]:
        out_ref[:, start:] = jnp.zeros_like(out_ref[:, start:])


def merge(mine, theirs, columns):
    rows = mine[0].shape[0]
    spec = lambda n: pl.BlockSpec((128, n), lambda i: (i, 0))
    return pl.pallas_call(
        functools.partial(merge_kernel, len(mine)),
        grid=(rows // 128,),
        in_specs=[spec(a.shape[1]) for a in (*mine, *theirs)],
        out_specs=spec(columns),
        out_shape=jax.ShapeDtypeStruct((rows, columns), BF16),
        compiler_params=pltpu.CompilerParams(dimension_semantics=("arbitrary",)),
        cost_estimate=pl.CostEstimate(flops=rows * columns, bytes_accessed=6 * rows * columns, transcendentals=0),
        name="merge",
    )(*mine, *theirs)


EPS = 1e-06
BOTH = ("dp", "tensor")


def row_major(values):
    return with_layout_constraint(values, Layout(tuple(range(values.ndim))))


def norm_parts(values):
    factor = lax.rsqrt(jnp.mean(values * values, axis=-1, keepdims=True) + EPS)
    return values * factor, factor


def norm_back(incoming, gain, normalized, factor):
    scaled = incoming * gain
    gain_grad = jnp.sum(incoming * normalized, axis=0)
    input_grad = factor * (scaled - normalized * jnp.mean(scaled * normalized, axis=-1, keepdims=True))
    return input_grad, gain_grad


def swap(values):
    return lax.ppermute(values, "tensor", [(0, 1), (1, 0)])


def part(values, index, count, axis):
    size = values.shape[axis] // count
    return lax.dynamic_slice_in_dim(values, index * size, size, axis)


def in_order(mine, theirs, axis):
    first = lax.axis_index("tensor") == 0
    return jnp.concatenate([jnp.where(first, mine, theirs), jnp.where(first, theirs, mine)], axis=axis)


def gather_rows(rows, count):
    if count != 2:
        return lax.all_gather(rows, "tensor", axis=0, tiled=True)
    return in_order(rows, swap(rows), 0)


def heads_to_rows(values, count):
    if count != 2:
        return lax.all_to_all(values, "tensor", split_axis=0, concat_axis=1, tiled=True)
    me = lax.axis_index("tensor")
    theirs = swap(part(values, 1 - me, 2, 0))
    return in_order(part(values, me, 2, 0), theirs, 1)


def rows_to_heads(values, count):
    if count != 2:
        return lax.all_to_all(values, "tensor", split_axis=1, concat_axis=0, tiled=True)
    me = lax.axis_index("tensor")
    theirs = swap(part(values, 1 - me, 2, 1))
    return in_order(part(values, me, 2, 1), theirs, 0)


def scatter_product(left, weights, count):
    def product(rows):
        total, start = 0.0, 0
        for weight in weights:
            size = weight.shape[1]
            total = total + dot_nt(rows[:, start : start + size], weight)
            start += size
        return total

    if count != 2:
        return lax.psum_scatter(product(left), "tensor", scatter_dimension=0, tiled=True)
    me = lax.axis_index("tensor")
    theirs = swap(product(part(left, 1 - me, 2, 0)).astype(BF16))
    return product(part(left, me, 2, 0)) + theirs.astype(F32)


def tensor_sum(values, count):
    if count != 2:
        return lax.psum(values, "tensor")
    return values + swap(values)


def pack_hidden(gate, up, down, blocks):
    rows = gate.shape[0]
    stacked = jnp.stack([w.reshape(rows, blocks, -1) for w in (gate, up, down)], axis=2)
    return stacked.reshape(rows, -1)


def unpack_hidden(packed, blocks):
    rows = packed.shape[0]
    pieces = packed.reshape(rows, blocks, 3, -1)
    return [pieces[:, :, which].reshape(rows, -1) for which in range(3)]


def plane_pairs(bit):
    return [(d, d ^ bit) for d in range(16)]


def ring_pairs(shift):
    return [(d, (d + 4 * shift) % 16) for d in range(16)]


def places():
    me = lax.axis_index("dp")
    return me // 4, me // 2 % 2, me % 2


def pick(values, index, axis):
    return lax.dynamic_index_in_dim(values, index, axis, keepdims=False)


def gather_column(shard):
    z, y, x = places()
    column = jnp.zeros((4,) + shard.shape, shard.dtype)
    for shift in range(4):
        piece = shard if shift == 0 else lax.ppermute(shard, "dp", ring_pairs(shift))
        column = lax.dynamic_update_index_in_dim(column, piece, (z + 4 - shift) % 4, 0)
    return column


def gather_plane(column, cuts):
    z, y, x = places()
    mine, start = [], 0
    for size in cuts:
        mine.append(column[:, :, start : start + size])
        start += size
    orders = ((1, 2), (2, 1))
    mine = lax.optimization_barrier(mine)
    beside = [lax.ppermute(own, "dp", plane_pairs(near)) for own, (near, far) in zip(mine, orders)]
    mine, beside = lax.optimization_barrier((mine, beside))
    across = [
        (lax.ppermute(own, "dp", plane_pairs(far)), lax.ppermute(next_own, "dp", plane_pairs(far)))
        for own, next_own, (near, far) in zip(mine, beside, orders)
    ]
    across = lax.optimization_barrier(across)
    out = []
    for own, next_own, (far_own, far_next), (near, far), size in zip(mine, beside, across, orders, cuts):
        pieces = {0: own, near: next_own, far: far_own, 3: far_next}
        whole = jnp.zeros((4, 2, 2) + own.shape[1:], column.dtype)
        for bits, piece in pieces.items():
            spot = (0, y ^ (bits // 2), x ^ (bits % 2), 0, 0)
            whole = lax.dynamic_update_slice(whole, piece[:, None, None], spot)
        out.append(whole.reshape(-1, size))
    return out


def halve(values, index, axis, bit):
    other = lax.ppermute(pick(values, 1 - index, axis), "dp", plane_pairs(bit))
    return pick(values, index, axis) + other


def plane_sends(values):
    z, y, x = places()
    values = values.reshape(4, 2, 2, -1, values.shape[1])
    half = (values.shape[4] // 128 + 1) // 2 * 128
    one, two = values[..., :half], values[..., half:]
    return pick(one, 1 - x, 2), pick(two, 1 - y, 1), pick(one, x, 2), pick(two, y, 1)


def plane_turn(state):
    z, y, x = places()
    send_one, send_two, keep_one, keep_two = state
    one = keep_one + lax.ppermute(send_one, "dp", plane_pairs(1))
    two = keep_two + lax.ppermute(send_two, "dp", plane_pairs(2))
    return pick(one, 1 - y, 1), pick(two, 1 - x, 1), pick(one, y, 1), pick(two, x, 1)


def column_parts(state):
    send_one, send_two, keep_one, keep_two = state
    one = keep_one + lax.ppermute(send_one, "dp", plane_pairs(2))
    two = keep_two + lax.ppermute(send_two, "dp", plane_pairs(1))
    return jnp.concatenate([one, two], axis=2)


def column_sum(parts):
    z, y, x = places()
    total = pick(parts, z, 0).astype(F32)
    for shift in range(1, 4):
        total = total + lax.ppermute(pick(parts, (z + shift) % 4, 0), "dp", ring_pairs(shift)).astype(F32)
    return total


def gain_tree(grads):
    z, y, x = places()
    grads = grads.reshape(2, 4, 2, 2, -1)
    grads = halve(halve(grads, x, 3, 1), y, 2, 2)
    total = pick(grads, z, 1)
    for shift in range(1, 4):
        total = total + lax.ppermute(pick(grads, (z + shift) % 4, 1), "dp", ring_pairs(shift))
    return total.T


def per_device(dp, count, hidden_in, value_first, segment_ids, out_cotangent, attn_gain, w_query, w_key, w_value, w_output, mlp_gain, w_gate, w_up, w_down):
    rows, depth = hidden_in.shape
    width = w_query.shape[1]
    pairs = width // 128
    length = segment_ids.shape[1]
    slab = w_query.shape[0]
    blocks = w_gate.shape[1] * count // 256
    hidden_columns = 3 * w_gate.shape[1]
    tree = dp == 16 and count == 2

    gains = jnp.pad(jnp.stack([attn_gain, mlp_gain], axis=1), ((0, 0), (0, 126)))
    projections = jnp.stack([w.reshape(slab, pairs, 128) for w in (w_query, w_key, w_value)], axis=2).reshape(slab, -1)
    hidden_pack = pack_hidden(w_gate, w_up, w_down.T, blocks)
    if tree:
        early = 6 * 384
        packs = [jnp.concatenate([hidden_pack[:, :early], w_output.T], axis=1), hidden_pack[:, early:]]
        sizes = (pairs - pairs // 2, pairs // 2)
        cut = sizes[0] * 384
        first_pack = jnp.concatenate([projections[:, :cut], projections[:, cut:], gains], axis=1)
        first_column = gather_column(first_pack)
    else:
        early = hidden_columns
        packs = [jnp.concatenate([hidden_pack, w_output.T], axis=1)]
        sizes = (pairs,)
        first_all = [lax.all_gather(jnp.concatenate([projections, gains], axis=1), "dp", axis=0, tiled=True)]
    second_all = [lax.all_gather(pack, BOTH, axis=0, tiled=True).reshape(dp, count, slab, -1) for pack in packs]
    doc_ids = segment_ids[0]
    counts = [jnp.sum(doc_ids < d) for d in (1, 2, 3)]
    starts = jnp.where(doc_ids == 1, counts[0], jnp.where(doc_ids == 2, counts[1], jnp.where(doc_ids == 3, counts[2], 0))).astype(jnp.int32)
    first = starts[::BLK] // BLK
    starts = starts[None, :]
    frequency = 10000.0 ** (-(jnp.arange(HEAD // 2, dtype=F32) * 2.0 / HEAD))
    angles = jnp.arange(length, dtype=F32)[:, None] * frequency[None, :]
    cos, sin = jnp.cos(angles), jnp.sin(angles)
    cosine = jnp.concatenate([cos] * 4, axis=1)
    sine = jnp.concatenate([-sin, sin] * 2, axis=1)
    cost, sint = cos.T, sin.T

    residual = hidden_in.astype(F32)
    flat_one, factor_one = norm_parts(residual)
    if tree:
        first_column, first, starts, cosine, sine, cost, sint, flat_one, factor_one = lax.optimization_barrier(
            (first_column, first, starts, cosine, sine, cost, sint, flat_one, factor_one)
        )
        first_all = gather_plane(first_column, (cut, 3 * width - cut + 128))
        all_gains = first_all[1][:, sizes[1] * 384 :]
    else:
        all_gains = first_all[0][:, 3 * width :]
    gain_one = all_gains[:, 0].astype(F32)
    gain_two = all_gains[:, 1].astype(F32)
    rows_one = row_major(gather_rows(row_major((flat_one * gain_one).astype(BF16)), count))
    query, key, value, key_t, value_t = project(rows_one, first_all, sizes, value_first, cosine, sine)
    attended, log_totals = attention_forward(first, starts, query, key, value_t)
    attended_rows = heads_to_rows(attended, count)
    output_w = second_all[0][:, :, :, early:].transpose(0, 2, 1, 3).reshape(depth, count * width)
    middle = row_major(residual + dot_nt(attended_rows, output_w))

    flat_two, factor_two = norm_parts(middle)
    normed_two = row_major((flat_two * gain_two).astype(BF16))
    if count == 2:
        hidden_w = second_all
    else:
        whole = second_all[0][:, :, :, :hidden_columns].reshape(dp, 2, count // 2, slab, blocks, 3, -1)
        hidden_w = [whole.transpose(1, 0, 3, 4, 5, 2, 6).reshape(1, 2, depth, blocks * 3 * PIECE)]
    side = jnp.full((1,), lax.axis_index("tensor") if tree else 0, jnp.int32)
    partial, keeps, sends = None, [], []
    for w, steps in zip(hidden_w, (6, blocks - 6) if tree else (blocks,)):
        *partial, keep, send = feedforward(side, normed_two, normed_two.T, out_cotangent, out_cotangent.T, w, 0, steps, partial)
        keeps.append(keep)
        sends.append(swap(send) if tree else send)
    branch, normed_two_grad = [row_major(p) for p in partial]
    layer_out = (middle + branch).astype(BF16)
    middle_norm_grad, gain_two_grad = norm_back(normed_two_grad, gain_two, flat_two, factor_two)
    middle_grad = row_major(out_cotangent.astype(F32) + middle_norm_grad)
    branch_grad = row_major(middle_grad.astype(BF16))
    if tree:
        hidden_grads = merge(keeps, sends, hidden_columns + -hidden_columns % 768)
        hidden_grads, branch_grad = lax.optimization_barrier((hidden_grads, branch_grad))
        hidden_sum = lax.psum_scatter(hidden_grads, "dp", scatter_dimension=0, tiled=True).astype(F32)

    attended_grad = rows_to_heads(dot_nn(branch_grad, output_w).astype(BF16), count)
    output_grad = lax.dot_general(branch_grad, attended_rows, (((0,), (0,)), ((), ())), preferred_element_type=F32).astype(BF16)
    if tree:
        me = lax.axis_index("tensor")
        output_grad = row_major(output_grad)
        output_grad = row_major(part(output_grad, me, 2, 1) + swap(part(output_grad, 1 - me, 2, 1)))
    else:
        output_grad = output_grad.reshape(dp, slab, count, width).transpose(0, 2, 1, 3)
        hidden_grads = jnp.stack([keeps[0], sends[0]]).reshape(2, dp, slab, blocks, 3, count // 2, -1).transpose(1, 0, 5, 2, 3, 4, 6)
        second_grads = jnp.concatenate([hidden_grads.reshape(dp, count, slab, -1), output_grad], axis=3)
        second_sum = lax.psum_scatter(second_grads.reshape(dp * count * slab, -1), BOTH, scatter_dimension=0, tiled=True).astype(F32)
        hidden_sum, grad_output = second_sum[:, :hidden_columns], second_sum[:, hidden_columns:].T
    pre, grad_value_first, pair_grads = [], None, []
    for pair in range(pairs):
        pair_pre, grad_value_first = attention_backward(
            pair, first, starts, query, key, key_t, value, attended_grad, attended, log_totals, cosine, sine, cost, sint, grad_value_first
        )
        if tree and pair == 3:
            tree_one, pair_pre = lax.optimization_barrier((column_parts(tree_one), pair_pre))
        pre.append(pair_pre)
        pair_grads.append(row_major(lax.dot_general(rows_one, pair_pre, (((0,), (0,)), ((), ())), preferred_element_type=F32).astype(BF16)))
        if tree and pair == 1:
            tree_one, attended_grad = lax.optimization_barrier((plane_sends(jnp.concatenate([output_grad] + pair_grads, axis=1)), attended_grad))
        if tree and pair == 2:
            tree_one, attended_grad = lax.optimization_barrier((plane_turn(tree_one), attended_grad))
    if tree:
        tree_two, pre = lax.optimization_barrier((plane_sends(jnp.concatenate(pair_grads[2:], axis=1)), pre))
    else:
        projection_grads = jnp.concatenate(pair_grads, axis=1)
    weights = [w[:, : size * 384] for w, size in zip(first_all, sizes)]
    normed_one_grad = row_major(scatter_product(jnp.concatenate(pre, axis=1), weights, count))
    if tree:
        tree_two, tree_one, normed_one_grad = lax.optimization_barrier((plane_turn(tree_two), column_sum(tree_one), normed_one_grad))
    input_norm_grad, gain_one_grad = norm_back(normed_one_grad, gain_one, flat_one, factor_one)
    grad_input = row_major(middle_grad + input_norm_grad)
    gain_grads = jnp.stack([gain_one_grad, gain_two_grad], axis=1)
    if tree:
        gain_grads = gain_grads.T
        tree_two, gain_grads = lax.optimization_barrier((column_parts(tree_two), gain_grads + swap(gain_grads)))
        gain_sum = gain_tree(gain_grads)
        grad_output = tree_one[:, :width].T
        first_sum = jnp.concatenate([tree_one[:, width:], column_sum(tree_two)], axis=1)
    else:
        gain_grads = jnp.pad(lax.psum(gain_grads, "tensor").astype(BF16), ((0, 0), (0, 126)))
        first_sum = lax.psum_scatter(jnp.concatenate([projection_grads, gain_grads], axis=1), "dp", scatter_dimension=0, tiled=True).astype(F32)
        gain_sum = first_sum[:, 3 * width : 3 * width + 2]
        first_sum = first_sum[:, : 3 * width]
    grad_gate, grad_up, grad_down = unpack_hidden(hidden_sum[:, :hidden_columns], blocks)
    grad_query, grad_key, grad_value = unpack_hidden(first_sum, pairs)
    return (
        layer_out,
        grad_input,
        grad_value_first,
        gain_sum[:, 0],
        grad_query,
        grad_key,
        grad_value,
        grad_output,
        gain_sum[:, 1],
        grad_gate,
        grad_up,
        grad_down.T,
    )


def solution(mesh):
    tokens, split = P(BOTH, None), P("dp", "tensor")
    across = P("tensor", "dp")
    return jax.shard_map(
        functools.partial(per_device, mesh.shape["dp"], mesh.shape["tensor"]),
        mesh=mesh,
        in_specs=(tokens, split, P("dp", None), tokens, P("dp"), split, split, split, across, P("dp"), split, split, across),
        out_specs=(tokens, tokens, split, P("dp"), split, split, split, across, P("dp"), split, split, across),
        check_vma=False,
    )
```

```python
import functools

import jax
import jax.numpy as jnp
from jax import lax
from jax.experimental import pallas as pl
from jax.experimental.pallas import tpu as pltpu
from jax.experimental.layout import Layout, with_layout_constraint
from jax.sharding import PartitionSpec as P

HEAD = 64
PIECE = 128
NEG = -1e30
BLK = 256
F32 = jnp.float32
BF16 = jnp.bfloat16


def dot_nt(a, b, precision=None):
    return lax.dot_general(a, b, (((1,), (1,)), ((), ())), precision=precision, preferred_element_type=F32)


def dot_nn(a, b):
    return jnp.dot(a, b, preferred_element_type=F32)


def bias_tile(starts_ref, first_key, first_query):
    place = lax.broadcasted_iota(jnp.int32, (BLK, BLK), 0)
    low = starts_ref[...] - first_key
    high = lax.broadcasted_iota(jnp.int32, (1, BLK), 1) + (first_query - first_key)
    return jnp.where((place >= low) & (place <= high), 0.0, NEG)


def forward_kernel(heads, first_ref, starts_ref, q_ref, k_ref, vt_ref, out_ref, lse_ref, masked_q, bias_ref, top_ref, total_ref, acc_ref):
    step = pl.program_id(0)
    lane = lax.broadcasted_iota(jnp.int32, (BLK, 128), 1)
    for head in range(heads):
        pair = pl.ds((head // 2) * 128, 128)
        block = q_ref[:, pair]
        keep = (lane < 64) if head % 2 == 0 else (lane >= 64)
        masked_q[head] = jnp.where(keep, block, jnp.zeros_like(block))
    top_ref[...] = jnp.full_like(top_ref, NEG)
    total_ref[...] = jnp.zeros_like(total_ref)
    acc_ref[...] = jnp.zeros_like(acc_ref)

    def chunk(c, carry):
        base = pl.multiple_of(c * BLK, BLK)
        bias_ref[...] = bias_tile(starts_ref, base, step * BLK)
        for head in range(heads):
            keys = k_ref[pl.ds(base, BLK), pl.ds((head // 2) * 128, 128)]
            scores = dot_nt(keys, masked_q[head]) + bias_ref[...]
            old = top_ref[head : head + 1, :]
            new = jnp.maximum(old, jnp.max(scores, axis=0, keepdims=True))
            probs = jnp.exp(scores - new)
            shrink = jnp.exp(old - new)
            top_ref[head : head + 1, :] = new
            total_ref[head : head + 1, :] = total_ref[head : head + 1, :] * shrink + jnp.sum(probs, axis=0, keepdims=True)
            rows = slice(head * 64, head * 64 + 64)
            part = dot_nn(vt_ref[rows, pl.ds(base, BLK)], probs.astype(BF16))
            acc_ref[rows, :] = acc_ref[rows, :] * shrink + part
        return carry

    lax.fori_loop(first_ref[step], step + 1, chunk, 0)
    for head in range(heads):
        rows = slice(head * 64, head * 64 + 64)
        acc_ref[rows, :] = acc_ref[rows, :] / total_ref[head : head + 1, :]
    out_ref[...] = acc_ref[...].T.astype(BF16)
    lse_ref[...] = (top_ref[...] + jnp.log(total_ref[...])).reshape(lse_ref.shape)


def attention_forward(first, starts, q, k, vt):
    length, width = q.shape
    heads = width // HEAD
    return pl.pallas_call(
        functools.partial(forward_kernel, heads),
        grid_spec=pltpu.PrefetchScalarGridSpec(
            num_scalar_prefetch=1,
            grid=(length // BLK,),
            in_specs=[
                pl.BlockSpec((1, BLK), lambda i, f: (0, i)),
                pl.BlockSpec((BLK, width), lambda i, f: (i, 0)),
                pl.BlockSpec((length, width), lambda i, f: (0, 0)),
                pl.BlockSpec((width, length), lambda i, f: (0, 0)),
            ],
            out_specs=[
                pl.BlockSpec((BLK, width), lambda i, f: (i, 0)),
                pl.BlockSpec((heads // 2, 2, BLK), lambda i, f: (0, 0, i)),
            ],
            scratch_shapes=[
                pltpu.VMEM((heads, BLK, 128), BF16),
                pltpu.VMEM((BLK, BLK), F32),
                pltpu.VMEM((heads, BLK), F32),
                pltpu.VMEM((heads, BLK), F32),
                pltpu.VMEM((width, BLK), F32),
            ],
        ),
        out_shape=[
            jax.ShapeDtypeStruct((length, width), BF16),
            jax.ShapeDtypeStruct((heads // 2, 2, length), F32),
        ],
        compiler_params=pltpu.CompilerParams(dimension_semantics=("arbitrary",)),
        name="attention_forward",
    )(first, starts, q, k, vt)


def unrotate_lanes(block, cosine, sine, lane):
    other = jnp.where(lane % 64 < 32, pltpu.roll(block, 96, 1), pltpu.roll(block, 32, 1))
    return block * cosine - other * sine


def backward_kernel(first_ref, starts_ref, q_ref, k_ref, kt_ref, v_ref, do_ref, o_ref, lse_ref, cosine_ref, sine_ref, cost_ref, sint_ref, *refs):
    pre_ref, gv_ref, masked_q, masked_do, bias_ref, delta_ref, dqt_ref, dk_acc, dv_acc = refs[-9:]
    step = pl.program_id(0)
    lane = lax.broadcasted_iota(jnp.int32, (BLK, 128), 1)

    @pl.when(step == 0)
    def _():
        dk_acc[...] = jnp.zeros_like(dk_acc)
        dv_acc[...] = jnp.zeros_like(dv_acc)

    for head in range(2):
        keep = (lane < 64) if head == 0 else (lane >= 64)
        masked_q[head] = jnp.where(keep, q_ref[...], jnp.zeros_like(q_ref))
        masked_do[head] = jnp.where(keep, do_ref[...], jnp.zeros_like(do_ref))
    product = do_ref[...].astype(F32) * o_ref[...].astype(F32)
    chooser = (lax.broadcasted_iota(jnp.int32, (8, 128), 1) // HEAD == lax.broadcasted_iota(jnp.int32, (8, 128), 0)).astype(F32)
    delta_ref[...] = dot_nt(chooser, product, lax.Precision.HIGHEST)
    dqt_ref[...] = jnp.zeros_like(dqt_ref)
    both_q = masked_q[...].reshape(2 * BLK, 128)
    both_do = masked_do[...].reshape(2 * BLK, 128)

    def chunk(c, carry):
        here = pl.ds(pl.multiple_of(c * BLK, BLK), BLK)
        bias_ref[...] = bias_tile(starts_ref, c * BLK, step * BLK)
        keys = k_ref[here, :]
        vals = v_ref[here, :]
        probs_low, grads_low = [], []
        for head in range(2):
            scores = dot_nt(keys, masked_q[head]) + bias_ref[...]
            probs = jnp.exp(scores - lse_ref[0, head : head + 1, :])
            prob_grad = dot_nt(vals, masked_do[head])
            score_grad = (probs * (prob_grad - delta_ref[head : head + 1, :])).astype(BF16)
            probs_low.append(probs.astype(BF16))
            grads_low.append(score_grad)
            rows = slice(head * 64, head * 64 + 64)
            dqt_ref[rows, :] += dot_nn(kt_ref[rows, here], score_grad)
        dv_acc[here, :] += dot_nn(jnp.concatenate(probs_low, axis=1), both_do)
        dk_acc[here, :] += dot_nn(jnp.concatenate(grads_low, axis=1), both_q)
        return carry

    lax.fori_loop(first_ref[step], step + 1, chunk, 0)
    cost, sint = cost_ref[...] * (HEAD**-0.5), sint_ref[...] * (HEAD**-0.5)
    for head in range(2):
        low = dqt_ref[head * 64 : head * 64 + 32, :]
        high = dqt_ref[head * 64 + 32 : head * 64 + 64, :]
        dqt_ref[head * 64 : head * 64 + 32, :] = low * cost + high * sint
        dqt_ref[head * 64 + 32 : head * 64 + 64, :] = high * cost - low * sint
    pre_ref[pl.ds(pl.multiple_of(step * BLK, BLK), BLK), :128] = dqt_ref[...].T.astype(BF16)

    @pl.when(step == pl.num_programs(0) - 1)
    def _():
        def finish(c, carry):
            here = pl.ds(pl.multiple_of(c * BLK, BLK), BLK)
            pre_ref[here, 128:256] = unrotate_lanes(dk_acc[here, :], cosine_ref[here, :], sine_ref[here, :], lane).astype(BF16)
            half = 0.5 * dv_acc[here, :]
            gv_ref[here, :] = half
            pre_ref[here, 256:] = half.astype(BF16)
            return carry
        lax.fori_loop(0, dk_acc.shape[0] // BLK, finish, 0)


def attention_backward(pair, first, starts, q, k, kt, v, do, o, lse, cosine, sine, cost, sint, values=None):
    length = q.shape[0]
    earlier = [] if values is None else [values]
    rows = pl.BlockSpec((BLK, 128), lambda i, f: (i, pair))
    whole = pl.BlockSpec((length, 128), lambda i, f: (0, pair))
    table = pl.BlockSpec((length, 128), lambda i, f: (0, 0))
    tile = length * BLK * 2 * 3
    return pl.pallas_call(
        backward_kernel,
        grid_spec=pltpu.PrefetchScalarGridSpec(
            num_scalar_prefetch=1,
            grid=(length // BLK,),
            in_specs=[
                pl.BlockSpec((1, BLK), lambda i, f: (0, i)),
                rows, whole,
                pl.BlockSpec((128, length), lambda i, f: (pair, 0)),
                whole, rows, rows,
                pl.BlockSpec((1, 2, BLK), lambda i, f: (pair, 0, i)),
                table, table,
                pl.BlockSpec((32, BLK), lambda i, f: (0, i)),
                pl.BlockSpec((32, BLK), lambda i, f: (0, i)),
            ] + [pl.BlockSpec(memory_space=pl.ANY)] * len(earlier),
            out_specs=[pl.BlockSpec((length, 384), lambda i, f: (0, 0)), whole],
            scratch_shapes=[
                pltpu.VMEM((2, BLK, 128), BF16),
                pltpu.VMEM((2, BLK, 128), BF16),
                pltpu.VMEM((BLK, BLK), F32),
                pltpu.VMEM((8, BLK), F32),
                pltpu.VMEM((128, BLK), F32),
                pltpu.VMEM((length, 128), F32),
                pltpu.VMEM((length, 128), F32),
            ],
        ),
        out_shape=[jax.ShapeDtypeStruct((length, 384), BF16), jax.ShapeDtypeStruct(q.shape, F32)],
        input_output_aliases={13: 1} if earlier else {},
        compiler_params=pltpu.CompilerParams(dimension_semantics=("arbitrary",)),
        cost_estimate=pl.CostEstimate(flops=tile * 128 * 32, bytes_accessed=8 << 20, transcendentals=tile),
        name="attention_backward",
    )(first, starts, q, k, kt, v, do, o, lse, cosine, sine, cost, sint, *earlier)

def feedforward_kernel(width, chained, side_ref, n_ref, nt_ref, y_ref, yt_ref, w_ref, *refs):
    if chained:
        out_in, e_in, *refs = refs
    out_ref, e_ref, keep_ref, send_ref, h_ref, dg_ref, du_ref = refs
    step = pl.program_id(0)
    rows = n_ref.shape[0]
    tile = 1024 if rows % 1024 == 0 else rows

    @pl.when(step == 0)
    def _():
        out_ref[...] = out_in[...] if chained else jnp.zeros_like(out_ref)
        e_ref[...] = e_in[...] if chained else jnp.zeros_like(e_ref)

    def weight(which):
        cols = slice(which * PIECE, which * PIECE + PIECE)
        return jnp.concatenate([w_ref[:, side, :, cols].reshape(width, PIECE) for side in range(2)], axis=1)

    gate_w, up_w, down_w = weight(0), weight(1), weight(2)

    def row_block(i, carry):
        here = pl.ds(pl.multiple_of(i * tile, tile), tile)
        gate = dot_nn(n_ref[here, :], gate_w)
        up = dot_nn(n_ref[here, :], up_w)
        dhid = dot_nn(y_ref[here, :], down_w)
        sig = 1.0 / (1.0 + jnp.exp(-gate))
        silu = gate * sig
        hidden = (silu * up).astype(BF16)
        dgate = (dhid * up * (sig * (1.0 + gate * (1.0 - sig)))).astype(BF16)
        dup = (dhid * silu).astype(BF16)
        h_ref[here, :] = hidden
        dg_ref[here, :] = dgate
        du_ref[here, :] = dup
        out_ref[here, :] += dot_nt(hidden, down_w)
        e_ref[here, :] += dot_nt(dgate, gate_w) + dot_nt(dup, up_w)
        return carry

    lax.fori_loop(0, rows // tile, row_block, 0)
    swapped = side_ref[0] != 0
    for which, (left, right) in enumerate(((nt_ref, dg_ref), (nt_ref, du_ref), (yt_ref, h_ref))):
        cols = slice(which * PIECE, which * PIECE + PIECE)
        grad = dot_nn(left[...], right[...])
        low, high = grad[:, :PIECE], grad[:, PIECE:]
        keep_ref[:, cols] = jnp.where(swapped, high, low).astype(BF16)
        send_ref[:, cols] = jnp.where(swapped, low, high).astype(BF16)


def feedforward(side, n, nt, y, yt, w, start, steps, partial=None):
    rows, width = n.shape
    outer, _, inner, _ = w.shape
    chained = partial is not None
    full = lambda shape: pl.BlockSpec(shape, lambda j, s: (0, 0), pipeline_mode=pl.Buffered(1))
    grads = pl.BlockSpec((width, 3 * PIECE), lambda j, s: (0, j))
    total = pl.BlockSpec((rows, width), lambda j, s: (0, 0))
    grads_shape = jax.ShapeDtypeStruct((width, steps * 3 * PIECE), BF16)
    flops = 18 * rows * width * steps * 2 * PIECE
    return pl.pallas_call(
        functools.partial(feedforward_kernel, width, chained),
        grid_spec=pltpu.PrefetchScalarGridSpec(
            num_scalar_prefetch=1,
            grid=(steps,),
            in_specs=[
                full((rows, width)), full((width, rows)), full((rows, width)), full((width, rows)),
                pl.BlockSpec((outer, 2, inner, 3 * PIECE), lambda j, s: (0, 0, 0, j + start)),
            ] + ([full((rows, width))] * 2 if chained else []),
            out_specs=[total, total, grads, grads],
            scratch_shapes=[pltpu.VMEM((rows, 2 * PIECE), BF16)] * 3,
        ),
        out_shape=[jax.ShapeDtypeStruct((rows, width), F32)] * 2 + [grads_shape] * 2,
        compiler_params=pltpu.CompilerParams(dimension_semantics=("arbitrary",), vmem_limit_bytes=60 << 20),
        cost_estimate=pl.CostEstimate(flops=flops, bytes_accessed=40 << 20, transcendentals=rows * steps * 256),
        name="feedforward",
    )(side, n, nt, y, yt, w, *(partial or ()))


def project_kernel(pairs, sizes, x_ref, *refs):
    weights, refs = refs[: len(sizes)], refs[len(sizes) :]
    first_ref, cosine_ref, sine_ref, q_ref, k_ref, v_ref, kt_ref, vt_ref = refs
    lane = lax.broadcasted_iota(jnp.int32, (x_ref.shape[0], 128), 1)
    first = lane % 64 < 32
    cosine, sine = cosine_ref[...], sine_ref[...]

    def turn(u):
        return u * cosine + jnp.where(first, pltpu.roll(u, 96, 1), pltpu.roll(u, 32, 1)) * sine

    pair = 0
    for ref, size in zip(weights, sizes):
        lin = dot_nn(x_ref[...], ref[:, : size * 384])
        for p in range(size):
            cols = slice(pair * 128, pair * 128 + 128)
            q_ref[:, cols] = (turn(lin[:, p * 384 : p * 384 + 128]) * 0.125).astype(BF16)
            k_ref[:, cols] = turn(lin[:, p * 384 + 128 : p * 384 + 256]).astype(BF16)
            v_ref[:, cols] = (0.5 * lin[:, p * 384 + 256 : p * 384 + 384] + 0.5 * first_ref[:, cols].astype(F32)).astype(BF16)
            pair += 1
    kt_ref[...] = k_ref[...].T
    vt_ref[...] = v_ref[...].T


def project(x, weights, sizes, first, cosine, sine):
    length, depth = x.shape
    width = first.shape[1]
    block = min(256, length)
    rows = lambda n: pl.BlockSpec((block, n), lambda i: (i, 0))
    out = jax.ShapeDtypeStruct((length, width), BF16)
    turned = jax.ShapeDtypeStruct((width, length), BF16)
    across = pl.BlockSpec((width, block), lambda i: (0, i))
    return pl.pallas_call(
        functools.partial(project_kernel, width // 128, sizes),
        grid=(length // block,),
        in_specs=[rows(depth)] + [pl.BlockSpec(w.shape, lambda i: (0, 0), pipeline_mode=pl.Buffered(1)) for w in weights] + [rows(width), rows(128), rows(128)],
        out_specs=[rows(width)] * 3 + [across] * 2,
        out_shape=[out] * 3 + [turned] * 2,
        compiler_params=pltpu.CompilerParams(dimension_semantics=("arbitrary",), vmem_limit_bytes=60 << 20),
        cost_estimate=pl.CostEstimate(flops=6 * length * depth * width, bytes_accessed=20 << 20, transcendentals=0),
        name="project",
    )(x, *weights, first, cosine, sine)


def merge_kernel(count, *refs):
    out_ref, start = refs[-1], 0
    for mine, theirs in zip(refs[:count], refs[count:-1]):
        size = mine.shape[1]
        out_ref[:, start : start + size] = (mine[...].astype(F32) + theirs[...].astype(F32)).astype(BF16)
        start += size
    if start < out_ref.shape[1]:
        out_ref[:, start:] = jnp.zeros_like(out_ref[:, start:])


def merge(mine, theirs, columns):
    rows = mine[0].shape[0]
    spec = lambda n: pl.BlockSpec((128, n), lambda i: (i, 0))
    return pl.pallas_call(
        functools.partial(merge_kernel, len(mine)),
        grid=(rows // 128,),
        in_specs=[spec(a.shape[1]) for a in (*mine, *theirs)],
        out_specs=spec(columns),
        out_shape=jax.ShapeDtypeStruct((rows, columns), BF16),
        compiler_params=pltpu.CompilerParams(dimension_semantics=("arbitrary",)),
        cost_estimate=pl.CostEstimate(flops=rows * columns, bytes_accessed=6 * rows * columns, transcendentals=0),
        name="merge",
    )(*mine, *theirs)


EPS = 1e-06
BOTH = ("dp", "tensor")


def row_major(values):
    return with_layout_constraint(values, Layout(tuple(range(values.ndim))))


def norm_parts(values):
    factor = lax.rsqrt(jnp.mean(values * values, axis=-1, keepdims=True) + EPS)
    return values * factor, factor


def norm_back(incoming, gain, normalized, factor):
    scaled = incoming * gain
    gain_grad = jnp.sum(incoming * normalized, axis=0)
    input_grad = factor * (scaled - normalized * jnp.mean(scaled * normalized, axis=-1, keepdims=True))
    return input_grad, gain_grad


def swap(values):
    return lax.ppermute(values, "tensor", [(0, 1), (1, 0)])


def part(values, index, count, axis):
    size = values.shape[axis] // count
    return lax.dynamic_slice_in_dim(values, index * size, size, axis)


def in_order(mine, theirs, axis):
    first = lax.axis_index("tensor") == 0
    return jnp.concatenate([jnp.where(first, mine, theirs), jnp.where(first, theirs, mine)], axis=axis)


def gather_rows(rows, count):
    if count != 2:
        return lax.all_gather(rows, "tensor", axis=0, tiled=True)
    return in_order(rows, swap(rows), 0)


def heads_to_rows(values, count):
    if count != 2:
        return lax.all_to_all(values, "tensor", split_axis=0, concat_axis=1, tiled=True)
    me = lax.axis_index("tensor")
    theirs = swap(part(values, 1 - me, 2, 0))
    return in_order(part(values, me, 2, 0), theirs, 1)


def rows_to_heads(values, count):
    if count != 2:
        return lax.all_to_all(values, "tensor", split_axis=1, concat_axis=0, tiled=True)
    me = lax.axis_index("tensor")
    theirs = swap(part(values, 1 - me, 2, 1))
    return in_order(part(values, me, 2, 1), theirs, 0)


def scatter_product(left, weights, count):
    def product(rows):
        total, start = 0.0, 0
        for weight in weights:
            size = weight.shape[1]
            total = total + dot_nt(rows[:, start : start + size], weight)
            start += size
        return total

    if count != 2:
        return lax.psum_scatter(product(left), "tensor", scatter_dimension=0, tiled=True)
    me = lax.axis_index("tensor")
    theirs = swap(product(part(left, 1 - me, 2, 0)).astype(BF16))
    return product(part(left, me, 2, 0)) + theirs.astype(F32)


def tensor_sum(values, count):
    if count != 2:
        return lax.psum(values, "tensor")
    return values + swap(values)


def pack_hidden(gate, up, down, blocks):
    rows = gate.shape[0]
    stacked = jnp.stack([w.reshape(rows, blocks, -1) for w in (gate, up, down)], axis=2)
    return stacked.reshape(rows, -1)


def unpack_hidden(packed, blocks):
    rows = packed.shape[0]
    pieces = packed.reshape(rows, blocks, 3, -1)
    return [pieces[:, :, which].reshape(rows, -1) for which in range(3)]


def plane_pairs(bit):
    return [(d, d ^ bit) for d in range(16)]


def ring_pairs(shift):
    return [(d, (d + 4 * shift) % 16) for d in range(16)]


def places():
    me = lax.axis_index("dp")
    return me // 4, me // 2 % 2, me % 2


def pick(values, index, axis):
    return lax.dynamic_index_in_dim(values, index, axis, keepdims=False)


def gather_column(shard):
    z, y, x = places()
    column = jnp.zeros((4,) + shard.shape, shard.dtype)
    for shift in range(4):
        piece = shard if shift == 0 else lax.ppermute(shard, "dp", ring_pairs(shift))
        column = lax.dynamic_update_index_in_dim(column, piece, (z + 4 - shift) % 4, 0)
    return column


def gather_plane(column, cuts):
    z, y, x = places()
    mine, start = [], 0
    for size in cuts:
        mine.append(column[:, :, start : start + size])
        start += size
    orders = ((1, 2), (2, 1))
    mine = lax.optimization_barrier(mine)
    beside = [lax.ppermute(own, "dp", plane_pairs(near)) for own, (near, far) in zip(mine, orders)]
    mine, beside = lax.optimization_barrier((mine, beside))
    across = [
        (lax.ppermute(own, "dp", plane_pairs(far)), lax.ppermute(next_own, "dp", plane_pairs(far)))
        for own, next_own, (near, far) in zip(mine, beside, orders)
    ]
    across = lax.optimization_barrier(across)
    out = []
    for own, next_own, (far_own, far_next), (near, far), size in zip(mine, beside, across, orders, cuts):
        pieces = {0: own, near: next_own, far: far_own, 3: far_next}
        whole = jnp.zeros((4, 2, 2) + own.shape[1:], column.dtype)
        for bits, piece in pieces.items():
            spot = (0, y ^ (bits // 2), x ^ (bits % 2), 0, 0)
            whole = lax.dynamic_update_slice(whole, piece[:, None, None], spot)
        out.append(whole.reshape(-1, size))
    return out


def halve(values, index, axis, bit):
    other = lax.ppermute(pick(values, 1 - index, axis), "dp", plane_pairs(bit))
    return pick(values, index, axis) + other


def plane_sends(values):
    z, y, x = places()
    values = values.reshape(4, 2, 2, -1, values.shape[1])
    half = (values.shape[4] // 128 + 1) // 2 * 128
    one, two = values[..., :half], values[..., half:]
    return pick(one, 1 - x, 2), pick(two, 1 - y, 1), pick(one, x, 2), pick(two, y, 1)


def plane_turn(state):
    z, y, x = places()
    send_one, send_two, keep_one, keep_two = state
    one = keep_one + lax.ppermute(send_one, "dp", plane_pairs(1))
    two = keep_two + lax.ppermute(send_two, "dp", plane_pairs(2))
    return pick(one, 1 - y, 1), pick(two, 1 - x, 1), pick(one, y, 1), pick(two, x, 1)


def column_parts(state):
    send_one, send_two, keep_one, keep_two = state
    one = keep_one + lax.ppermute(send_one, "dp", plane_pairs(2))
    two = keep_two + lax.ppermute(send_two, "dp", plane_pairs(1))
    return jnp.concatenate([one, two], axis=2)


def column_sum(parts):
    z, y, x = places()
    total = pick(parts, z, 0).astype(F32)
    for shift in range(1, 4):
        total = total + lax.ppermute(pick(parts, (z + shift) % 4, 0), "dp", ring_pairs(shift)).astype(F32)
    return total


def gain_tree(grads):
    z, y, x = places()
    grads = grads.reshape(2, 4, 2, 2, -1)
    grads = halve(halve(grads, x, 3, 1), y, 2, 2)
    total = pick(grads, z, 1)
    for shift in range(1, 4):
        total = total + lax.ppermute(pick(grads, (z + shift) % 4, 1), "dp", ring_pairs(shift))
    return total.T


def per_device(dp, count, hidden_in, value_first, segment_ids, out_cotangent, attn_gain, w_query, w_key, w_value, w_output, mlp_gain, w_gate, w_up, w_down):
    rows, depth = hidden_in.shape
    width = w_query.shape[1]
    pairs = width // 128
    length = segment_ids.shape[1]
    slab = w_query.shape[0]
    blocks = w_gate.shape[1] * count // 256
    hidden_columns = 3 * w_gate.shape[1]
    tree = dp == 16 and count == 2

    gains = jnp.pad(jnp.stack([attn_gain, mlp_gain], axis=1), ((0, 0), (0, 126)))
    projections = jnp.stack([w.reshape(slab, pairs, 128) for w in (w_query, w_key, w_value)], axis=2).reshape(slab, -1)
    hidden_pack = pack_hidden(w_gate, w_up, w_down.T, blocks)
    if tree:
        early = 6 * 384
        packs = [jnp.concatenate([hidden_pack[:, :early], w_output.T], axis=1), hidden_pack[:, early:]]
        sizes = (pairs - pairs // 2, pairs // 2)
        cut = sizes[0] * 384
        first_pack = jnp.concatenate([projections[:, :cut], projections[:, cut:], gains], axis=1)
        first_column = gather_column(first_pack)
    else:
        early = hidden_columns
        packs = [jnp.concatenate([hidden_pack, w_output.T], axis=1)]
        sizes = (pairs,)
        first_all = [lax.all_gather(jnp.concatenate([projections, gains], axis=1), "dp", axis=0, tiled=True)]
    second_all = [lax.all_gather(pack, BOTH, axis=0, tiled=True).reshape(dp, count, slab, -1) for pack in packs]
    doc_ids = segment_ids[0]
    counts = [jnp.sum(doc_ids < d) for d in (1, 2, 3)]
    starts = jnp.where(doc_ids == 1, counts[0], jnp.where(doc_ids == 2, counts[1], jnp.where(doc_ids == 3, counts[2], 0))).astype(jnp.int32)
    first = starts[::BLK] // BLK
    starts = starts[None, :]
    frequency = 10000.0 ** (-(jnp.arange(HEAD // 2, dtype=F32) * 2.0 / HEAD))
    angles = jnp.arange(length, dtype=F32)[:, None] * frequency[None, :]
    cos, sin = jnp.cos(angles), jnp.sin(angles)
    cosine = jnp.concatenate([cos] * 4, axis=1)
    sine = jnp.concatenate([-sin, sin] * 2, axis=1)
    cost, sint = cos.T, sin.T

    residual = hidden_in.astype(F32)
    flat_one, factor_one = norm_parts(residual)
    if tree:
        first_column, first, starts, cosine, sine, cost, sint, flat_one, factor_one = lax.optimization_barrier(
            (first_column, first, starts, cosine, sine, cost, sint, flat_one, factor_one)
        )
        first_all = gather_plane(first_column, (cut, 3 * width - cut + 128))
        all_gains = first_all[1][:, sizes[1] * 384 :]
    else:
        all_gains = first_all[0][:, 3 * width :]
    gain_one = all_gains[:, 0].astype(F32)
    gain_two = all_gains[:, 1].astype(F32)
    rows_one = row_major(gather_rows(row_major((flat_one * gain_one).astype(BF16)), count))
    query, key, value, key_t, value_t = project(rows_one, first_all, sizes, value_first, cosine, sine)
    attended, log_totals = attention_forward(first, starts, query, key, value_t)
    attended_rows = heads_to_rows(attended, count)
    output_w = second_all[0][:, :, :, early:].transpose(0, 2, 1, 3).reshape(depth, count * width)
    middle = row_major(residual + dot_nt(attended_rows, output_w))

    flat_two, factor_two = norm_parts(middle)
    normed_two = row_major((flat_two * gain_two).astype(BF16))
    if count == 2:
        hidden_w = second_all
    else:
        whole = second_all[0][:, :, :, :hidden_columns].reshape(dp, 2, count // 2, slab, blocks, 3, -1)
        hidden_w = [whole.transpose(1, 0, 3, 4, 5, 2, 6).reshape(1, 2, depth, blocks * 3 * PIECE)]
    side = jnp.full((1,), lax.axis_index("tensor") if tree else 0, jnp.int32)
    partial, keeps, sends = None, [], []
    for w, steps in zip(hidden_w, (6, blocks - 6) if tree else (blocks,)):
        *partial, keep, send = feedforward(side, normed_two, normed_two.T, out_cotangent, out_cotangent.T, w, 0, steps, partial)
        keeps.append(keep)
        sends.append(swap(send) if tree else send)
    branch, normed_two_grad = [row_major(p) for p in partial]
    layer_out = (middle + branch).astype(BF16)
    middle_norm_grad, gain_two_grad = norm_back(normed_two_grad, gain_two, flat_two, factor_two)
    middle_grad = row_major(out_cotangent.astype(F32) + middle_norm_grad)
    branch_grad = row_major(middle_grad.astype(BF16))
    if tree:
        hidden_grads = merge(keeps, sends, hidden_columns + -hidden_columns % 768)
        hidden_grads, branch_grad = lax.optimization_barrier((hidden_grads, branch_grad))
        hidden_sum = lax.psum_scatter(hidden_grads, "dp", scatter_dimension=0, tiled=True).astype(F32)

    attended_grad = rows_to_heads(dot_nn(branch_grad, output_w).astype(BF16), count)
    output_grad = lax.dot_general(branch_grad, attended_rows, (((0,), (0,)), ((), ())), preferred_element_type=F32).astype(BF16)
    if tree:
        me = lax.axis_index("tensor")
        output_grad = row_major(output_grad)
        output_grad = row_major(part(output_grad, me, 2, 1) + swap(part(output_grad, 1 - me, 2, 1)))
    else:
        output_grad = output_grad.reshape(dp, slab, count, width).transpose(0, 2, 1, 3)
        hidden_grads = jnp.stack([keeps[0], sends[0]]).reshape(2, dp, slab, blocks, 3, count // 2, -1).transpose(1, 0, 5, 2, 3, 4, 6)
        second_grads = jnp.concatenate([hidden_grads.reshape(dp, count, slab, -1), output_grad], axis=3)
        second_sum = lax.psum_scatter(second_grads.reshape(dp * count * slab, -1), BOTH, scatter_dimension=0, tiled=True).astype(F32)
        hidden_sum, grad_output = second_sum[:, :hidden_columns], second_sum[:, hidden_columns:].T
    pre, grad_value_first, pair_grads = [], None, []
    for pair in range(pairs):
        pair_pre, grad_value_first = attention_backward(
            pair, first, starts, query, key, key_t, value, attended_grad, attended, log_totals, cosine, sine, cost, sint, grad_value_first
        )
        if tree and pair == 3:
            tree_one, pair_pre = lax.optimization_barrier((column_parts(tree_one), pair_pre))
        pre.append(pair_pre)
        pair_grads.append(row_major(lax.dot_general(rows_one, pair_pre, (((0,), (0,)), ((), ())), preferred_element_type=F32).astype(BF16)))
        if tree and pair == 1:
            tree_one, attended_grad = lax.optimization_barrier((plane_sends(jnp.concatenate([output_grad] + pair_grads, axis=1)), attended_grad))
        if tree and pair == 2:
            tree_one, attended_grad = lax.optimization_barrier((plane_turn(tree_one), attended_grad))
    if tree:
        tree_two, pre = lax.optimization_barrier((plane_sends(jnp.concatenate(pair_grads[2:], axis=1)), pre))
    else:
        projection_grads = jnp.concatenate(pair_grads, axis=1)
    weights = [w[:, : size * 384] for w, size in zip(first_all, sizes)]
    normed_one_grad = row_major(scatter_product(jnp.concatenate(pre, axis=1), weights, count))
    if tree:
        tree_two, tree_one, normed_one_grad = lax.optimization_barrier((plane_turn(tree_two), tree_one, normed_one_grad))
        tree_one = column_sum(tree_one)
    input_norm_grad, gain_one_grad = norm_back(normed_one_grad, gain_one, flat_one, factor_one)
    grad_input = row_major(middle_grad + input_norm_grad)
    gain_grads = jnp.stack([gain_one_grad, gain_two_grad], axis=1)
    if tree:
        gain_grads = gain_grads.T
        tree_two, gain_grads = lax.optimization_barrier((column_parts(tree_two), gain_grads + swap(gain_grads)))
        gain_sum = gain_tree(gain_grads)
        grad_output = tree_one[:, :width].T
        first_sum = jnp.concatenate([tree_one[:, width:], column_sum(tree_two)], axis=1)
    else:
        gain_grads = jnp.pad(lax.psum(gain_grads, "tensor").astype(BF16), ((0, 0), (0, 126)))
        first_sum = lax.psum_scatter(jnp.concatenate([projection_grads, gain_grads], axis=1), "dp", scatter_dimension=0, tiled=True).astype(F32)
        gain_sum = first_sum[:, 3 * width : 3 * width + 2]
        first_sum = first_sum[:, : 3 * width]
    grad_gate, grad_up, grad_down = unpack_hidden(hidden_sum[:, :hidden_columns], blocks)
    grad_query, grad_key, grad_value = unpack_hidden(first_sum, pairs)
    return (
        layer_out,
        grad_input,
        grad_value_first,
        gain_sum[:, 0],
        grad_query,
        grad_key,
        grad_value,
        grad_output,
        gain_sum[:, 1],
        grad_gate,
        grad_up,
        grad_down.T,
    )


def solution(mesh):
    tokens, split = P(BOTH, None), P("dp", "tensor")
    across = P("tensor", "dp")
    return jax.shard_map(
        functools.partial(per_device, mesh.shape["dp"], mesh.shape["tensor"]),
        mesh=mesh,
        in_specs=(tokens, split, P("dp", None), tokens, P("dp"), split, split, split, across, P("dp"), split, split, across),
        out_specs=(tokens, tokens, split, P("dp"), split, split, split, across, P("dp"), split, split, across),
        check_vma=False,
    )
```

```python
import functools

import jax
import jax.numpy as jnp
from jax import lax
from jax.experimental import pallas as pl
from jax.experimental.pallas import tpu as pltpu
from jax.experimental.layout import Layout, with_layout_constraint
from jax.sharding import PartitionSpec as P

HEAD = 64
PIECE = 128
NEG = -1e30
BLK = 256
F32 = jnp.float32
BF16 = jnp.bfloat16


def dot_nt(a, b, precision=None):
    return lax.dot_general(a, b, (((1,), (1,)), ((), ())), precision=precision, preferred_element_type=F32)


def dot_nn(a, b):
    return jnp.dot(a, b, preferred_element_type=F32)


def bias_tile(starts_ref, first_key, first_query):
    place = lax.broadcasted_iota(jnp.int32, (BLK, BLK), 0)
    low = starts_ref[...] - first_key
    high = lax.broadcasted_iota(jnp.int32, (1, BLK), 1) + (first_query - first_key)
    return jnp.where((place >= low) & (place <= high), 0.0, NEG)


def forward_kernel(heads, first_ref, starts_ref, q_ref, k_ref, vt_ref, out_ref, lse_ref, masked_q, bias_ref, top_ref, total_ref, acc_ref):
    step = pl.program_id(0)
    lane = lax.broadcasted_iota(jnp.int32, (BLK, 128), 1)
    for head in range(heads):
        pair = pl.ds((head // 2) * 128, 128)
        block = q_ref[:, pair]
        keep = (lane < 64) if head % 2 == 0 else (lane >= 64)
        masked_q[head] = jnp.where(keep, block, jnp.zeros_like(block))
    top_ref[...] = jnp.full_like(top_ref, NEG)
    total_ref[...] = jnp.zeros_like(total_ref)
    acc_ref[...] = jnp.zeros_like(acc_ref)

    def chunk(c, carry):
        base = pl.multiple_of(c * BLK, BLK)
        bias_ref[...] = bias_tile(starts_ref, base, step * BLK)
        for head in range(heads):
            keys = k_ref[pl.ds(base, BLK), pl.ds((head // 2) * 128, 128)]
            scores = dot_nt(keys, masked_q[head]) + bias_ref[...]
            old = top_ref[head : head + 1, :]
            new = jnp.maximum(old, jnp.max(scores, axis=0, keepdims=True))
            probs = jnp.exp(scores - new)
            shrink = jnp.exp(old - new)
            top_ref[head : head + 1, :] = new
            total_ref[head : head + 1, :] = total_ref[head : head + 1, :] * shrink + jnp.sum(probs, axis=0, keepdims=True)
            rows = slice(head * 64, head * 64 + 64)
            part = dot_nn(vt_ref[rows, pl.ds(base, BLK)], probs.astype(BF16))
            acc_ref[rows, :] = acc_ref[rows, :] * shrink + part
        return carry

    lax.fori_loop(first_ref[step], step + 1, chunk, 0)
    for head in range(heads):
        rows = slice(head * 64, head * 64 + 64)
        acc_ref[rows, :] = acc_ref[rows, :] / total_ref[head : head + 1, :]
    out_ref[...] = acc_ref[...].T.astype(BF16)
    lse_ref[...] = (top_ref[...] + jnp.log(total_ref[...])).reshape(lse_ref.shape)


def attention_forward(first, starts, q, k, vt):
    length, width = q.shape
    heads = width // HEAD
    return pl.pallas_call(
        functools.partial(forward_kernel, heads),
        grid_spec=pltpu.PrefetchScalarGridSpec(
            num_scalar_prefetch=1,
            grid=(length // BLK,),
            in_specs=[
                pl.BlockSpec((1, BLK), lambda i, f: (0, i)),
                pl.BlockSpec((BLK, width), lambda i, f: (i, 0)),
                pl.BlockSpec((length, width), lambda i, f: (0, 0)),
                pl.BlockSpec((width, length), lambda i, f: (0, 0)),
            ],
            out_specs=[
                pl.BlockSpec((BLK, width), lambda i, f: (i, 0)),
                pl.BlockSpec((heads // 2, 2, BLK), lambda i, f: (0, 0, i)),
            ],
            scratch_shapes=[
                pltpu.VMEM((heads, BLK, 128), BF16),
                pltpu.VMEM((BLK, BLK), F32),
                pltpu.VMEM((heads, BLK), F32),
                pltpu.VMEM((heads, BLK), F32),
                pltpu.VMEM((width, BLK), F32),
            ],
        ),
        out_shape=[
            jax.ShapeDtypeStruct((length, width), BF16),
            jax.ShapeDtypeStruct((heads // 2, 2, length), F32),
        ],
        compiler_params=pltpu.CompilerParams(dimension_semantics=("arbitrary",)),
        name="attention_forward",
    )(first, starts, q, k, vt)


def unrotate_lanes(block, cosine, sine, lane):
    other = jnp.where(lane % 64 < 32, pltpu.roll(block, 96, 1), pltpu.roll(block, 32, 1))
    return block * cosine - other * sine


def backward_kernel(first_ref, starts_ref, q_ref, k_ref, kt_ref, v_ref, do_ref, o_ref, lse_ref, cosine_ref, sine_ref, cost_ref, sint_ref, *refs):
    pre_ref, gv_ref, masked_q, masked_do, bias_ref, delta_ref, dqt_ref, dk_acc, dv_acc = refs[-9:]
    step = pl.program_id(0)
    lane = lax.broadcasted_iota(jnp.int32, (BLK, 128), 1)

    @pl.when(step == 0)
    def _():
        dk_acc[...] = jnp.zeros_like(dk_acc)
        dv_acc[...] = jnp.zeros_like(dv_acc)

    for head in range(2):
        keep = (lane < 64) if head == 0 else (lane >= 64)
        masked_q[head] = jnp.where(keep, q_ref[...], jnp.zeros_like(q_ref))
        masked_do[head] = jnp.where(keep, do_ref[...], jnp.zeros_like(do_ref))
    product = do_ref[...].astype(F32) * o_ref[...].astype(F32)
    chooser = (lax.broadcasted_iota(jnp.int32, (8, 128), 1) // HEAD == lax.broadcasted_iota(jnp.int32, (8, 128), 0)).astype(F32)
    delta_ref[...] = dot_nt(chooser, product, lax.Precision.HIGHEST)
    dqt_ref[...] = jnp.zeros_like(dqt_ref)
    both_q = masked_q[...].reshape(2 * BLK, 128)
    both_do = masked_do[...].reshape(2 * BLK, 128)

    def chunk(c, carry):
        here = pl.ds(pl.multiple_of(c * BLK, BLK), BLK)
        bias_ref[...] = bias_tile(starts_ref, c * BLK, step * BLK)
        keys = k_ref[here, :]
        vals = v_ref[here, :]
        probs_low, grads_low = [], []
        for head in range(2):
            scores = dot_nt(keys, masked_q[head]) + bias_ref[...]
            probs = jnp.exp(scores - lse_ref[0, head : head + 1, :])
            prob_grad = dot_nt(vals, masked_do[head])
            score_grad = (probs * (prob_grad - delta_ref[head : head + 1, :])).astype(BF16)
            probs_low.append(probs.astype(BF16))
            grads_low.append(score_grad)
            rows = slice(head * 64, head * 64 + 64)
            dqt_ref[rows, :] += dot_nn(kt_ref[rows, here], score_grad)
        dv_acc[here, :] += dot_nn(jnp.concatenate(probs_low, axis=1), both_do)
        dk_acc[here, :] += dot_nn(jnp.concatenate(grads_low, axis=1), both_q)
        return carry

    lax.fori_loop(first_ref[step], step + 1, chunk, 0)
    cost, sint = cost_ref[...] * (HEAD**-0.5), sint_ref[...] * (HEAD**-0.5)
    for head in range(2):
        low = dqt_ref[head * 64 : head * 64 + 32, :]
        high = dqt_ref[head * 64 + 32 : head * 64 + 64, :]
        dqt_ref[head * 64 : head * 64 + 32, :] = low * cost + high * sint
        dqt_ref[head * 64 + 32 : head * 64 + 64, :] = high * cost - low * sint
    pre_ref[pl.ds(pl.multiple_of(step * BLK, BLK), BLK), :128] = dqt_ref[...].T.astype(BF16)

    @pl.when(step == pl.num_programs(0) - 1)
    def _():
        def finish(c, carry):
            here = pl.ds(pl.multiple_of(c * BLK, BLK), BLK)
            pre_ref[here, 128:256] = unrotate_lanes(dk_acc[here, :], cosine_ref[here, :], sine_ref[here, :], lane).astype(BF16)
            half = 0.5 * dv_acc[here, :]
            gv_ref[here, :] = half
            pre_ref[here, 256:] = half.astype(BF16)
            return carry
        lax.fori_loop(0, dk_acc.shape[0] // BLK, finish, 0)


def attention_backward(pair, first, starts, q, k, kt, v, do, o, lse, cosine, sine, cost, sint, values=None):
    length = q.shape[0]
    earlier = [] if values is None else [values]
    rows = pl.BlockSpec((BLK, 128), lambda i, f: (i, pair))
    whole = pl.BlockSpec((length, 128), lambda i, f: (0, pair))
    table = pl.BlockSpec((length, 128), lambda i, f: (0, 0))
    tile = length * BLK * 2 * 3
    return pl.pallas_call(
        backward_kernel,
        grid_spec=pltpu.PrefetchScalarGridSpec(
            num_scalar_prefetch=1,
            grid=(length // BLK,),
            in_specs=[
                pl.BlockSpec((1, BLK), lambda i, f: (0, i)),
                rows, whole,
                pl.BlockSpec((128, length), lambda i, f: (pair, 0)),
                whole, rows, rows,
                pl.BlockSpec((1, 2, BLK), lambda i, f: (pair, 0, i)),
                table, table,
                pl.BlockSpec((32, BLK), lambda i, f: (0, i)),
                pl.BlockSpec((32, BLK), lambda i, f: (0, i)),
            ] + [pl.BlockSpec(memory_space=pl.ANY)] * len(earlier),
            out_specs=[pl.BlockSpec((length, 384), lambda i, f: (0, 0)), whole],
            scratch_shapes=[
                pltpu.VMEM((2, BLK, 128), BF16),
                pltpu.VMEM((2, BLK, 128), BF16),
                pltpu.VMEM((BLK, BLK), F32),
                pltpu.VMEM((8, BLK), F32),
                pltpu.VMEM((128, BLK), F32),
                pltpu.VMEM((length, 128), F32),
                pltpu.VMEM((length, 128), F32),
            ],
        ),
        out_shape=[jax.ShapeDtypeStruct((length, 384), BF16), jax.ShapeDtypeStruct(q.shape, F32)],
        input_output_aliases={13: 1} if earlier else {},
        compiler_params=pltpu.CompilerParams(dimension_semantics=("arbitrary",)),
        cost_estimate=pl.CostEstimate(flops=tile * 128 * 32, bytes_accessed=8 << 20, transcendentals=tile),
        name="attention_backward",
    )(first, starts, q, k, kt, v, do, o, lse, cosine, sine, cost, sint, *earlier)

def feedforward_kernel(width, chained, side_ref, n_ref, nt_ref, y_ref, yt_ref, w_ref, *refs):
    if chained:
        out_in, e_in, *refs = refs
    out_ref, e_ref, keep_ref, send_ref, h_ref, dg_ref, du_ref = refs
    step = pl.program_id(0)
    rows = n_ref.shape[0]
    tile = 1024 if rows % 1024 == 0 else rows

    @pl.when(step == 0)
    def _():
        out_ref[...] = out_in[...] if chained else jnp.zeros_like(out_ref)
        e_ref[...] = e_in[...] if chained else jnp.zeros_like(e_ref)

    def weight(which):
        cols = slice(which * PIECE, which * PIECE + PIECE)
        return jnp.concatenate([w_ref[:, side, :, cols].reshape(width, PIECE) for side in range(2)], axis=1)

    gate_w, up_w, down_w = weight(0), weight(1), weight(2)

    def row_block(i, carry):
        here = pl.ds(pl.multiple_of(i * tile, tile), tile)
        gate = dot_nn(n_ref[here, :], gate_w)
        up = dot_nn(n_ref[here, :], up_w)
        dhid = dot_nn(y_ref[here, :], down_w)
        sig = 1.0 / (1.0 + jnp.exp(-gate))
        silu = gate * sig
        hidden = (silu * up).astype(BF16)
        dgate = (dhid * up * (sig * (1.0 + gate * (1.0 - sig)))).astype(BF16)
        dup = (dhid * silu).astype(BF16)
        h_ref[here, :] = hidden
        dg_ref[here, :] = dgate
        du_ref[here, :] = dup
        out_ref[here, :] += dot_nt(hidden, down_w)
        e_ref[here, :] += dot_nt(dgate, gate_w) + dot_nt(dup, up_w)
        return carry

    lax.fori_loop(0, rows // tile, row_block, 0)
    swapped = side_ref[0] != 0
    for which, (left, right) in enumerate(((nt_ref, dg_ref), (nt_ref, du_ref), (yt_ref, h_ref))):
        cols = slice(which * PIECE, which * PIECE + PIECE)
        grad = dot_nn(left[...], right[...])
        low, high = grad[:, :PIECE], grad[:, PIECE:]
        keep_ref[:, cols] = jnp.where(swapped, high, low).astype(BF16)
        send_ref[:, cols] = jnp.where(swapped, low, high).astype(BF16)


def feedforward(side, n, nt, y, yt, w, start, steps, partial=None):
    rows, width = n.shape
    outer, _, inner, _ = w.shape
    chained = partial is not None
    full = lambda shape: pl.BlockSpec(shape, lambda j, s: (0, 0), pipeline_mode=pl.Buffered(1))
    grads = pl.BlockSpec((width, 3 * PIECE), lambda j, s: (0, j))
    total = pl.BlockSpec((rows, width), lambda j, s: (0, 0))
    grads_shape = jax.ShapeDtypeStruct((width, steps * 3 * PIECE), BF16)
    flops = 18 * rows * width * steps * 2 * PIECE
    return pl.pallas_call(
        functools.partial(feedforward_kernel, width, chained),
        grid_spec=pltpu.PrefetchScalarGridSpec(
            num_scalar_prefetch=1,
            grid=(steps,),
            in_specs=[
                full((rows, width)), full((width, rows)), full((rows, width)), full((width, rows)),
                pl.BlockSpec((outer, 2, inner, 3 * PIECE), lambda j, s: (0, 0, 0, j + start)),
            ] + ([full((rows, width))] * 2 if chained else []),
            out_specs=[total, total, grads, grads],
            scratch_shapes=[pltpu.VMEM((rows, 2 * PIECE), BF16)] * 3,
        ),
        out_shape=[jax.ShapeDtypeStruct((rows, width), F32)] * 2 + [grads_shape] * 2,
        compiler_params=pltpu.CompilerParams(dimension_semantics=("arbitrary",), vmem_limit_bytes=60 << 20),
        cost_estimate=pl.CostEstimate(flops=flops, bytes_accessed=40 << 20, transcendentals=rows * steps * 256),
        name="feedforward",
    )(side, n, nt, y, yt, w, *(partial or ()))


def project_kernel(pairs, sizes, x_ref, *refs):
    weights, refs = refs[: len(sizes)], refs[len(sizes) :]
    first_ref, cosine_ref, sine_ref, q_ref, k_ref, v_ref, kt_ref, vt_ref = refs
    lane = lax.broadcasted_iota(jnp.int32, (x_ref.shape[0], 128), 1)
    first = lane % 64 < 32
    cosine, sine = cosine_ref[...], sine_ref[...]

    def turn(u):
        return u * cosine + jnp.where(first, pltpu.roll(u, 96, 1), pltpu.roll(u, 32, 1)) * sine

    pair = 0
    for ref, size in zip(weights, sizes):
        lin = dot_nn(x_ref[...], ref[:, : size * 384])
        for p in range(size):
            cols = slice(pair * 128, pair * 128 + 128)
            q_ref[:, cols] = (turn(lin[:, p * 384 : p * 384 + 128]) * 0.125).astype(BF16)
            k_ref[:, cols] = turn(lin[:, p * 384 + 128 : p * 384 + 256]).astype(BF16)
            v_ref[:, cols] = (0.5 * lin[:, p * 384 + 256 : p * 384 + 384] + 0.5 * first_ref[:, cols].astype(F32)).astype(BF16)
            pair += 1
    kt_ref[...] = k_ref[...].T
    vt_ref[...] = v_ref[...].T


def project(x, weights, sizes, first, cosine, sine):
    length, depth = x.shape
    width = first.shape[1]
    block = min(256, length)
    rows = lambda n: pl.BlockSpec((block, n), lambda i: (i, 0))
    out = jax.ShapeDtypeStruct((length, width), BF16)
    turned = jax.ShapeDtypeStruct((width, length), BF16)
    across = pl.BlockSpec((width, block), lambda i: (0, i))
    return pl.pallas_call(
        functools.partial(project_kernel, width // 128, sizes),
        grid=(length // block,),
        in_specs=[rows(depth)] + [pl.BlockSpec(w.shape, lambda i: (0, 0), pipeline_mode=pl.Buffered(1)) for w in weights] + [rows(width), rows(128), rows(128)],
        out_specs=[rows(width)] * 3 + [across] * 2,
        out_shape=[out] * 3 + [turned] * 2,
        compiler_params=pltpu.CompilerParams(dimension_semantics=("arbitrary",), vmem_limit_bytes=60 << 20),
        cost_estimate=pl.CostEstimate(flops=6 * length * depth * width, bytes_accessed=20 << 20, transcendentals=0),
        name="project",
    )(x, *weights, first, cosine, sine)


def merge_kernel(count, *refs):
    out_ref, start = refs[-1], 0
    for mine, theirs in zip(refs[:count], refs[count:-1]):
        size = mine.shape[1]
        out_ref[:, start : start + size] = (mine[...].astype(F32) + theirs[...].astype(F32)).astype(BF16)
        start += size
    if start < out_ref.shape[1]:
        out_ref[:, start:] = jnp.zeros_like(out_ref[:, start:])


def merge(mine, theirs, columns):
    rows = mine[0].shape[0]
    spec = lambda n: pl.BlockSpec((256, n), lambda i: (i, 0))
    return pl.pallas_call(
        functools.partial(merge_kernel, len(mine)),
        grid=(rows // 256,),
        in_specs=[spec(a.shape[1]) for a in (*mine, *theirs)],
        out_specs=spec(columns),
        out_shape=jax.ShapeDtypeStruct((rows, columns), BF16),
        compiler_params=pltpu.CompilerParams(dimension_semantics=("arbitrary",)),
        cost_estimate=pl.CostEstimate(flops=rows * columns, bytes_accessed=6 * rows * columns, transcendentals=0),
        name="merge",
    )(*mine, *theirs)


EPS = 1e-06
BOTH = ("dp", "tensor")


def row_major(values):
    return with_layout_constraint(values, Layout(tuple(range(values.ndim))))


def norm_parts(values):
    factor = lax.rsqrt(jnp.mean(values * values, axis=-1, keepdims=True) + EPS)
    return values * factor, factor


def norm_back(incoming, gain, normalized, factor):
    scaled = incoming * gain
    gain_grad = jnp.sum(incoming * normalized, axis=0)
    input_grad = factor * (scaled - normalized * jnp.mean(scaled * normalized, axis=-1, keepdims=True))
    return input_grad, gain_grad


def swap(values):
    return lax.ppermute(values, "tensor", [(0, 1), (1, 0)])


def part(values, index, count, axis):
    size = values.shape[axis] // count
    return lax.dynamic_slice_in_dim(values, index * size, size, axis)


def in_order(mine, theirs, axis):
    first = lax.axis_index("tensor") == 0
    return jnp.concatenate([jnp.where(first, mine, theirs), jnp.where(first, theirs, mine)], axis=axis)


def gather_rows(rows, count):
    if count != 2:
        return lax.all_gather(rows, "tensor", axis=0, tiled=True)
    return in_order(rows, swap(rows), 0)


def heads_to_rows(values, count):
    if count != 2:
        return lax.all_to_all(values, "tensor", split_axis=0, concat_axis=1, tiled=True)
    me = lax.axis_index("tensor")
    theirs = swap(part(values, 1 - me, 2, 0))
    return in_order(part(values, me, 2, 0), theirs, 1)


def rows_to_heads(values, count):
    if count != 2:
        return lax.all_to_all(values, "tensor", split_axis=1, concat_axis=0, tiled=True)
    me = lax.axis_index("tensor")
    theirs = swap(part(values, 1 - me, 2, 1))
    return in_order(part(values, me, 2, 1), theirs, 0)


def scatter_product(left, weights, count):
    def product(rows):
        total, start = 0.0, 0
        for weight in weights:
            size = weight.shape[1]
            total = total + dot_nt(rows[:, start : start + size], weight)
            start += size
        return total

    if count != 2:
        return lax.psum_scatter(product(left), "tensor", scatter_dimension=0, tiled=True)
    me = lax.axis_index("tensor")
    theirs = swap(product(part(left, 1 - me, 2, 0)).astype(BF16))
    return product(part(left, me, 2, 0)) + theirs.astype(F32)


def tensor_sum(values, count):
    if count != 2:
        return lax.psum(values, "tensor")
    return values + swap(values)


def pack_hidden(gate, up, down, blocks):
    rows = gate.shape[0]
    stacked = jnp.stack([w.reshape(rows, blocks, -1) for w in (gate, up, down)], axis=2)
    return stacked.reshape(rows, -1)


def unpack_hidden(packed, blocks):
    rows = packed.shape[0]
    pieces = packed.reshape(rows, blocks, 3, -1)
    return [pieces[:, :, which].reshape(rows, -1) for which in range(3)]


def plane_pairs(bit):
    return [(d, d ^ bit) for d in range(16)]


def ring_pairs(shift):
    return [(d, (d + 4 * shift) % 16) for d in range(16)]


def places():
    me = lax.axis_index("dp")
    return me // 4, me // 2 % 2, me % 2


def pick(values, index, axis):
    return lax.dynamic_index_in_dim(values, index, axis, keepdims=False)


def gather_column(shard):
    z, y, x = places()
    column = jnp.zeros((4,) + shard.shape, shard.dtype)
    for shift in range(4):
        piece = shard if shift == 0 else lax.ppermute(shard, "dp", ring_pairs(shift))
        column = lax.dynamic_update_index_in_dim(column, piece, (z + 4 - shift) % 4, 0)
    return column


def gather_plane(column, cuts):
    z, y, x = places()
    mine, start = [], 0
    for size in cuts:
        mine.append(column[:, :, start : start + size])
        start += size
    orders = ((1, 2), (2, 1))
    mine = lax.optimization_barrier(mine)
    beside = [lax.ppermute(own, "dp", plane_pairs(near)) for own, (near, far) in zip(mine, orders)]
    mine, beside = lax.optimization_barrier((mine, beside))
    across = [
        (lax.ppermute(own, "dp", plane_pairs(far)), lax.ppermute(next_own, "dp", plane_pairs(far)))
        for own, next_own, (near, far) in zip(mine, beside, orders)
    ]
    across = lax.optimization_barrier(across)
    out = []
    for own, next_own, (far_own, far_next), (near, far), size in zip(mine, beside, across, orders, cuts):
        pieces = {0: own, near: next_own, far: far_own, 3: far_next}
        whole = jnp.zeros((4, 2, 2) + own.shape[1:], column.dtype)
        for bits, piece in pieces.items():
            spot = (0, y ^ (bits // 2), x ^ (bits % 2), 0, 0)
            whole = lax.dynamic_update_slice(whole, piece[:, None, None], spot)
        out.append(whole.reshape(-1, size))
    return out


def halve(values, index, axis, bit):
    other = lax.ppermute(pick(values, 1 - index, axis), "dp", plane_pairs(bit))
    return pick(values, index, axis) + other


def plane_sends(values):
    z, y, x = places()
    values = values.reshape(4, 2, 2, -1, values.shape[1])
    half = (values.shape[4] // 128 + 1) // 2 * 128
    one, two = values[..., :half], values[..., half:]
    return pick(one, 1 - x, 2), pick(two, 1 - y, 1), pick(one, x, 2), pick(two, y, 1)


def plane_turn(state):
    z, y, x = places()
    send_one, send_two, keep_one, keep_two = state
    one = keep_one + lax.ppermute(send_one, "dp", plane_pairs(1))
    two = keep_two + lax.ppermute(send_two, "dp", plane_pairs(2))
    return pick(one, 1 - y, 1), pick(two, 1 - x, 1), pick(one, y, 1), pick(two, x, 1)


def column_parts(state):
    send_one, send_two, keep_one, keep_two = state
    one = keep_one + lax.ppermute(send_one, "dp", plane_pairs(2))
    two = keep_two + lax.ppermute(send_two, "dp", plane_pairs(1))
    return jnp.concatenate([one, two], axis=2)


def column_sum(parts, beside=None):
    z, y, x = places()
    arrived = [lax.ppermute(pick(parts, (z + shift) % 4, 0), "dp", ring_pairs(shift)) for shift in range(1, 4)]
    if beside is not None:
        arrived, beside = lax.optimization_barrier((arrived, beside))
    total = pick(parts, z, 0).astype(F32)
    for piece in arrived:
        total = total + piece.astype(F32)
    return total if beside is None else (total, beside)


def gain_tree(grads):
    z, y, x = places()
    grads = grads.reshape(2, 4, 2, 2, -1)
    grads = halve(halve(grads, x, 3, 1), y, 2, 2)
    total = pick(grads, z, 1)
    for shift in range(1, 4):
        total = total + lax.ppermute(pick(grads, (z + shift) % 4, 1), "dp", ring_pairs(shift))
    return total.T


def per_device(dp, count, hidden_in, value_first, segment_ids, out_cotangent, attn_gain, w_query, w_key, w_value, w_output, mlp_gain, w_gate, w_up, w_down):
    rows, depth = hidden_in.shape
    width = w_query.shape[1]
    pairs = width // 128
    length = segment_ids.shape[1]
    slab = w_query.shape[0]
    blocks = w_gate.shape[1] * count // 256
    hidden_columns = 3 * w_gate.shape[1]
    tree = dp == 16 and count == 2

    gains = jnp.pad(jnp.stack([attn_gain, mlp_gain], axis=1), ((0, 0), (0, 126)))
    projections = jnp.stack([w.reshape(slab, pairs, 128) for w in (w_query, w_key, w_value)], axis=2).reshape(slab, -1)
    if tree:
        early = 6 * 384
        sizes = (pairs - pairs // 2, pairs // 2)
        cut = sizes[0] * 384
        first_pack = jnp.concatenate([projections, gains], axis=1)
        first_pack, w_gate, w_up, w_down, w_output = lax.optimization_barrier((first_pack, w_gate, w_up, w_down, w_output))
        hidden_pack = pack_hidden(w_gate, w_up, w_down.T, blocks)
        packs = [jnp.concatenate([hidden_pack[:, :early], w_output.T], axis=1), hidden_pack[:, early:]]
        first_column = gather_column(first_pack)
    else:
        early = hidden_columns
        packs = [jnp.concatenate([pack_hidden(w_gate, w_up, w_down.T, blocks), w_output.T], axis=1)]
        sizes = (pairs,)
        first_all = [lax.all_gather(jnp.concatenate([projections, gains], axis=1), "dp", axis=0, tiled=True)]
    second_all = [lax.all_gather(pack, BOTH, axis=0, tiled=True).reshape(dp, count, slab, -1) for pack in packs]
    doc_ids = segment_ids[0]
    counts = [jnp.sum(doc_ids < d) for d in (1, 2, 3)]
    starts = jnp.where(doc_ids == 1, counts[0], jnp.where(doc_ids == 2, counts[1], jnp.where(doc_ids == 3, counts[2], 0))).astype(jnp.int32)
    first = starts[::BLK] // BLK
    starts = starts[None, :]
    frequency = 10000.0 ** (-(jnp.arange(HEAD // 2, dtype=F32) * 2.0 / HEAD))
    angles = jnp.arange(length, dtype=F32)[:, None] * frequency[None, :]
    cos, sin = jnp.cos(angles), jnp.sin(angles)
    cosine = jnp.concatenate([cos] * 4, axis=1)
    sine = jnp.concatenate([-sin, sin] * 2, axis=1)
    cost, sint = cos.T, sin.T

    residual = hidden_in.astype(F32)
    flat_one, factor_one = norm_parts(residual)
    if tree:
        first_column, first, starts, cosine, sine, cost, sint, flat_one, factor_one = lax.optimization_barrier(
            (first_column, first, starts, cosine, sine, cost, sint, flat_one, factor_one)
        )
        first_all = gather_plane(first_column, (cut, 3 * width - cut + 128))
        all_gains = first_all[1][:, sizes[1] * 384 :]
    else:
        all_gains = first_all[0][:, 3 * width :]
    gain_one = all_gains[:, 0].astype(F32)
    gain_two = all_gains[:, 1].astype(F32)
    rows_one = row_major(gather_rows(row_major((flat_one * gain_one).astype(BF16)), count))
    query, key, value, key_t, value_t = project(rows_one, first_all, sizes, value_first, cosine, sine)
    attended, log_totals = attention_forward(first, starts, query, key, value_t)
    attended_rows = heads_to_rows(attended, count)
    output_w = second_all[0][:, :, :, early:].transpose(0, 2, 1, 3).reshape(depth, count * width)
    middle = row_major(residual + dot_nt(attended_rows, output_w))

    flat_two, factor_two = norm_parts(middle)
    normed_two = row_major((flat_two * gain_two).astype(BF16))
    if count == 2:
        hidden_w = second_all
    else:
        whole = second_all[0][:, :, :, :hidden_columns].reshape(dp, 2, count // 2, slab, blocks, 3, -1)
        hidden_w = [whole.transpose(1, 0, 3, 4, 5, 2, 6).reshape(1, 2, depth, blocks * 3 * PIECE)]
    side = jnp.full((1,), lax.axis_index("tensor") if tree else 0, jnp.int32)
    partial, keeps, sends = None, [], []
    for w, steps in zip(hidden_w, (6, blocks - 6) if tree else (blocks,)):
        *partial, keep, send = feedforward(side, normed_two, normed_two.T, out_cotangent, out_cotangent.T, w, 0, steps, partial)
        keeps.append(keep)
        sends.append(swap(send) if tree else send)
    branch, normed_two_grad = [row_major(p) for p in partial]
    layer_out = (middle + branch).astype(BF16)
    middle_norm_grad, gain_two_grad = norm_back(normed_two_grad, gain_two, flat_two, factor_two)
    middle_grad = row_major(out_cotangent.astype(F32) + middle_norm_grad)
    branch_grad = row_major(middle_grad.astype(BF16))
    if tree:
        hidden_grads = merge(keeps, sends, hidden_columns + -hidden_columns % 768)
        hidden_grads, branch_grad = lax.optimization_barrier((hidden_grads, branch_grad))
        hidden_sum = lax.psum_scatter(hidden_grads, "dp", scatter_dimension=0, tiled=True).astype(F32)

    attended_grad = rows_to_heads(dot_nn(branch_grad, output_w).astype(BF16), count)
    output_grad = lax.dot_general(branch_grad, attended_rows, (((0,), (0,)), ((), ())), preferred_element_type=F32).astype(BF16)
    if tree:
        me = lax.axis_index("tensor")
        output_grad = row_major(output_grad)
        output_grad = row_major(part(output_grad, me, 2, 1) + swap(part(output_grad, 1 - me, 2, 1)))
    else:
        output_grad = output_grad.reshape(dp, slab, count, width).transpose(0, 2, 1, 3)
        hidden_grads = jnp.stack([keeps[0], sends[0]]).reshape(2, dp, slab, blocks, 3, count // 2, -1).transpose(1, 0, 5, 2, 3, 4, 6)
        second_grads = jnp.concatenate([hidden_grads.reshape(dp, count, slab, -1), output_grad], axis=3)
        second_sum = lax.psum_scatter(second_grads.reshape(dp * count * slab, -1), BOTH, scatter_dimension=0, tiled=True).astype(F32)
        hidden_sum, grad_output = second_sum[:, :hidden_columns], second_sum[:, hidden_columns:].T
    pre, grad_value_first, pair_grads = [], None, []
    for pair in range(pairs):
        pair_pre, grad_value_first = attention_backward(
            pair, first, starts, query, key, key_t, value, attended_grad, attended, log_totals, cosine, sine, cost, sint, grad_value_first
        )
        if tree and pair == 3:
            tree_one, pair_pre = lax.optimization_barrier((column_parts(tree_one), pair_pre))
        pre.append(pair_pre)
        pair_grads.append(row_major(lax.dot_general(rows_one, pair_pre, (((0,), (0,)), ((), ())), preferred_element_type=F32).astype(BF16)))
        if tree and pair == 1:
            tree_one, attended_grad = lax.optimization_barrier((plane_sends(jnp.concatenate([output_grad] + pair_grads, axis=1)), attended_grad))
        if tree and pair == 2:
            tree_one, attended_grad = lax.optimization_barrier((plane_turn(tree_one), attended_grad))
    if tree:
        tree_two, pre = lax.optimization_barrier((plane_sends(jnp.concatenate(pair_grads[2:], axis=1)), pre))
    else:
        projection_grads = jnp.concatenate(pair_grads, axis=1)
    weights = [w[:, : size * 384] for w, size in zip(first_all, sizes)]
    normed_one_grad = row_major(scatter_product(jnp.concatenate(pre, axis=1), weights, count))
    if tree:
        tree_two, tree_one, normed_one_grad = lax.optimization_barrier((plane_turn(tree_two), tree_one, normed_one_grad))
        tree_one = column_sum(tree_one)
    input_norm_grad, gain_one_grad = norm_back(normed_one_grad, gain_one, flat_one, factor_one)
    grad_input = row_major(middle_grad + input_norm_grad)
    gain_grads = jnp.stack([gain_one_grad, gain_two_grad], axis=1)
    hidden_shards = unpack_hidden(hidden_sum[:, :hidden_columns], blocks)
    hidden_shards[2] = hidden_shards[2].T
    if tree:
        gain_grads = gain_grads.T
        tree_two, gain_grads = lax.optimization_barrier((column_parts(tree_two), gain_grads + swap(gain_grads)))
        gain_sum = gain_tree(gain_grads)
        grad_output = tree_one[:, :width].T
        tree_two, hidden_shards = column_sum(tree_two, hidden_shards)
        first_sum = jnp.concatenate([tree_one[:, width:], tree_two], axis=1)
    else:
        gain_grads = jnp.pad(lax.psum(gain_grads, "tensor").astype(BF16), ((0, 0), (0, 126)))
        first_sum = lax.psum_scatter(jnp.concatenate([projection_grads, gain_grads], axis=1), "dp", scatter_dimension=0, tiled=True).astype(F32)
        gain_sum = first_sum[:, 3 * width : 3 * width + 2]
        first_sum = first_sum[:, : 3 * width]
    grad_gate, grad_up, grad_down = hidden_shards
    grad_query, grad_key, grad_value = unpack_hidden(first_sum, pairs)
    return (
        layer_out,
        grad_input,
        grad_value_first,
        gain_sum[:, 0],
        grad_query,
        grad_key,
        grad_value,
        grad_output,
        gain_sum[:, 1],
        grad_gate,
        grad_up,
        grad_down,
    )


def solution(mesh):
    tokens, split = P(BOTH, None), P("dp", "tensor")
    across = P("tensor", "dp")
    return jax.shard_map(
        functools.partial(per_device, mesh.shape["dp"], mesh.shape["tensor"]),
        mesh=mesh,
        in_specs=(tokens, split, P("dp", None), tokens, P("dp"), split, split, split, across, P("dp"), split, split, across),
        out_specs=(tokens, tokens, split, P("dp"), split, split, split, across, P("dp"), split, split, across),
        check_vma=False,
    )
```

```python
import functools

import jax
import jax.numpy as jnp
from jax import lax
from jax.experimental import pallas as pl
from jax.experimental.pallas import tpu as pltpu
from jax.experimental.layout import Layout, with_layout_constraint
from jax.sharding import PartitionSpec as P

HEAD = 64
PIECE = 128
NEG = -1e30
BLK = 256
F32 = jnp.float32
BF16 = jnp.bfloat16


def dot_nt(a, b, precision=None):
    return lax.dot_general(a, b, (((1,), (1,)), ((), ())), precision=precision, preferred_element_type=F32)


def dot_nn(a, b):
    return jnp.dot(a, b, preferred_element_type=F32)


def bias_tile(starts_ref, first_key, first_query):
    place = lax.broadcasted_iota(jnp.int32, (BLK, BLK), 0)
    low = starts_ref[...] - first_key
    high = lax.broadcasted_iota(jnp.int32, (1, BLK), 1) + (first_query - first_key)
    return jnp.where((place >= low) & (place <= high), 0.0, NEG)


def forward_kernel(heads, first_ref, starts_ref, q_ref, k_ref, vt_ref, out_ref, lse_ref, masked_q, bias_ref, top_ref, total_ref, acc_ref):
    step = pl.program_id(0)
    lane = lax.broadcasted_iota(jnp.int32, (BLK, 128), 1)
    for head in range(heads):
        pair = pl.ds((head // 2) * 128, 128)
        block = q_ref[:, pair]
        keep = (lane < 64) if head % 2 == 0 else (lane >= 64)
        masked_q[head] = jnp.where(keep, block, jnp.zeros_like(block))
    top_ref[...] = jnp.full_like(top_ref, NEG)
    total_ref[...] = jnp.zeros_like(total_ref)
    acc_ref[...] = jnp.zeros_like(acc_ref)

    def chunk(c, carry):
        base = pl.multiple_of(c * BLK, BLK)
        bias_ref[...] = bias_tile(starts_ref, base, step * BLK)
        for head in range(heads):
            keys = k_ref[pl.ds(base, BLK), pl.ds((head // 2) * 128, 128)]
            scores = dot_nt(keys, masked_q[head]) + bias_ref[...]
            old = top_ref[head : head + 1, :]
            new = jnp.maximum(old, jnp.max(scores, axis=0, keepdims=True))
            probs = jnp.exp(scores - new)
            shrink = jnp.exp(old - new)
            top_ref[head : head + 1, :] = new
            total_ref[head : head + 1, :] = total_ref[head : head + 1, :] * shrink + jnp.sum(probs, axis=0, keepdims=True)
            rows = slice(head * 64, head * 64 + 64)
            part = dot_nn(vt_ref[rows, pl.ds(base, BLK)], probs.astype(BF16))
            acc_ref[rows, :] = acc_ref[rows, :] * shrink + part
        return carry

    lax.fori_loop(first_ref[step], step + 1, chunk, 0)
    for head in range(heads):
        rows = slice(head * 64, head * 64 + 64)
        acc_ref[rows, :] = acc_ref[rows, :] / total_ref[head : head + 1, :]
    out_ref[...] = acc_ref[...].T.astype(BF16)
    lse_ref[...] = (top_ref[...] + jnp.log(total_ref[...])).reshape(lse_ref.shape)


def attention_forward(first, starts, q, k, vt):
    length, width = q.shape
    heads = width // HEAD
    return pl.pallas_call(
        functools.partial(forward_kernel, heads),
        grid_spec=pltpu.PrefetchScalarGridSpec(
            num_scalar_prefetch=1,
            grid=(length // BLK,),
            in_specs=[
                pl.BlockSpec((1, BLK), lambda i, f: (0, i)),
                pl.BlockSpec((BLK, width), lambda i, f: (i, 0)),
                pl.BlockSpec((length, width), lambda i, f: (0, 0)),
                pl.BlockSpec((width, length), lambda i, f: (0, 0)),
            ],
            out_specs=[
                pl.BlockSpec((BLK, width), lambda i, f: (i, 0)),
                pl.BlockSpec((heads // 2, 2, BLK), lambda i, f: (0, 0, i)),
            ],
            scratch_shapes=[
                pltpu.VMEM((heads, BLK, 128), BF16),
                pltpu.VMEM((BLK, BLK), F32),
                pltpu.VMEM((heads, BLK), F32),
                pltpu.VMEM((heads, BLK), F32),
                pltpu.VMEM((width, BLK), F32),
            ],
        ),
        out_shape=[
            jax.ShapeDtypeStruct((length, width), BF16),
            jax.ShapeDtypeStruct((heads // 2, 2, length), F32),
        ],
        compiler_params=pltpu.CompilerParams(dimension_semantics=("arbitrary",)),
        name="attention_forward",
    )(first, starts, q, k, vt)


def unrotate_lanes(block, cosine, sine, lane):
    other = jnp.where(lane % 64 < 32, pltpu.roll(block, 96, 1), pltpu.roll(block, 32, 1))
    return block * cosine - other * sine


def backward_kernel(first_ref, starts_ref, q_ref, k_ref, kt_ref, v_ref, do_ref, o_ref, lse_ref, cosine_ref, sine_ref, cost_ref, sint_ref, *refs):
    pre_ref, gv_ref, masked_q, masked_do, bias_ref, delta_ref, dqt_ref, dk_acc, dv_acc = refs[-9:]
    step = pl.program_id(0)
    lane = lax.broadcasted_iota(jnp.int32, (BLK, 128), 1)

    @pl.when(step == 0)
    def _():
        dk_acc[...] = jnp.zeros_like(dk_acc)
        dv_acc[...] = jnp.zeros_like(dv_acc)

    for head in range(2):
        keep = (lane < 64) if head == 0 else (lane >= 64)
        masked_q[head] = jnp.where(keep, q_ref[...], jnp.zeros_like(q_ref))
        masked_do[head] = jnp.where(keep, do_ref[...], jnp.zeros_like(do_ref))
    product = do_ref[...].astype(F32) * o_ref[...].astype(F32)
    chooser = (lax.broadcasted_iota(jnp.int32, (8, 128), 1) // HEAD == lax.broadcasted_iota(jnp.int32, (8, 128), 0)).astype(F32)
    delta_ref[...] = dot_nt(chooser, product, lax.Precision.HIGHEST)
    dqt_ref[...] = jnp.zeros_like(dqt_ref)
    both_q = masked_q[...].reshape(2 * BLK, 128)
    both_do = masked_do[...].reshape(2 * BLK, 128)

    def chunk(c, carry):
        here = pl.ds(pl.multiple_of(c * BLK, BLK), BLK)
        bias_ref[...] = bias_tile(starts_ref, c * BLK, step * BLK)
        keys = k_ref[here, :]
        vals = v_ref[here, :]
        probs_low, grads_low = [], []
        for head in range(2):
            scores = dot_nt(keys, masked_q[head]) + bias_ref[...]
            probs = jnp.exp(scores - lse_ref[0, head : head + 1, :])
            prob_grad = dot_nt(vals, masked_do[head])
            score_grad = (probs * (prob_grad - delta_ref[head : head + 1, :])).astype(BF16)
            probs_low.append(probs.astype(BF16))
            grads_low.append(score_grad)
            rows = slice(head * 64, head * 64 + 64)
            dqt_ref[rows, :] += dot_nn(kt_ref[rows, here], score_grad)
        dv_acc[here, :] += dot_nn(jnp.concatenate(probs_low, axis=1), both_do)
        dk_acc[here, :] += dot_nn(jnp.concatenate(grads_low, axis=1), both_q)
        return carry

    lax.fori_loop(first_ref[step], step + 1, chunk, 0)
    cost, sint = cost_ref[...] * (HEAD**-0.5), sint_ref[...] * (HEAD**-0.5)
    for head in range(2):
        low = dqt_ref[head * 64 : head * 64 + 32, :]
        high = dqt_ref[head * 64 + 32 : head * 64 + 64, :]
        dqt_ref[head * 64 : head * 64 + 32, :] = low * cost + high * sint
        dqt_ref[head * 64 + 32 : head * 64 + 64, :] = high * cost - low * sint
    pre_ref[pl.ds(pl.multiple_of(step * BLK, BLK), BLK), :128] = dqt_ref[...].T.astype(BF16)

    @pl.when(step == pl.num_programs(0) - 1)
    def _():
        def finish(c, carry):
            here = pl.ds(pl.multiple_of(c * BLK, BLK), BLK)
            pre_ref[here, 128:256] = unrotate_lanes(dk_acc[here, :], cosine_ref[here, :], sine_ref[here, :], lane).astype(BF16)
            half = 0.5 * dv_acc[here, :]
            gv_ref[here, :] = half
            pre_ref[here, 256:] = half.astype(BF16)
            return carry
        lax.fori_loop(0, dk_acc.shape[0] // BLK, finish, 0)


def attention_backward(pair, first, starts, q, k, kt, v, do, o, lse, cosine, sine, cost, sint, values=None):
    length = q.shape[0]
    earlier = [] if values is None else [values]
    rows = pl.BlockSpec((BLK, 128), lambda i, f: (i, pair))
    whole = pl.BlockSpec((length, 128), lambda i, f: (0, pair))
    table = pl.BlockSpec((length, 128), lambda i, f: (0, 0))
    tile = length * BLK * 2 * 3
    return pl.pallas_call(
        backward_kernel,
        grid_spec=pltpu.PrefetchScalarGridSpec(
            num_scalar_prefetch=1,
            grid=(length // BLK,),
            in_specs=[
                pl.BlockSpec((1, BLK), lambda i, f: (0, i)),
                rows, whole,
                pl.BlockSpec((128, length), lambda i, f: (pair, 0)),
                whole, rows, rows,
                pl.BlockSpec((1, 2, BLK), lambda i, f: (pair, 0, i)),
                table, table,
                pl.BlockSpec((32, BLK), lambda i, f: (0, i)),
                pl.BlockSpec((32, BLK), lambda i, f: (0, i)),
            ] + [pl.BlockSpec(memory_space=pl.ANY)] * len(earlier),
            out_specs=[pl.BlockSpec((length, 384), lambda i, f: (0, 0)), whole],
            scratch_shapes=[
                pltpu.VMEM((2, BLK, 128), BF16),
                pltpu.VMEM((2, BLK, 128), BF16),
                pltpu.VMEM((BLK, BLK), F32),
                pltpu.VMEM((8, BLK), F32),
                pltpu.VMEM((128, BLK), F32),
                pltpu.VMEM((length, 128), F32),
                pltpu.VMEM((length, 128), F32),
            ],
        ),
        out_shape=[jax.ShapeDtypeStruct((length, 384), BF16), jax.ShapeDtypeStruct(q.shape, F32)],
        input_output_aliases={13: 1} if earlier else {},
        compiler_params=pltpu.CompilerParams(dimension_semantics=("arbitrary",)),
        cost_estimate=pl.CostEstimate(flops=tile * 128 * 32, bytes_accessed=8 << 20, transcendentals=tile),
        name="attention_backward",
    )(first, starts, q, k, kt, v, do, o, lse, cosine, sine, cost, sint, *earlier)

def feedforward_kernel(width, chained, side_ref, n_ref, nt_ref, y_ref, yt_ref, w_ref, *refs):
    if chained:
        out_in, e_in, *refs = refs
    out_ref, e_ref, keep_ref, send_ref, h_ref, dg_ref, du_ref = refs
    step = pl.program_id(0)
    rows = n_ref.shape[0]
    tile = 1024 if rows % 1024 == 0 else rows

    @pl.when(step == 0)
    def _():
        out_ref[...] = out_in[...] if chained else jnp.zeros_like(out_ref)
        e_ref[...] = e_in[...] if chained else jnp.zeros_like(e_ref)

    def weight(which):
        cols = slice(which * PIECE, which * PIECE + PIECE)
        return jnp.concatenate([w_ref[:, side, :, cols].reshape(width, PIECE) for side in range(2)], axis=1)

    gate_w, up_w, down_w = weight(0), weight(1), weight(2)

    def row_block(i, carry):
        here = pl.ds(pl.multiple_of(i * tile, tile), tile)
        gate = dot_nn(n_ref[here, :], gate_w)
        up = dot_nn(n_ref[here, :], up_w)
        dhid = dot_nn(y_ref[here, :], down_w)
        sig = 1.0 / (1.0 + jnp.exp(-gate))
        silu = gate * sig
        hidden = (silu * up).astype(BF16)
        dgate = (dhid * up * (sig * (1.0 + gate * (1.0 - sig)))).astype(BF16)
        dup = (dhid * silu).astype(BF16)
        h_ref[here, :] = hidden
        dg_ref[here, :] = dgate
        du_ref[here, :] = dup
        out_ref[here, :] += dot_nt(hidden, down_w)
        e_ref[here, :] += dot_nt(dgate, gate_w) + dot_nt(dup, up_w)
        return carry

    lax.fori_loop(0, rows // tile, row_block, 0)
    swapped = side_ref[0] != 0
    for which, (left, right) in enumerate(((nt_ref, dg_ref), (nt_ref, du_ref), (yt_ref, h_ref))):
        cols = slice(which * PIECE, which * PIECE + PIECE)
        grad = dot_nn(left[...], right[...])
        low, high = grad[:, :PIECE], grad[:, PIECE:]
        keep_ref[:, cols] = jnp.where(swapped, high, low).astype(BF16)
        send_ref[:, cols] = jnp.where(swapped, low, high).astype(BF16)


def feedforward(side, n, nt, y, yt, w, start, steps, partial=None):
    rows, width = n.shape
    outer, _, inner, _ = w.shape
    chained = partial is not None
    full = lambda shape: pl.BlockSpec(shape, lambda j, s: (0, 0), pipeline_mode=pl.Buffered(1))
    grads = pl.BlockSpec((width, 3 * PIECE), lambda j, s: (0, j))
    total = pl.BlockSpec((rows, width), lambda j, s: (0, 0))
    grads_shape = jax.ShapeDtypeStruct((width, steps * 3 * PIECE), BF16)
    flops = 18 * rows * width * steps * 2 * PIECE
    return pl.pallas_call(
        functools.partial(feedforward_kernel, width, chained),
        grid_spec=pltpu.PrefetchScalarGridSpec(
            num_scalar_prefetch=1,
            grid=(steps,),
            in_specs=[
                full((rows, width)), full((width, rows)), full((rows, width)), full((width, rows)),
                pl.BlockSpec((outer, 2, inner, 3 * PIECE), lambda j, s: (0, 0, 0, j + start)),
            ] + ([full((rows, width))] * 2 if chained else []),
            out_specs=[total, total, grads, grads],
            scratch_shapes=[pltpu.VMEM((rows, 2 * PIECE), BF16)] * 3,
        ),
        out_shape=[jax.ShapeDtypeStruct((rows, width), F32)] * 2 + [grads_shape] * 2,
        compiler_params=pltpu.CompilerParams(dimension_semantics=("arbitrary",), vmem_limit_bytes=60 << 20),
        cost_estimate=pl.CostEstimate(flops=flops, bytes_accessed=40 << 20, transcendentals=rows * steps * 256),
        name="feedforward",
    )(side, n, nt, y, yt, w, *(partial or ()))


def project_kernel(pairs, sizes, x_ref, *refs):
    weights, refs = refs[: len(sizes)], refs[len(sizes) :]
    first_ref, cosine_ref, sine_ref, q_ref, k_ref, v_ref, kt_ref, vt_ref = refs
    lane = lax.broadcasted_iota(jnp.int32, (x_ref.shape[0], 128), 1)
    first = lane % 64 < 32
    cosine, sine = cosine_ref[...], sine_ref[...]

    def turn(u):
        return u * cosine + jnp.where(first, pltpu.roll(u, 96, 1), pltpu.roll(u, 32, 1)) * sine

    pair = 0
    for ref, size in zip(weights, sizes):
        lin = dot_nn(x_ref[...], ref[:, : size * 384])
        for p in range(size):
            cols = slice(pair * 128, pair * 128 + 128)
            q_ref[:, cols] = (turn(lin[:, p * 384 : p * 384 + 128]) * 0.125).astype(BF16)
            k_ref[:, cols] = turn(lin[:, p * 384 + 128 : p * 384 + 256]).astype(BF16)
            v_ref[:, cols] = (0.5 * lin[:, p * 384 + 256 : p * 384 + 384] + 0.5 * first_ref[:, cols].astype(F32)).astype(BF16)
            pair += 1
    kt_ref[...] = k_ref[...].T
    vt_ref[...] = v_ref[...].T


def project(x, weights, sizes, first, cosine, sine):
    length, depth = x.shape
    width = first.shape[1]
    block = min(512, length)
    rows = lambda n: pl.BlockSpec((block, n), lambda i: (i, 0))
    out = jax.ShapeDtypeStruct((length, width), BF16)
    turned = jax.ShapeDtypeStruct((width, length), BF16)
    across = pl.BlockSpec((width, block), lambda i: (0, i))
    return pl.pallas_call(
        functools.partial(project_kernel, width // 128, sizes),
        grid=(length // block,),
        in_specs=[rows(depth)] + [pl.BlockSpec(w.shape, lambda i: (0, 0), pipeline_mode=pl.Buffered(1)) for w in weights] + [rows(width), rows(128), rows(128)],
        out_specs=[rows(width)] * 3 + [across] * 2,
        out_shape=[out] * 3 + [turned] * 2,
        compiler_params=pltpu.CompilerParams(dimension_semantics=("arbitrary",), vmem_limit_bytes=60 << 20),
        cost_estimate=pl.CostEstimate(flops=6 * length * depth * width, bytes_accessed=20 << 20, transcendentals=0),
        name="project",
    )(x, *weights, first, cosine, sine)


def merge_kernel(count, *refs):
    out_ref, start = refs[-1], 0
    for mine, theirs in zip(refs[:count], refs[count:-1]):
        size = mine.shape[1]
        out_ref[:, start : start + size] = (mine[...].astype(F32) + theirs[...].astype(F32)).astype(BF16)
        start += size
    if start < out_ref.shape[1]:
        out_ref[:, start:] = jnp.zeros_like(out_ref[:, start:])


def merge(mine, theirs, columns):
    rows = mine[0].shape[0]
    spec = lambda n: pl.BlockSpec((256, n), lambda i: (i, 0))
    return pl.pallas_call(
        functools.partial(merge_kernel, len(mine)),
        grid=(rows // 256,),
        in_specs=[spec(a.shape[1]) for a in (*mine, *theirs)],
        out_specs=spec(columns),
        out_shape=jax.ShapeDtypeStruct((rows, columns), BF16),
        compiler_params=pltpu.CompilerParams(dimension_semantics=("arbitrary",)),
        cost_estimate=pl.CostEstimate(flops=rows * columns, bytes_accessed=6 * rows * columns, transcendentals=0),
        name="merge",
    )(*mine, *theirs)


EPS = 1e-06
BOTH = ("dp", "tensor")


def row_major(values):
    return with_layout_constraint(values, Layout(tuple(range(values.ndim))))


def norm_parts(values):
    factor = lax.rsqrt(jnp.mean(values * values, axis=-1, keepdims=True) + EPS)
    return values * factor, factor


def norm_back(incoming, gain, normalized, factor):
    scaled = incoming * gain
    gain_grad = jnp.sum(incoming * normalized, axis=0)
    input_grad = factor * (scaled - normalized * jnp.mean(scaled * normalized, axis=-1, keepdims=True))
    return input_grad, gain_grad


def swap(values):
    return lax.ppermute(values, "tensor", [(0, 1), (1, 0)])


def part(values, index, count, axis):
    size = values.shape[axis] // count
    return lax.dynamic_slice_in_dim(values, index * size, size, axis)


def in_order(mine, theirs, axis):
    first = lax.axis_index("tensor") == 0
    return jnp.concatenate([jnp.where(first, mine, theirs), jnp.where(first, theirs, mine)], axis=axis)


def gather_rows(rows, count):
    if count != 2:
        return lax.all_gather(rows, "tensor", axis=0, tiled=True)
    return in_order(rows, swap(rows), 0)


def heads_to_rows(values, count):
    if count != 2:
        return lax.all_to_all(values, "tensor", split_axis=0, concat_axis=1, tiled=True)
    me = lax.axis_index("tensor")
    theirs = swap(part(values, 1 - me, 2, 0))
    return in_order(part(values, me, 2, 0), theirs, 1)


def rows_to_heads(values, count):
    if count != 2:
        return lax.all_to_all(values, "tensor", split_axis=1, concat_axis=0, tiled=True)
    me = lax.axis_index("tensor")
    theirs = swap(part(values, 1 - me, 2, 1))
    return in_order(part(values, me, 2, 1), theirs, 0)


def scatter_product(left, weights, count):
    def product(rows):
        total, start = 0.0, 0
        for weight in weights:
            size = weight.shape[1]
            total = total + dot_nt(rows[:, start : start + size], weight)
            start += size
        return total

    if count != 2:
        return lax.psum_scatter(product(left), "tensor", scatter_dimension=0, tiled=True)
    me = lax.axis_index("tensor")
    theirs = swap(product(part(left, 1 - me, 2, 0)).astype(BF16))
    return product(part(left, me, 2, 0)) + theirs.astype(F32)


def tensor_sum(values, count):
    if count != 2:
        return lax.psum(values, "tensor")
    return values + swap(values)


def pack_hidden(gate, up, down, blocks):
    rows = gate.shape[0]
    stacked = jnp.stack([w.reshape(rows, blocks, -1) for w in (gate, up, down)], axis=2)
    return stacked.reshape(rows, -1)


def unpack_hidden(packed, blocks):
    rows = packed.shape[0]
    pieces = packed.reshape(rows, blocks, 3, -1)
    return [pieces[:, :, which].reshape(rows, -1) for which in range(3)]


def plane_pairs(bit):
    return [(d, d ^ bit) for d in range(16)]


def ring_pairs(shift):
    return [(d, (d + 4 * shift) % 16) for d in range(16)]


def places():
    me = lax.axis_index("dp")
    return me // 4, me // 2 % 2, me % 2


def pick(values, index, axis):
    return lax.dynamic_index_in_dim(values, index, axis, keepdims=False)


def gather_column(shard):
    z, y, x = places()
    column = jnp.zeros((4,) + shard.shape, shard.dtype)
    for shift in range(4):
        piece = shard if shift == 0 else lax.ppermute(shard, "dp", ring_pairs(shift))
        column = lax.dynamic_update_index_in_dim(column, piece, (z + 4 - shift) % 4, 0)
    return column


def gather_plane(column, cuts):
    z, y, x = places()
    mine, start = [], 0
    for size in cuts:
        mine.append(column[:, :, start : start + size])
        start += size
    orders = ((1, 2), (2, 1))
    mine = lax.optimization_barrier(mine)
    beside = [lax.ppermute(own, "dp", plane_pairs(near)) for own, (near, far) in zip(mine, orders)]
    mine, beside = lax.optimization_barrier((mine, beside))
    across = [
        (lax.ppermute(own, "dp", plane_pairs(far)), lax.ppermute(next_own, "dp", plane_pairs(far)))
        for own, next_own, (near, far) in zip(mine, beside, orders)
    ]
    across = lax.optimization_barrier(across)
    out = []
    for own, next_own, (far_own, far_next), (near, far), size in zip(mine, beside, across, orders, cuts):
        pieces = {0: own, near: next_own, far: far_own, 3: far_next}
        whole = jnp.zeros((4, 2, 2) + own.shape[1:], column.dtype)
        for bits, piece in pieces.items():
            spot = (0, y ^ (bits // 2), x ^ (bits % 2), 0, 0)
            whole = lax.dynamic_update_slice(whole, piece[:, None, None], spot)
        out.append(whole.reshape(-1, size))
    return out


def halve(values, index, axis, bit):
    other = lax.ppermute(pick(values, 1 - index, axis), "dp", plane_pairs(bit))
    return pick(values, index, axis) + other


def plane_sends(values):
    z, y, x = places()
    values = values.reshape(4, 2, 2, -1, values.shape[1])
    half = (values.shape[4] // 128 + 1) // 2 * 128
    one, two = values[..., :half], values[..., half:]
    return pick(one, 1 - x, 2), pick(two, 1 - y, 1), pick(one, x, 2), pick(two, y, 1)


def plane_turn(state):
    z, y, x = places()
    send_one, send_two, keep_one, keep_two = state
    one = keep_one + lax.ppermute(send_one, "dp", plane_pairs(1))
    two = keep_two + lax.ppermute(send_two, "dp", plane_pairs(2))
    return pick(one, 1 - y, 1), pick(two, 1 - x, 1), pick(one, y, 1), pick(two, x, 1)


def column_parts(state):
    send_one, send_two, keep_one, keep_two = state
    one = keep_one + lax.ppermute(send_one, "dp", plane_pairs(2))
    two = keep_two + lax.ppermute(send_two, "dp", plane_pairs(1))
    return jnp.concatenate([one, two], axis=2)


def column_sum(parts, beside=None):
    z, y, x = places()
    arrived = [lax.ppermute(pick(parts, (z + shift) % 4, 0), "dp", ring_pairs(shift)) for shift in range(1, 4)]
    if beside is not None:
        arrived, beside = lax.optimization_barrier((arrived, beside))
    total = pick(parts, z, 0).astype(F32)
    for piece in arrived:
        total = total + piece.astype(F32)
    return total if beside is None else (total, beside)


def gain_tree(grads):
    z, y, x = places()
    grads = grads.reshape(2, 4, 2, 2, -1)
    grads = halve(halve(grads, x, 3, 1), y, 2, 2)
    total = pick(grads, z, 1)
    for shift in range(1, 4):
        total = total + lax.ppermute(pick(grads, (z + shift) % 4, 1), "dp", ring_pairs(shift))
    return total.T


def per_device(dp, count, hidden_in, value_first, segment_ids, out_cotangent, attn_gain, w_query, w_key, w_value, w_output, mlp_gain, w_gate, w_up, w_down):
    rows, depth = hidden_in.shape
    width = w_query.shape[1]
    pairs = width // 128
    length = segment_ids.shape[1]
    slab = w_query.shape[0]
    blocks = w_gate.shape[1] * count // 256
    hidden_columns = 3 * w_gate.shape[1]
    tree = dp == 16 and count == 2

    gains = jnp.pad(jnp.stack([attn_gain, mlp_gain], axis=1), ((0, 0), (0, 126)))
    projections = jnp.stack([w.reshape(slab, pairs, 128) for w in (w_query, w_key, w_value)], axis=2).reshape(slab, -1)
    if tree:
        early = 6 * 384
        sizes = (pairs - pairs // 2, pairs // 2)
        cut = sizes[0] * 384
        first_pack = jnp.concatenate([projections, gains], axis=1)
        first_pack, w_gate, w_up, w_down, w_output = lax.optimization_barrier((first_pack, w_gate, w_up, w_down, w_output))
        hidden_pack = pack_hidden(w_gate, w_up, w_down.T, blocks)
        packs = [jnp.concatenate([hidden_pack[:, :early], w_output.T], axis=1), hidden_pack[:, early:]]
        first_column = gather_column(first_pack)
    else:
        early = hidden_columns
        packs = [jnp.concatenate([pack_hidden(w_gate, w_up, w_down.T, blocks), w_output.T], axis=1)]
        sizes = (pairs,)
        first_all = [lax.all_gather(jnp.concatenate([projections, gains], axis=1), "dp", axis=0, tiled=True)]
    second_all = [lax.all_gather(pack, BOTH, axis=0, tiled=True).reshape(dp, count, slab, -1) for pack in packs]
    doc_ids = segment_ids[0]
    counts = [jnp.sum(doc_ids < d) for d in (1, 2, 3)]
    starts = jnp.where(doc_ids == 1, counts[0], jnp.where(doc_ids == 2, counts[1], jnp.where(doc_ids == 3, counts[2], 0))).astype(jnp.int32)
    first = starts[::BLK] // BLK
    starts = starts[None, :]
    frequency = 10000.0 ** (-(jnp.arange(HEAD // 2, dtype=F32) * 2.0 / HEAD))
    angles = jnp.arange(length, dtype=F32)[:, None] * frequency[None, :]
    cos, sin = jnp.cos(angles), jnp.sin(angles)
    cosine = jnp.concatenate([cos] * 4, axis=1)
    sine = jnp.concatenate([-sin, sin] * 2, axis=1)
    cost, sint = cos.T, sin.T

    residual = hidden_in.astype(F32)
    flat_one, factor_one = norm_parts(residual)
    if tree:
        first_column, first, starts, cosine, sine, cost, sint, flat_one, factor_one = lax.optimization_barrier(
            (first_column, first, starts, cosine, sine, cost, sint, flat_one, factor_one)
        )
        first_all = gather_plane(first_column, (cut, 3 * width - cut + 128))
        all_gains = first_all[1][:, sizes[1] * 384 :]
    else:
        all_gains = first_all[0][:, 3 * width :]
    gain_one = all_gains[:, 0].astype(F32)
    gain_two = all_gains[:, 1].astype(F32)
    rows_one = row_major(gather_rows(row_major((flat_one * gain_one).astype(BF16)), count))
    query, key, value, key_t, value_t = project(rows_one, first_all, sizes, value_first, cosine, sine)
    attended, log_totals = attention_forward(first, starts, query, key, value_t)
    attended_rows = heads_to_rows(attended, count)
    output_w = second_all[0][:, :, :, early:].transpose(0, 2, 1, 3).reshape(depth, count * width)
    middle = row_major(residual + dot_nt(attended_rows, output_w))

    flat_two, factor_two = norm_parts(middle)
    normed_two = row_major((flat_two * gain_two).astype(BF16))
    if count == 2:
        hidden_w = second_all
    else:
        whole = second_all[0][:, :, :, :hidden_columns].reshape(dp, 2, count // 2, slab, blocks, 3, -1)
        hidden_w = [whole.transpose(1, 0, 3, 4, 5, 2, 6).reshape(1, 2, depth, blocks * 3 * PIECE)]
    side = jnp.full((1,), lax.axis_index("tensor") if tree else 0, jnp.int32)
    partial, keeps, sends = None, [], []
    for w, steps in zip(hidden_w, (6, blocks - 6) if tree else (blocks,)):
        *partial, keep, send = feedforward(side, normed_two, normed_two.T, out_cotangent, out_cotangent.T, w, 0, steps, partial)
        keeps.append(keep)
        sends.append(swap(send) if tree else send)
    branch, normed_two_grad = [row_major(p) for p in partial]
    layer_out = (middle + branch).astype(BF16)
    middle_norm_grad, gain_two_grad = norm_back(normed_two_grad, gain_two, flat_two, factor_two)
    middle_grad = row_major(out_cotangent.astype(F32) + middle_norm_grad)
    branch_grad = row_major(middle_grad.astype(BF16))
    if tree:
        hidden_grads = merge(keeps, sends, hidden_columns + -hidden_columns % 768)
        hidden_grads, branch_grad = lax.optimization_barrier((hidden_grads, branch_grad))
        hidden_sum = lax.psum_scatter(hidden_grads, "dp", scatter_dimension=0, tiled=True).astype(F32)

    attended_grad = rows_to_heads(dot_nn(branch_grad, output_w).astype(BF16), count)
    output_grad = lax.dot_general(branch_grad, attended_rows, (((0,), (0,)), ((), ())), preferred_element_type=F32).astype(BF16)
    if tree:
        me = lax.axis_index("tensor")
        output_grad = row_major(output_grad)
        output_grad = row_major(part(output_grad, me, 2, 1) + swap(part(output_grad, 1 - me, 2, 1)))
    else:
        output_grad = output_grad.reshape(dp, slab, count, width).transpose(0, 2, 1, 3)
        hidden_grads = jnp.stack([keeps[0], sends[0]]).reshape(2, dp, slab, blocks, 3, count // 2, -1).transpose(1, 0, 5, 2, 3, 4, 6)
        second_grads = jnp.concatenate([hidden_grads.reshape(dp, count, slab, -1), output_grad], axis=3)
        second_sum = lax.psum_scatter(second_grads.reshape(dp * count * slab, -1), BOTH, scatter_dimension=0, tiled=True).astype(F32)
        hidden_sum, grad_output = second_sum[:, :hidden_columns], second_sum[:, hidden_columns:].T
    pre, grad_value_first, pair_grads = [], None, []
    for pair in range(pairs):
        pair_pre, grad_value_first = attention_backward(
            pair, first, starts, query, key, key_t, value, attended_grad, attended, log_totals, cosine, sine, cost, sint, grad_value_first
        )
        if tree and pair == 3:
            tree_one, pair_pre = lax.optimization_barrier((column_parts(tree_one), pair_pre))
        pre.append(pair_pre)
        pair_grads.append(row_major(lax.dot_general(rows_one, pair_pre, (((0,), (0,)), ((), ())), preferred_element_type=F32).astype(BF16)))
        if tree and pair == 1:
            tree_one, attended_grad = lax.optimization_barrier((plane_sends(jnp.concatenate([output_grad] + pair_grads, axis=1)), attended_grad))
        if tree and pair == 2:
            tree_one, attended_grad = lax.optimization_barrier((plane_turn(tree_one), attended_grad))
    if tree:
        tree_two, pre = lax.optimization_barrier((plane_sends(jnp.concatenate(pair_grads[2:], axis=1)), pre))
    else:
        projection_grads = jnp.concatenate(pair_grads, axis=1)
    weights = [w[:, : size * 384] for w, size in zip(first_all, sizes)]
    normed_one_grad = row_major(scatter_product(jnp.concatenate(pre, axis=1), weights, count))
    if tree:
        tree_two, tree_one, normed_one_grad = lax.optimization_barrier((plane_turn(tree_two), tree_one, normed_one_grad))
        tree_one = column_sum(tree_one)
    input_norm_grad, gain_one_grad = norm_back(normed_one_grad, gain_one, flat_one, factor_one)
    grad_input = row_major(middle_grad + input_norm_grad)
    gain_grads = jnp.stack([gain_one_grad, gain_two_grad], axis=1)
    hidden_shards = unpack_hidden(hidden_sum[:, :hidden_columns], blocks)
    hidden_shards[2] = hidden_shards[2].T
    if tree:
        gain_grads = gain_grads.T
        tree_two, gain_grads = lax.optimization_barrier((column_parts(tree_two), gain_grads + swap(gain_grads)))
        gain_sum = gain_tree(gain_grads)
        grad_output = tree_one[:, :width].T
        tree_two, hidden_shards = column_sum(tree_two, hidden_shards)
        first_sum = jnp.concatenate([tree_one[:, width:], tree_two], axis=1)
    else:
        gain_grads = jnp.pad(lax.psum(gain_grads, "tensor").astype(BF16), ((0, 0), (0, 126)))
        first_sum = lax.psum_scatter(jnp.concatenate([projection_grads, gain_grads], axis=1), "dp", scatter_dimension=0, tiled=True).astype(F32)
        gain_sum = first_sum[:, 3 * width : 3 * width + 2]
        first_sum = first_sum[:, : 3 * width]
    grad_gate, grad_up, grad_down = hidden_shards
    grad_query, grad_key, grad_value = unpack_hidden(first_sum, pairs)
    return (
        layer_out,
        grad_input,
        grad_value_first,
        gain_sum[:, 0],
        grad_query,
        grad_key,
        grad_value,
        grad_output,
        gain_sum[:, 1],
        grad_gate,
        grad_up,
        grad_down,
    )


def solution(mesh):
    tokens, split = P(BOTH, None), P("dp", "tensor")
    across = P("tensor", "dp")
    return jax.shard_map(
        functools.partial(per_device, mesh.shape["dp"], mesh.shape["tensor"]),
        mesh=mesh,
        in_specs=(tokens, split, P("dp", None), tokens, P("dp"), split, split, split, across, P("dp"), split, split, across),
        out_specs=(tokens, tokens, split, P("dp"), split, split, split, across, P("dp"), split, split, across),
        check_vma=False,
    )
```
